32 devices in a mesh: rep: 4 (over x, core), shard: 8 (over z, y).
Axes of the slice: x: 2, y: 2, z: 4, core: 2. Of those that a mesh axis runs over, the one named last changes fastest.
Arguments:
- tokens: bfloat16 [4096, 896], P(('rep', 'shard')), may hold values from -6 to 6
- cotangent: bfloat16 [4096, 896], P(('rep', 'shard')), may hold values from -6 to 6
- lengths: int32 [32, 8], P(('rep', 'shard')), may hold values from 1 to 64, 128 in all within a row
- query_weight: bfloat16 [896, 896], P('shard'), may hold values from -0.1875 to 0.1875
- key_weight: bfloat16 [896, 128], P('shard'), may hold values from -0.1875 to 0.1875
- value_weight: bfloat16 [896, 128], P('shard'), may hold values from -0.1875 to 0.1875
- output_weight: bfloat16 [896, 896], P('shard'), may hold values from -0.5 to 0.5
- query_bias: bfloat16 [896], P('shard'), may hold values from -3 to 3
- key_bias: bfloat16 [128], P('shard'), may hold values from -3 to 3
- value_bias: bfloat16 [128], P('shard'), may hold values from -3 to 3
- attn_gain: bfloat16 [896], P('shard'), may hold values from 0.5 to 1.5
- gate_weight: bfloat16 [896, 4864], P('shard'), may hold values from -0.1875 to 0.1875
- up_weight: bfloat16 [896, 4864], P('shard'), may hold values from -0.1875 to 0.1875
- down_weight: bfloat16 [4864, 896], P('shard'), may hold values from -0.15625 to 0.15625
- mlp_gain: bfloat16 [896], P('shard'), may hold values from 0.5 to 1.5
Outputs:
- result: bfloat16 [4096, 896], P(('rep', 'shard'))
- grad_tokens: float32 [4096, 896], P(('rep', 'shard'))
- grad_query_weight: float32 [896, 896], P('shard')
- grad_key_weight: float32 [896, 128], P('shard')
- grad_value_weight: float32 [896, 128], P('shard')
- grad_output_weight: float32 [896, 896], P('shard')
- grad_query_bias: float32 [896], P('shard')
- grad_key_bias: float32 [128], P('shard')
- grad_value_bias: float32 [128], P('shard')
- grad_attn_gain: float32 [896], P('shard')
- grad_gate_weight: float32 [896, 4864], P('shard')
- grad_up_weight: float32 [896, 4864], P('shard')
- grad_down_weight: float32 [4864, 896], P('shard')
- grad_mlp_gain: float32 [896], P('shard')
The draws below stay inside these ranges and needn't reach their ends.
Inputs may be any that keep to these rules, and one draw needn't show every extreme that they name: Row b lists the lengths of the 8 sequences packed in order on the b-th block of 128 tokens; they fill it exactly, and the longest of every row is exactly 64.
All inputs are finite; a program needn't handle non-finite values.
Results may differ from the reference program's by a relative error of at most 0.02.
The reference program's roundings to bfloat16 on the way count: a program that leaves them out, or rounds other values in their place, can miss the bound.
Values may be sent and summed in bfloat16 or wider, within the bound.
A program may use at most 192 MiB of HBM per device.

```python
import math
import jax
import jax.numpy as jnp
import numpy as np
from jax import lax

D = 896
HEADS = 14
KVH = 2
HD = 64
FF = 4864
TOK_DEV = 128
SEQS = 8
KVD = 128
MAXLEN = 64
DEVBLK = 32
TOKENS = 4096


def block_levels(key, extent, pieces, least, largest):
    def one(position, parts):
        draws = jax.random.uniform(jax.random.fold_in(jax.random.fold_in(key, 6), position), (parts,), jnp.float32, least / len(pieces), largest / len(pieces))
        return jnp.repeat(jnp.exp(draws), extent[position] // parts).reshape((-1,) + (1,) * (len(extent) - position - 1))

    factor_of = one(*pieces[0])
    for cut in pieces[1:]:
        factor_of = factor_of * one(*cut)
    return factor_of


def length_profile(number_of, total, most, lean):
    weights = [(1 << 20) // math.isqrt(standing ** lean) + 1 for standing in range(2, number_of + 1)]
    rest, holding = total - most - (number_of - 1), [1] * (number_of - 1)
    while rest > 0:
        movable = [i for i in range(number_of - 1) if holding[i] < most]
        pool, left = sum([weights[i] for i in movable]), rest
        for i in movable:
            more = min(most - holding[i], max(1, left * weights[i] // pool), rest)
            holding[i] = holding[i] + more
            rest = rest - more
    return np.array([most] + holding)


def ragged_sizes(rng, number_of, total, bound, lean):
    if number_of == 2:
        one = jax.random.randint(rng, (), max(1, total - bound), min(bound, total - 1) + 1)
        return jnp.stack([one, total - one])
    tallies = jnp.asarray(length_profile(number_of, total, bound, lean), jnp.int32)
    twos = (number_of - 1) // 2
    source_of, receiver = tallies[1:1 + 2 * twos:2], tallies[2:2 + 2 * twos:2]
    room = jnp.minimum(source_of - 1, bound - receiver)
    shifted = jax.random.randint(jax.random.fold_in(rng, 1), (twos,), 0, 1 << 20) % (room + 1)
    tallies = tallies.at[1:1 + 2 * twos:2].set(source_of - shifted).at[2:2 + 2 * twos:2].set(receiver + shifted)
    return tallies[jax.random.permutation(jax.random.fold_in(rng, 2), number_of)]


def noise(key, dims, scale, most, pieces=(), kind=jnp.bfloat16):
    entries = scale * jax.random.normal(key, dims, jnp.float32)
    if pieces:
        entries = entries * block_levels(key, dims, pieces, -0.22, 0.18)
    return jnp.clip(entries, -most, most).astype(kind)


def setup_inputs(seed: int = 0) -> dict:
    splits = jax.random.split(jax.random.key(seed), 16)
    tokens = noise(splits[0], (TOKENS, D), 1.0, 6.0, ((0, 32),))
    cotangent = noise(splits[1], (TOKENS, D), 1.0, 6.0, ((0, 32),))
    lengths = jax.vmap(lambda own: ragged_sizes(own, SEQS, TOK_DEV, MAXLEN, 2))(jax.random.split(splits[2], DEVBLK)).reshape((DEVBLK, SEQS)).astype(jnp.int32)
    query_weight = noise(splits[3], (D, D), D ** -0.5, 0.1875, ((0, 8),))
    key_weight = noise(splits[4], (D, KVD), D ** -0.5, 0.1875, ((0, 8),))
    value_weight = noise(splits[5], (D, KVD), D ** -0.5, 0.1875, ((0, 8),))
    output_weight = noise(splits[6], (D, D), (D // 8) ** -0.5, 0.5, ((0, 8),))
    query_bias = noise(splits[7], (D,), 0.5, 3.0, ((0, 8),))
    key_bias = noise(splits[8], (KVD,), 0.5, 3.0, ((0, 8),))
    value_bias = noise(splits[9], (KVD,), 0.5, 3.0, ((0, 8),))
    attn_gain = jnp.clip(1.0 + 0.1 * jax.random.normal(splits[10], (D,), jnp.float32), 0.5, 1.5).astype(jnp.bfloat16)
    gate_weight = noise(splits[11], (D, FF), D ** -0.5, 0.1875, ((0, 8),))
    up_weight = noise(splits[12], (D, FF), D ** -0.5, 0.1875, ((0, 8),))
    down_weight = noise(splits[13], (FF, D), (FF // 4) ** -0.5, 0.15625, ((0, 8),))
    mlp_gain = jnp.clip(1.0 + 0.1 * jax.random.normal(splits[14], (D,), jnp.float32), 0.5, 1.5).astype(jnp.bfloat16)
    return dict(tokens=tokens, cotangent=cotangent, lengths=lengths, query_weight=query_weight, key_weight=key_weight, value_weight=value_weight, output_weight=output_weight, query_bias=query_bias, key_bias=key_bias, value_bias=value_bias, attn_gain=attn_gain, gate_weight=gate_weight, up_weight=up_weight, down_weight=down_weight, mlp_gain=mlp_gain)


theta_base = 1000000.0
eps_norm = 1e-06
masked_score = -1000000000.0

def tables(lengths_row, rows):
    ends = jnp.cumsum(lengths_row)
    starts = ends - lengths_row
    places = jnp.arange(rows, dtype=jnp.int32)
    inside = ((places[:, None] >= starts[None, :]) & (places[:, None] < ends[None, :])).astype(jnp.int32)
    slots = jnp.arange(lengths_row.shape[0], dtype=jnp.int32)
    segment = lax.optimization_barrier(jnp.sum(inside * slots[None, :], axis=1))
    first = lax.optimization_barrier(jnp.sum(inside * starts[None, :], axis=1))
    offset = (places - first).astype(jnp.float32)
    half = HD // 2
    freq = theta_base ** (-(jnp.arange(half, dtype=jnp.float32) * (2.0 / HD)))
    angles = offset[:, None] * freq[None, :]
    return (segment, places, jnp.cos(angles), jnp.sin(angles))

def rotate(values, cosine, sine):
    half = values.shape[-1] // 2
    first, second = (values[..., :half], values[..., half:])
    cosine = cosine[:, :, None, :]
    sine = sine[:, :, None, :]
    return jnp.concatenate([first * cosine - second * sine, second * cosine + first * sine], axis=-1)

def unrotate(grads, cosine, sine):
    half = grads.shape[-1] // 2
    first, second = (grads[..., :half], grads[..., half:])
    cosine = cosine[:, :, None, :]
    sine = sine[:, :, None, :]
    return jnp.concatenate([first * cosine + second * sine, second * cosine - first * sine], axis=-1)

def norm_fwd(hidden, gain):
    scale = lax.rsqrt(lax.optimization_barrier(jnp.mean(hidden * hidden, axis=-1, keepdims=True)) + eps_norm)
    return (scale, hidden * scale * gain.astype(jnp.float32))

def norm_bwd(dnormed, hidden, scale, gain):
    gain_f = gain.astype(jnp.float32)
    dgain = lax.optimization_barrier(jnp.sum(dnormed * hidden * scale, axis=0))
    inner = dnormed * gain_f
    dhidden = scale * inner - hidden * (scale * scale * scale) * lax.optimization_barrier(jnp.mean(inner * hidden, axis=-1, keepdims=True))
    return (dhidden, dgain)

def scores_of(query, keys, segment, places):
    raw = jnp.einsum('igha,jga->ghij', query.astype(jnp.float32), keys.astype(jnp.float32)) * (1.0 / math.sqrt(HD))
    allowed = (segment[:, None] == segment[None, :]) & (places[None, :] <= places[:, None])
    return jnp.where(allowed[None, None], raw, masked_score)

def attend(query, keys, values, segment, places):
    raw = scores_of(query, keys, segment, places)
    top = lax.optimization_barrier(jnp.max(raw, axis=-1, keepdims=True))
    total = lax.optimization_barrier(jnp.sum(jnp.exp(raw - top), axis=-1))
    lse = top[..., 0] + jnp.log(total)
    probs = jnp.exp(raw - lse[..., None]).astype(jnp.bfloat16)
    mixed = jnp.einsum('ghij,jga->igha', probs.astype(jnp.float32), values.astype(jnp.float32)).astype(jnp.bfloat16)
    return (mixed, lse)

def attend_back(query, keys, values, mixed, dmixed, lse, segment, places):
    raw = scores_of(query, keys, segment, places)
    probs_f = jnp.exp(raw - lse[..., None])
    probs = probs_f.astype(jnp.bfloat16)
    dvals = jnp.einsum('ghij,igha->jga', probs.astype(jnp.float32), dmixed.astype(jnp.float32))
    dprobs = jnp.einsum('igha,jga->ghij', dmixed.astype(jnp.float32), values.astype(jnp.float32))
    delta = jnp.einsum('igha,igha->ghi', dmixed.astype(jnp.float32), mixed.astype(jnp.float32))
    dscores = (probs_f * (dprobs - delta[..., None]) * (1.0 / math.sqrt(HD))).astype(jnp.bfloat16)
    dquery = jnp.einsum('ghij,jga->igha', dscores.astype(jnp.float32), keys.astype(jnp.float32))
    dkeys = jnp.einsum('ghij,igha->jga', dscores.astype(jnp.float32), query.astype(jnp.float32))
    return (dquery, dkeys, dvals)

def forward(tokens, lengths, attn_params, mlp_params):
    blocks, rows, width = tokens.shape
    query_weight, key_weight, value_weight, output_weight, query_bias, key_bias, value_bias, attn_gain = attn_params
    gate_weight, up_weight, down_weight, mlp_gain = mlp_params
    segment, places, cosine, sine = jax.vmap(lambda lens: tables(lens, rows))(lengths)
    flat = tokens.reshape(blocks * rows, width).astype(jnp.float32)
    scale_one, normed_one = norm_fwd(flat, attn_gain)
    normed_one = normed_one.astype(jnp.bfloat16)
    query = jnp.dot(normed_one, query_weight, preferred_element_type=jnp.float32) + query_bias.astype(jnp.float32)
    keys = jnp.dot(normed_one, key_weight, preferred_element_type=jnp.float32) + key_bias.astype(jnp.float32)
    values = jnp.dot(normed_one, value_weight, preferred_element_type=jnp.float32) + value_bias.astype(jnp.float32)
    query = rotate(query.reshape(blocks, rows, HEADS, HD), cosine, sine).astype(jnp.bfloat16)
    query = query.reshape(blocks, rows, KVH, HEADS // KVH, HD)
    keys = rotate(keys.reshape(blocks, rows, KVH, HD), cosine, sine).astype(jnp.bfloat16)
    values = values.reshape(blocks, rows, KVH, HD).astype(jnp.bfloat16)
    mixed, lse = jax.vmap(attend)(query, keys, values, segment, places)
    mixed_flat = mixed.reshape(blocks * rows, width)
    hidden_one = flat + jnp.dot(mixed_flat, output_weight, preferred_element_type=jnp.float32)
    scale_two, normed_two = norm_fwd(hidden_one, mlp_gain)
    normed_two = normed_two.astype(jnp.bfloat16)
    gate = jnp.dot(normed_two, gate_weight, preferred_element_type=jnp.float32)
    upper = jnp.dot(normed_two, up_weight, preferred_element_type=jnp.float32)
    product = (jax.nn.silu(gate) * upper).astype(jnp.bfloat16)
    result = (hidden_one + jnp.dot(product, down_weight, preferred_element_type=jnp.float32)).astype(jnp.bfloat16)
    saved = (segment, places, cosine, sine, flat, scale_one, normed_one, query, keys, values, mixed, lse, hidden_one, scale_two, normed_two, gate, upper, product)
    return (result.reshape(blocks, rows, width), saved)

def backward(cotangent, saved, attn_params, mlp_params):
    blocks, rows, width = cotangent.shape
    query_weight, key_weight, value_weight, output_weight, query_bias, key_bias, value_bias, attn_gain = attn_params
    gate_weight, up_weight, down_weight, mlp_gain = mlp_params
    segment, places, cosine, sine, flat, scale_one, normed_one, query, keys, values, mixed, lse, hidden_one, scale_two, normed_two, gate, upper, product = saved
    cot_b = cotangent.reshape(blocks * rows, width)
    cot_f = cot_b.astype(jnp.float32)
    grad_down = jnp.dot(product.T, cot_b, preferred_element_type=jnp.float32)
    dprod = jnp.dot(cot_b, down_weight.T, preferred_element_type=jnp.float32)
    sigma = jax.nn.sigmoid(gate)
    dgate = (dprod * upper * sigma * (1.0 + gate * (1.0 - sigma))).astype(jnp.bfloat16)
    dup = (dprod * gate * sigma).astype(jnp.bfloat16)
    grad_gate = jnp.dot(normed_two.T, dgate, preferred_element_type=jnp.float32)
    grad_up = jnp.dot(normed_two.T, dup, preferred_element_type=jnp.float32)
    dnormed_two = jnp.dot(dgate, gate_weight.T, preferred_element_type=jnp.float32) + jnp.dot(dup, up_weight.T, preferred_element_type=jnp.float32)
    dh_two, grad_mlp_gain = norm_bwd(dnormed_two, hidden_one, scale_two, mlp_gain)
    dhidden = cot_f + dh_two
    dres = dhidden.astype(jnp.bfloat16)
    mixed_flat = mixed.reshape(blocks * rows, width)
    grad_output = jnp.dot(mixed_flat.T, dres, preferred_element_type=jnp.float32)
    dmixed = jnp.dot(dres, output_weight.T, preferred_element_type=jnp.float32).astype(jnp.bfloat16)
    dmixed = dmixed.reshape(blocks, rows, KVH, HEADS // KVH, HD)
    dquery, dkeys, dvals = jax.vmap(attend_back)(query, keys, values, mixed, dmixed, lse, segment, places)
    dquery = unrotate(dquery.reshape(blocks, rows, HEADS, HD), cosine, sine).reshape(blocks * rows, width)
    dkeys = unrotate(dkeys, cosine, sine).reshape(blocks * rows, KVH * HD)
    dvals = dvals.reshape(blocks * rows, KVH * HD)
    grad_qbias = lax.optimization_barrier(jnp.sum(dquery, axis=0))
    grad_kbias = lax.optimization_barrier(jnp.sum(dkeys, axis=0))
    grad_vbias = lax.optimization_barrier(jnp.sum(dvals, axis=0))
    dquery_b = dquery.astype(jnp.bfloat16)
    dkeys_b = dkeys.astype(jnp.bfloat16)
    dvals_b = dvals.astype(jnp.bfloat16)
    grad_query = jnp.dot(normed_one.T, dquery_b, preferred_element_type=jnp.float32)
    grad_key = jnp.dot(normed_one.T, dkeys_b, preferred_element_type=jnp.float32)
    grad_value = jnp.dot(normed_one.T, dvals_b, preferred_element_type=jnp.float32)
    dnormed_one = jnp.dot(dquery_b, query_weight.T, preferred_element_type=jnp.float32) + jnp.dot(dkeys_b, key_weight.T, preferred_element_type=jnp.float32) + jnp.dot(dvals_b, value_weight.T, preferred_element_type=jnp.float32)
    dh_one, grad_attn_gain = norm_bwd(dnormed_one, flat, scale_one, attn_gain)
    grad_input = (dhidden + dh_one).reshape(blocks, rows, width)
    attn_grads = (grad_query, grad_key, grad_value, grad_output, grad_qbias, grad_kbias, grad_vbias, grad_attn_gain)
    mlp_grads = (grad_gate, grad_up, grad_down, grad_mlp_gain)
    return (grad_input, attn_grads, mlp_grads)

def reference(tokens, cotangent, lengths, query_weight, key_weight, value_weight, output_weight, query_bias, key_bias, value_bias, attn_gain, gate_weight, up_weight, down_weight, mlp_gain):
    attn_params = (query_weight, key_weight, value_weight, output_weight, query_bias, key_bias, value_bias, attn_gain)
    mlp_params = (gate_weight, up_weight, down_weight, mlp_gain)
    count = lengths.shape[0]
    group = math.gcd(count, max(1, 4096 // TOK_DEV))
    rounds = count // group
    tok_groups = tokens.reshape(rounds, group, TOK_DEV, D)
    cot_groups = cotangent.reshape(rounds, group, TOK_DEV, D)
    len_groups = lengths.reshape(rounds, group, SEQS)
    zeros = jax.tree.map(lambda weight: jnp.zeros(weight.shape, jnp.float32), (attn_params, mlp_params))

    def advance(carry, items):
        tok_block, cot_block, len_block = items
        result, saved = forward(tok_block, len_block, attn_params, mlp_params)
        grad_input, attn_grads, mlp_grads = backward(cot_block, saved, attn_params, mlp_params)
        carry = jax.tree.map(lambda left, right: left + right, carry, (attn_grads, mlp_grads))
        return (carry, (result, grad_input))
    totals, outputs = lax.scan(advance, zeros, (tok_groups, cot_groups, len_groups))
    attn_total, mlp_total = totals
    results = outputs[0].reshape(TOKENS, D)
    grads_in = outputs[1].reshape(TOKENS, D)
    return (results, grads_in, attn_total[0], attn_total[1], attn_total[2], attn_total[3], attn_total[4], attn_total[5], attn_total[6], attn_total[7], mlp_total[0], mlp_total[1], mlp_total[2], mlp_total[3])
```

```python
import math

import jax
import jax.numpy as jnp
from jax import lax
from jax.sharding import PartitionSpec as P

HEADS = 14
KVH = 2
HD = 64


theta_base = 1000000.0
eps_norm = 1e-06
masked_score = -1000000000.0


def times_transposed(left, weight):
    return lax.dot_general(
        left, weight, (((1,), (1,)), ((), ())), preferred_element_type=jnp.float32
    )


def tables(lengths_row, rows):
    order = jnp.arange(lengths_row.shape[0])
    ends = jnp.sum(jnp.where(order[None, :] <= order[:, None], lengths_row[None, :], 0), axis=1)
    starts = ends - lengths_row
    places = jnp.arange(rows, dtype=jnp.int32)
    inside = ((places[:, None] >= starts[None, :]) & (places[:, None] < ends[None, :])).astype(
        jnp.int32
    )
    slots = jnp.arange(lengths_row.shape[0], dtype=jnp.int32)
    segment = jnp.sum(inside * slots[None, :], axis=1)
    first = jnp.sum(inside * starts[None, :], axis=1)
    offset = (places - first).astype(jnp.float32)
    half = HD // 2
    freq = theta_base ** (-(jnp.arange(half, dtype=jnp.float32) * (2.0 / HD)))
    angles = offset[:, None] * freq[None, :]
    return (segment, places, jnp.cos(angles), jnp.sin(angles))


def rotate(values, cosine, sine):
    half = values.shape[-1] // 2
    first, second = (values[..., :half], values[..., half:])
    cosine = cosine[:, :, None, :]
    sine = sine[:, :, None, :]
    return jnp.concatenate(
        [first * cosine - second * sine, second * cosine + first * sine], axis=-1
    )


def unrotate(grads, cosine, sine):
    half = grads.shape[-1] // 2
    first, second = (grads[..., :half], grads[..., half:])
    cosine = cosine[:, :, None, :]
    sine = sine[:, :, None, :]
    return jnp.concatenate(
        [first * cosine + second * sine, second * cosine - first * sine], axis=-1
    )


def norm_fwd(hidden, gain):
    scale = lax.rsqrt(jnp.mean(hidden * hidden, axis=-1, keepdims=True) + eps_norm)
    return (scale, hidden * scale * gain.astype(jnp.float32))


def norm_bwd(dnormed, hidden, scale, gain):
    gain_f = gain.astype(jnp.float32)
    dgain = jnp.sum(dnormed * hidden * scale, axis=0)
    inner = dnormed * gain_f
    dhidden = scale * inner - hidden * (scale * scale * scale) * jnp.mean(
        inner * hidden, axis=-1, keepdims=True
    )
    return (dhidden, dgain)


def scores_of(query, keys, segment, places):
    raw = jnp.einsum("igha,jga->ghij", query, keys, preferred_element_type=jnp.float32) * (
        1.0 / math.sqrt(HD)
    )
    allowed = (segment[:, None] == segment[None, :]) & (places[None, :] <= places[:, None])
    return jnp.where(allowed[None, None], raw, masked_score)


def attend(query, keys, values, segment, places):
    raw = scores_of(query, keys, segment, places)
    top = jnp.max(raw, axis=-1, keepdims=True)
    total = jnp.sum(jnp.exp(raw - top), axis=-1)
    lse = top[..., 0] + jnp.log(total)
    probs = jnp.exp(raw - lse[..., None]).astype(jnp.bfloat16)
    mixed = jnp.einsum("ghij,jga->igha", probs, values, preferred_element_type=jnp.float32).astype(
        jnp.bfloat16
    )
    return (mixed, lse)


def attend_back(query, keys, values, mixed, dmixed, lse, segment, places):
    raw = scores_of(query, keys, segment, places)
    probs_f = jnp.exp(raw - lse[..., None])
    probs = probs_f.astype(jnp.bfloat16)
    dvals = jnp.einsum("ghij,igha->jga", probs, dmixed, preferred_element_type=jnp.float32)
    dprobs = jnp.einsum("igha,jga->ghij", dmixed, values, preferred_element_type=jnp.float32)
    delta = jnp.einsum("igha,igha->ghi", dmixed, mixed, preferred_element_type=jnp.float32)
    dscores = (probs_f * (dprobs - delta[..., None]) * (1.0 / math.sqrt(HD))).astype(jnp.bfloat16)
    dquery = jnp.einsum("ghij,jga->igha", dscores, keys, preferred_element_type=jnp.float32)
    dkeys = jnp.einsum("ghij,igha->jga", dscores, query, preferred_element_type=jnp.float32)
    return (dquery, dkeys, dvals)


class Grid:
    def __init__(self):
        self.reps = lax.axis_size("rep")
        self.shards = lax.axis_size("shard")
        c = 2 if self.reps % 2 == 0 else 1
        x = self.reps // c
        y = x if self.shards % x == 0 else 1
        z = self.shards // y
        l = 2 if z % 2 == 0 else 1
        self.size = dict(x=x, c=c, h=z // l, l=l, y=y, z=z)
        rep, shard = lax.axis_index("rep"), lax.axis_index("shard")
        zz = shard // y
        self.at = dict(x=rep // c, c=rep % c, z=zz, y=shard % y, h=zz // l, l=zz % l)

    def send(self, value, **by):
        n = self.size
        pairs = []
        for rep in range(self.reps):
            for shard in range(self.shards):
                at = dict(x=rep // n["c"], c=rep % n["c"], z=shard // n["y"], y=shard % n["y"])
                if "h" in by or "l" in by:
                    h = (at["z"] // n["l"] + by.get("h", 0)) % n["h"]
                    at["z"] = h * n["l"] + (at["z"] + by.get("l", 0)) % n["l"]
                for d in "xczy":
                    at[d] = (at[d] + by.get(d, 0)) % n[d]
                pairs.append(
                    (
                        rep * self.shards + shard,
                        (at["x"] * n["c"] + at["c"]) * self.shards + at["z"] * n["y"] + at["y"],
                    )
                )
        return lax.ppermute(value, ("rep", "shard"), pairs)

    def peer(self, d, k):
        return (self.at[d] + k + self.size[d]) % self.size[d]

    def gather(self, value, d):
        out = jnp.zeros((self.size[d],) + value.shape, value.dtype)
        out = lax.dynamic_update_index_in_dim(out, value, self.at[d], 0)
        for k in range(1, self.size[d]):
            out = lax.dynamic_update_index_in_dim(
                out, self.send(value, **{d: k}), self.peer(d, -k), 0
            )
        return out

    def scatter(self, value, d):
        pick = lambda k: lax.dynamic_index_in_dim(value, self.peer(d, k), 0, keepdims=False)
        total = pick(0).astype(jnp.float32)
        for k in range(1, self.size[d]):
            total = total + self.send(pick(k), **{d: k}).astype(jnp.float32)
        return total.astype(value.dtype)


def on_device(
    tokens,
    cotangent,
    lengths,
    query_weight,
    key_weight,
    value_weight,
    output_weight,
    query_bias,
    key_bias,
    value_bias,
    attn_gain,
    gate_weight,
    up_weight,
    down_weight,
    mlp_gain,
):
    grid = Grid()
    size, at = grid.size, grid.at
    shards, reps = grid.shards, grid.reps
    rep = lax.axis_index("rep")
    rows, width = tokens.shape
    own = query_weight.shape[0]
    kvd = key_weight.shape[1]
    own_kv = key_bias.shape[0]
    f32, bf16 = jnp.float32, jnp.bfloat16
    wide = width + 2 * kvd
    total_w = wide + width
    quarter = total_w // reps

    small = jnp.concatenate([query_bias, attn_gain, mlp_gain, key_bias, value_bias])
    extra = 8
    small = jnp.pad(small, (0, extra * quarter - small.shape[0])).reshape(extra, quarter)
    packed = jnp.concatenate([query_weight, key_weight, value_weight, output_weight], axis=1)
    mine = lax.dynamic_slice(packed, (0, rep * quarter), (own, quarter))
    mine = jnp.concatenate([mine, small], axis=0)
    mine = grid.gather(mine, "z")
    mine = grid.gather(mine, "y")
    mine = grid.gather(mine, "x")
    mine = grid.gather(mine, "c")
    full = mine[..., :own, :].transpose(3, 2, 4, 1, 0, 5).reshape(width, total_w)
    qkv_weight = full[:, :wide]
    output_full = full[:, wide:]
    vectors = mine[0, 0, :, :, own:, :].transpose(1, 0, 2, 3).reshape(shards, extra * quarter)
    piece = lambda first, count: vectors[:, first : first + count].reshape(shards * count)
    query_bias_f, attn_gain_f, mlp_gain_f = (piece(i * own, own) for i in range(3))
    key_bias_f = piece(3 * own, own_kv)
    value_bias_f = piece(3 * own + own_kv, own_kv)
    qkv_bias = jnp.concatenate([query_bias_f, key_bias_f, value_bias_f]).astype(f32)

    part = down_weight.shape[0] // reps
    sets = size["l"] * size["y"]
    hidden = size["h"] * part

    def column_sets(weight):
        split = weight.reshape(own, size["h"], sets, reps, part)
        split = lax.dynamic_index_in_dim(split, rep, 3, keepdims=False)
        return split.transpose(2, 0, 1, 3).reshape(sets, own, hidden)

    both_sets = jnp.concatenate([column_sets(gate_weight), column_sets(up_weight)], axis=2)
    down_part = lax.dynamic_slice(down_weight, (rep * part, 0), (part, width))
    both_mine = jnp.zeros((size["h"], size["l"], size["y"], own, 2 * hidden), bf16)
    for kl in range(size["l"]):
        for ky in range(size["y"]):
            block = lax.dynamic_index_in_dim(
                both_sets, grid.peer("l", kl) * size["y"] + grid.peer("y", ky), 0, keepdims=False
            )
            for kh in range(size["h"]):
                got = block if kl + ky + kh == 0 else grid.send(block, h=kh, l=kl, y=ky)
                both_mine = lax.dynamic_update_slice(
                    both_mine,
                    got[None, None, None],
                    (grid.peer("h", -kh), grid.peer("l", -kl), grid.peer("y", -ky), 0, 0),
                )
    both_mine = both_mine.reshape(width, 2 * hidden)
    down_mine = grid.gather(down_part, "h").reshape(hidden, width)

    def gather_tokens(value):
        for d in "lyxc":
            value = grid.gather(value, d)
        return value.reshape(-1, width)

    def scatter_tokens(value):
        value = value.reshape(size["c"], size["x"], size["y"], size["l"], rows, -1)
        for d in "cxyl":
            value = grid.scatter(value, d)
        return value

    cot_all = gather_tokens(cotangent)

    segment, places, cosine, sine = jax.vmap(lambda lens: tables(lens, rows))(lengths)
    flat = tokens.astype(f32)
    scale_one, normed_one = norm_fwd(flat, attn_gain_f)
    normed_one = normed_one.astype(bf16)
    qkv = jnp.dot(normed_one, qkv_weight, preferred_element_type=f32) + qkv_bias
    query = rotate(qkv[:, :width].reshape(1, rows, HEADS, HD), cosine, sine).astype(bf16)
    query = query.reshape(1, rows, KVH, HEADS // KVH, HD)
    keys = rotate(qkv[:, width : width + kvd].reshape(1, rows, KVH, HD), cosine, sine).astype(bf16)
    values = qkv[:, width + kvd :].reshape(1, rows, KVH, HD).astype(bf16)
    mixed, lse = jax.vmap(attend)(query, keys, values, segment, places)
    mixed_flat = mixed.reshape(rows, width)
    hidden_one = flat + jnp.dot(mixed_flat, output_full, preferred_element_type=f32)
    scale_two, normed_two = norm_fwd(hidden_one, mlp_gain_f)
    normed_all = gather_tokens(normed_two.astype(bf16))

    dprod = times_transposed(cot_all, down_mine)
    both = jnp.dot(normed_all, both_mine, preferred_element_type=f32)
    gate, upper = both[:, :hidden], both[:, hidden:]
    sigma = jax.nn.sigmoid(gate)
    product = (gate * sigma * upper).astype(bf16)
    dgate = (dprod * upper * sigma * (1.0 + gate * (1.0 - sigma))).astype(bf16)
    dup = (dprod * gate * sigma).astype(bf16)
    dboth = jnp.concatenate([dgate, dup], axis=1)
    dnormed_part = times_transposed(dboth, both_mine).astype(bf16)
    out_part = jnp.dot(product, down_mine, preferred_element_type=f32).astype(bf16)
    dnormed_two = scatter_tokens(dnormed_part).astype(f32)
    out_sum = scatter_tokens(out_part).astype(f32)
    grad_both = jnp.dot(normed_all.T, dboth, preferred_element_type=f32).astype(bf16)
    grad_down = jnp.dot(product.T, cot_all, preferred_element_type=f32).astype(bf16)

    grad_both = grid.scatter(grad_both.reshape(size["h"], sets, own, 2 * hidden), "h")
    grad_down = grid.scatter(grad_down.reshape(size["h"], part, width), "h")
    owned = jnp.zeros((size["l"], size["y"], own, 2 * hidden), bf16)
    for kl in range(size["l"]):
        for ky in range(size["y"]):
            block = lax.dynamic_index_in_dim(
                grad_both, grid.peer("l", kl) * size["y"] + grid.peer("y", ky), 0, keepdims=False
            )
            got = block if kl + ky == 0 else grid.send(block, l=kl, y=ky)
            owned = lax.dynamic_update_slice(
                owned, got[None, None], (grid.peer("l", -kl), grid.peer("y", -ky), 0, 0)
            )

    def from_replicas(value):
        return grid.gather(grid.gather(value, "c"), "x").reshape((reps,) + value.shape)

    both_all = from_replicas(owned.reshape(sets, own, 2 * hidden))
    down_all = from_replicas(grad_down).reshape(reps * part, width).astype(f32)

    def joined(first):
        half = both_all[..., first : first + hidden].reshape(reps, sets, own, size["h"], part)
        return half.transpose(2, 3, 1, 0, 4).reshape(own, -1).astype(f32)

    result = (hidden_one + out_sum).astype(bf16)

    dh_two, grad_mlp_gain = norm_bwd(dnormed_two, hidden_one, scale_two, mlp_gain_f)
    dhidden = cotangent.astype(f32) + dh_two
    dres = dhidden.astype(bf16)
    grad_output = jnp.dot(mixed_flat.T, dres, preferred_element_type=f32).astype(bf16)
    dmixed = times_transposed(dres, output_full).astype(bf16)
    dmixed = dmixed.reshape(1, rows, KVH, HEADS // KVH, HD)
    dquery, dkeys, dvals = jax.vmap(attend_back)(
        query, keys, values, mixed, dmixed, lse, segment, places
    )
    dquery = unrotate(dquery.reshape(1, rows, HEADS, HD), cosine, sine).reshape(rows, width)
    dkeys = unrotate(dkeys, cosine, sine).reshape(rows, kvd)
    dvals = dvals.reshape(rows, kvd)
    dqkv = jnp.concatenate([dquery, dkeys, dvals], axis=1)
    grad_bias = jnp.sum(dqkv, axis=0)
    dqkv_b = dqkv.astype(bf16)
    grad_qkv = jnp.dot(normed_one.T, dqkv_b, preferred_element_type=f32).astype(bf16)
    dnormed_one = times_transposed(dqkv_b, qkv_weight)
    dh_one, grad_attn_gain = norm_bwd(dnormed_one, flat, scale_one, attn_gain_f)
    grad_input = dhidden + dh_one

    cut = lambda v, count: v.reshape(shards, count)
    small_g = jnp.concatenate(
        [
            cut(grad_bias[:width], own),
            cut(grad_attn_gain, own),
            cut(grad_mlp_gain, own),
            cut(grad_bias[width : width + kvd], own_kv),
            cut(grad_bias[width + kvd :], own_kv),
        ],
        axis=1,
    )
    small_n = small_g.shape[1]
    small_g = jnp.pad(small_g, ((0, 0), (0, extra * quarter - small_n)))
    small_g = jnp.broadcast_to(
        small_g.reshape(shards, 1, extra, quarter).astype(bf16), (shards, reps, extra, quarter)
    )
    grads = jnp.concatenate([grad_qkv, grad_output], axis=1)
    grads = grads.reshape(shards, own, reps, quarter).transpose(0, 2, 1, 3)
    grads = jnp.concatenate([grads, small_g], axis=2)
    grads = grads.reshape(size["z"], size["y"], size["x"], size["c"], own + extra, quarter)
    grads = grid.scatter(grads.transpose(3, 2, 1, 0, 4, 5), "c")
    grads = grid.scatter(grads, "x")
    grads = grid.scatter(grads, "y")
    grads = grid.scatter(grads, "z")
    vec = grads[own:].reshape(extra * quarter)[:small_n].astype(f32)
    attn_all = from_replicas(grads[:own]).transpose(1, 0, 2).reshape(own, total_w).astype(f32)

    return (
        result,
        grad_input,
        attn_all[:, :width],
        attn_all[:, width : width + kvd],
        attn_all[:, width + kvd : wide],
        attn_all[:, wide:],
        vec[:own],
        vec[3 * own : 3 * own + own_kv],
        vec[3 * own + own_kv :],
        vec[own : 2 * own],
        joined(0),
        joined(hidden),
        down_all,
        vec[2 * own : 3 * own],
    )


def solution(mesh):
    in_specs = (
        P(("rep", "shard"), None),
        P(("rep", "shard"), None),
        P(("rep", "shard"), None),
        P("shard", None),
        P("shard", None),
        P("shard", None),
        P("shard", None),
        P("shard"),
        P("shard"),
        P("shard"),
        P("shard"),
        P("shard", None),
        P("shard", None),
        P("shard", None),
        P("shard"),
    )
    out_specs = (
        P(("rep", "shard"), None),
        P(("rep", "shard"), None),
        P("shard", None),
        P("shard", None),
        P("shard", None),
        P("shard", None),
        P("shard"),
        P("shard"),
        P("shard"),
        P("shard"),
        P("shard", None),
        P("shard", None),
        P("shard", None),
        P("shard"),
    )
    return jax.shard_map(
        on_device, mesh=mesh, in_specs=in_specs, out_specs=out_specs, check_vma=False
    )
```

```python
import functools
import math

import jax
import jax.numpy as jnp
from jax import lax
from jax.experimental import pallas as pl
from jax.experimental.pallas import tpu as pltpu
from jax.sharding import PartitionSpec as P

HEADS = 14
KVH = 2
HD = 64


theta_base = 1000000.0
eps_norm = 1e-06
masked_score = -1000000000.0


def times_transposed(left, weight):
    return lax.dot_general(
        left, weight, (((1,), (1,)), ((), ())), preferred_element_type=jnp.float32
    )


def tables(lengths_row, rows):
    order = jnp.arange(lengths_row.shape[0])
    ends = jnp.sum(jnp.where(order[None, :] <= order[:, None], lengths_row[None, :], 0), axis=1)
    starts = ends - lengths_row
    places = jnp.arange(rows, dtype=jnp.int32)
    inside = ((places[:, None] >= starts[None, :]) & (places[:, None] < ends[None, :])).astype(
        jnp.int32
    )
    slots = jnp.arange(lengths_row.shape[0], dtype=jnp.int32)
    segment = jnp.sum(inside * slots[None, :], axis=1)
    first = jnp.sum(inside * starts[None, :], axis=1)
    offset = (places - first).astype(jnp.float32)
    half = HD // 2
    freq = theta_base ** (-(jnp.arange(half, dtype=jnp.float32) * (2.0 / HD)))
    angles = offset[:, None] * freq[None, :]
    return (segment, places, jnp.cos(angles), jnp.sin(angles))


def rotate(values, cosine, sine):
    half = values.shape[-1] // 2
    first, second = (values[..., :half], values[..., half:])
    cosine = cosine[:, :, None, :]
    sine = sine[:, :, None, :]
    return jnp.concatenate(
        [first * cosine - second * sine, second * cosine + first * sine], axis=-1
    )


def unrotate(grads, cosine, sine):
    half = grads.shape[-1] // 2
    first, second = (grads[..., :half], grads[..., half:])
    cosine = cosine[:, :, None, :]
    sine = sine[:, :, None, :]
    return jnp.concatenate(
        [first * cosine + second * sine, second * cosine - first * sine], axis=-1
    )


def norm_fwd(hidden, gain):
    scale = lax.rsqrt(jnp.mean(hidden * hidden, axis=-1, keepdims=True) + eps_norm)
    return (scale, hidden * scale * gain.astype(jnp.float32))


def norm_bwd(dnormed, hidden, scale, gain):
    gain_f = gain.astype(jnp.float32)
    dgain = jnp.sum(dnormed * hidden * scale, axis=0)
    inner = dnormed * gain_f
    dhidden = scale * inner - hidden * (scale * scale * scale) * jnp.mean(
        inner * hidden, axis=-1, keepdims=True
    )
    return (dhidden, dgain)


def scores_of(query, keys, segment, places):
    raw = jnp.einsum("igha,jga->ghij", query, keys, preferred_element_type=jnp.float32) * (
        1.0 / math.sqrt(HD)
    )
    allowed = (segment[:, None] == segment[None, :]) & (places[None, :] <= places[:, None])
    return jnp.where(allowed[None, None], raw, masked_score)


def attend(query, keys, values, segment, places):
    raw = scores_of(query, keys, segment, places)
    top = jnp.max(raw, axis=-1, keepdims=True)
    total = jnp.sum(jnp.exp(raw - top), axis=-1)
    lse = top[..., 0] + jnp.log(total)
    probs = jnp.exp(raw - lse[..., None]).astype(jnp.bfloat16)
    mixed = jnp.einsum("ghij,jga->igha", probs, values, preferred_element_type=jnp.float32).astype(
        jnp.bfloat16
    )
    return (mixed, lse)


def attend_back(query, keys, values, mixed, dmixed, lse, segment, places):
    raw = scores_of(query, keys, segment, places)
    probs_f = jnp.exp(raw - lse[..., None])
    probs = probs_f.astype(jnp.bfloat16)
    dvals = jnp.einsum("ghij,igha->jga", probs, dmixed, preferred_element_type=jnp.float32)
    dprobs = jnp.einsum("igha,jga->ghij", dmixed, values, preferred_element_type=jnp.float32)
    delta = jnp.einsum("igha,igha->ghi", dmixed, mixed, preferred_element_type=jnp.float32)
    dscores = (probs_f * (dprobs - delta[..., None]) * (1.0 / math.sqrt(HD))).astype(jnp.bfloat16)
    dquery = jnp.einsum("ghij,jga->igha", dscores, keys, preferred_element_type=jnp.float32)
    dkeys = jnp.einsum("ghij,igha->jga", dscores, query, preferred_element_type=jnp.float32)
    return (dquery, dkeys, dvals)


class Grid:
    def __init__(self):
        self.reps = lax.axis_size("rep")
        self.shards = lax.axis_size("shard")
        c = 2 if self.reps % 2 == 0 else 1
        x = self.reps // c
        y = x if self.shards % x == 0 else 1
        z = self.shards // y
        l = 2 if z % 2 == 0 else 1
        self.size = dict(x=x, c=c, h=z // l, l=l, y=y, z=z)
        rep, shard = lax.axis_index("rep"), lax.axis_index("shard")
        zz = shard // y
        self.at = dict(x=rep // c, c=rep % c, z=zz, y=shard % y, h=zz // l, l=zz % l)

    def send(self, value, **by):
        n = self.size
        pairs = []
        for rep in range(self.reps):
            for shard in range(self.shards):
                at = dict(x=rep // n["c"], c=rep % n["c"], z=shard // n["y"], y=shard % n["y"])
                if "h" in by or "l" in by:
                    h = (at["z"] // n["l"] + by.get("h", 0)) % n["h"]
                    at["z"] = h * n["l"] + (at["z"] + by.get("l", 0)) % n["l"]
                for d in "xczy":
                    at[d] = (at[d] + by.get(d, 0)) % n[d]
                pairs.append(
                    (
                        rep * self.shards + shard,
                        (at["x"] * n["c"] + at["c"]) * self.shards + at["z"] * n["y"] + at["y"],
                    )
                )
        return lax.ppermute(value, ("rep", "shard"), pairs)

    def peer(self, d, k):
        return (self.at[d] + k + self.size[d]) % self.size[d]

    def gather(self, value, d):
        out = jnp.zeros((self.size[d],) + value.shape, value.dtype)
        out = lax.dynamic_update_index_in_dim(out, value, self.at[d], 0)
        for k in range(1, self.size[d]):
            out = lax.dynamic_update_index_in_dim(
                out, self.send(value, **{d: k}), self.peer(d, -k), 0
            )
        return out

    def scatter(self, value, d):
        pick = lambda k: lax.dynamic_index_in_dim(value, self.peer(d, k), 0, keepdims=False)
        total = pick(0).astype(jnp.float32)
        for k in range(1, self.size[d]):
            total = total + self.send(pick(k), **{d: k}).astype(jnp.float32)
        return total.astype(value.dtype)


def by_permutes(
    tokens,
    cotangent,
    lengths,
    query_weight,
    key_weight,
    value_weight,
    output_weight,
    query_bias,
    key_bias,
    value_bias,
    attn_gain,
    gate_weight,
    up_weight,
    down_weight,
    mlp_gain,
):
    grid = Grid()
    size, at = grid.size, grid.at
    shards, reps = grid.shards, grid.reps
    rep = lax.axis_index("rep")
    rows, width = tokens.shape
    own = query_weight.shape[0]
    kvd = key_weight.shape[1]
    own_kv = key_bias.shape[0]
    f32, bf16 = jnp.float32, jnp.bfloat16
    wide = width + 2 * kvd
    total_w = wide + width
    quarter = total_w // reps

    small = jnp.concatenate([query_bias, attn_gain, mlp_gain, key_bias, value_bias])
    extra = 8
    small = jnp.pad(small, (0, extra * quarter - small.shape[0])).reshape(extra, quarter)
    packed = jnp.concatenate([query_weight, key_weight, value_weight, output_weight], axis=1)
    mine = lax.dynamic_slice(packed, (0, rep * quarter), (own, quarter))
    mine = jnp.concatenate([mine, small], axis=0)
    mine = grid.gather(mine, "z")
    mine = grid.gather(mine, "y")
    mine = grid.gather(mine, "x")
    mine = grid.gather(mine, "c")
    full = mine[..., :own, :].transpose(3, 2, 4, 1, 0, 5).reshape(width, total_w)
    qkv_weight = full[:, :wide]
    output_full = full[:, wide:]
    vectors = mine[0, 0, :, :, own:, :].transpose(1, 0, 2, 3).reshape(shards, extra * quarter)
    piece = lambda first, count: vectors[:, first : first + count].reshape(shards * count)
    query_bias_f, attn_gain_f, mlp_gain_f = (piece(i * own, own) for i in range(3))
    key_bias_f = piece(3 * own, own_kv)
    value_bias_f = piece(3 * own + own_kv, own_kv)
    qkv_bias = jnp.concatenate([query_bias_f, key_bias_f, value_bias_f]).astype(f32)

    part = down_weight.shape[0] // reps
    sets = size["l"] * size["y"]
    hidden = size["h"] * part

    def column_sets(weight):
        split = weight.reshape(own, size["h"], sets, reps, part)
        split = lax.dynamic_index_in_dim(split, rep, 3, keepdims=False)
        return split.transpose(2, 0, 1, 3).reshape(sets, own, hidden)

    both_sets = jnp.concatenate([column_sets(gate_weight), column_sets(up_weight)], axis=2)
    down_part = lax.dynamic_slice(down_weight, (rep * part, 0), (part, width))
    both_mine = jnp.zeros((size["h"], size["l"], size["y"], own, 2 * hidden), bf16)
    for kl in range(size["l"]):
        for ky in range(size["y"]):
            block = lax.dynamic_index_in_dim(
                both_sets, grid.peer("l", kl) * size["y"] + grid.peer("y", ky), 0, keepdims=False
            )
            for kh in range(size["h"]):
                got = block if kl + ky + kh == 0 else grid.send(block, h=kh, l=kl, y=ky)
                both_mine = lax.dynamic_update_slice(
                    both_mine,
                    got[None, None, None],
                    (grid.peer("h", -kh), grid.peer("l", -kl), grid.peer("y", -ky), 0, 0),
                )
    both_mine = both_mine.reshape(width, 2 * hidden)
    down_mine = grid.gather(down_part, "h").reshape(hidden, width)

    def gather_tokens(value):
        for d in "lyxc":
            value = grid.gather(value, d)
        return value.reshape(-1, width)

    def scatter_tokens(value):
        value = value.reshape(size["c"], size["x"], size["y"], size["l"], rows, -1)
        for d in "cxyl":
            value = grid.scatter(value, d)
        return value

    cot_all = gather_tokens(cotangent)

    segment, places, cosine, sine = jax.vmap(lambda lens: tables(lens, rows))(lengths)
    flat = tokens.astype(f32)
    scale_one, normed_one = norm_fwd(flat, attn_gain_f)
    normed_one = normed_one.astype(bf16)
    qkv = jnp.dot(normed_one, qkv_weight, preferred_element_type=f32) + qkv_bias
    query = rotate(qkv[:, :width].reshape(1, rows, HEADS, HD), cosine, sine).astype(bf16)
    query = query.reshape(1, rows, KVH, HEADS // KVH, HD)
    keys = rotate(qkv[:, width : width + kvd].reshape(1, rows, KVH, HD), cosine, sine).astype(bf16)
    values = qkv[:, width + kvd :].reshape(1, rows, KVH, HD).astype(bf16)
    mixed, lse = jax.vmap(attend)(query, keys, values, segment, places)
    mixed_flat = mixed.reshape(rows, width)
    hidden_one = flat + jnp.dot(mixed_flat, output_full, preferred_element_type=f32)
    scale_two, normed_two = norm_fwd(hidden_one, mlp_gain_f)
    normed_all = gather_tokens(normed_two.astype(bf16))

    dprod = times_transposed(cot_all, down_mine)
    both = jnp.dot(normed_all, both_mine, preferred_element_type=f32)
    gate, upper = both[:, :hidden], both[:, hidden:]
    sigma = jax.nn.sigmoid(gate)
    product = (gate * sigma * upper).astype(bf16)
    dgate = (dprod * upper * sigma * (1.0 + gate * (1.0 - sigma))).astype(bf16)
    dup = (dprod * gate * sigma).astype(bf16)
    dboth = jnp.concatenate([dgate, dup], axis=1)
    dnormed_part = times_transposed(dboth, both_mine).astype(bf16)
    out_part = jnp.dot(product, down_mine, preferred_element_type=f32).astype(bf16)
    dnormed_two = scatter_tokens(dnormed_part).astype(f32)
    out_sum = scatter_tokens(out_part).astype(f32)
    grad_both = jnp.dot(normed_all.T, dboth, preferred_element_type=f32).astype(bf16)
    grad_down = jnp.dot(product.T, cot_all, preferred_element_type=f32).astype(bf16)

    grad_both = grid.scatter(grad_both.reshape(size["h"], sets, own, 2 * hidden), "h")
    grad_down = grid.scatter(grad_down.reshape(size["h"], part, width), "h")
    owned = jnp.zeros((size["l"], size["y"], own, 2 * hidden), bf16)
    for kl in range(size["l"]):
        for ky in range(size["y"]):
            block = lax.dynamic_index_in_dim(
                grad_both, grid.peer("l", kl) * size["y"] + grid.peer("y", ky), 0, keepdims=False
            )
            got = block if kl + ky == 0 else grid.send(block, l=kl, y=ky)
            owned = lax.dynamic_update_slice(
                owned, got[None, None], (grid.peer("l", -kl), grid.peer("y", -ky), 0, 0)
            )

    def from_replicas(value):
        return grid.gather(grid.gather(value, "c"), "x").reshape((reps,) + value.shape)

    both_all = from_replicas(owned.reshape(sets, own, 2 * hidden))
    down_all = from_replicas(grad_down).reshape(reps * part, width).astype(f32)

    def joined(first):
        half = both_all[..., first : first + hidden].reshape(reps, sets, own, size["h"], part)
        return half.transpose(2, 3, 1, 0, 4).reshape(own, -1).astype(f32)

    result = (hidden_one + out_sum).astype(bf16)

    dh_two, grad_mlp_gain = norm_bwd(dnormed_two, hidden_one, scale_two, mlp_gain_f)
    dhidden = cotangent.astype(f32) + dh_two
    dres = dhidden.astype(bf16)
    grad_output = jnp.dot(mixed_flat.T, dres, preferred_element_type=f32).astype(bf16)
    dmixed = times_transposed(dres, output_full).astype(bf16)
    dmixed = dmixed.reshape(1, rows, KVH, HEADS // KVH, HD)
    dquery, dkeys, dvals = jax.vmap(attend_back)(
        query, keys, values, mixed, dmixed, lse, segment, places
    )
    dquery = unrotate(dquery.reshape(1, rows, HEADS, HD), cosine, sine).reshape(rows, width)
    dkeys = unrotate(dkeys, cosine, sine).reshape(rows, kvd)
    dvals = dvals.reshape(rows, kvd)
    dqkv = jnp.concatenate([dquery, dkeys, dvals], axis=1)
    grad_bias = jnp.sum(dqkv, axis=0)
    dqkv_b = dqkv.astype(bf16)
    grad_qkv = jnp.dot(normed_one.T, dqkv_b, preferred_element_type=f32).astype(bf16)
    dnormed_one = times_transposed(dqkv_b, qkv_weight)
    dh_one, grad_attn_gain = norm_bwd(dnormed_one, flat, scale_one, attn_gain_f)
    grad_input = dhidden + dh_one

    cut = lambda v, count: v.reshape(shards, count)
    small_g = jnp.concatenate(
        [
            cut(grad_bias[:width], own),
            cut(grad_attn_gain, own),
            cut(grad_mlp_gain, own),
            cut(grad_bias[width : width + kvd], own_kv),
            cut(grad_bias[width + kvd :], own_kv),
        ],
        axis=1,
    )
    small_n = small_g.shape[1]
    small_g = jnp.pad(small_g, ((0, 0), (0, extra * quarter - small_n)))
    small_g = jnp.broadcast_to(
        small_g.reshape(shards, 1, extra, quarter).astype(bf16), (shards, reps, extra, quarter)
    )
    grads = jnp.concatenate([grad_qkv, grad_output], axis=1)
    grads = grads.reshape(shards, own, reps, quarter).transpose(0, 2, 1, 3)
    grads = jnp.concatenate([grads, small_g], axis=2)
    grads = grads.reshape(size["z"], size["y"], size["x"], size["c"], own + extra, quarter)
    grads = grid.scatter(grads.transpose(3, 2, 1, 0, 4, 5), "c")
    grads = grid.scatter(grads, "x")
    grads = grid.scatter(grads, "y")
    grads = grid.scatter(grads, "z")
    vec = grads[own:].reshape(extra * quarter)[:small_n].astype(f32)
    attn_all = from_replicas(grads[:own]).transpose(1, 0, 2).reshape(own, total_w).astype(f32)

    return (
        result,
        grad_input,
        attn_all[:, :width],
        attn_all[:, width : width + kvd],
        attn_all[:, width + kvd : wide],
        attn_all[:, wide:],
        vec[:own],
        vec[3 * own : 3 * own + own_kv],
        vec[3 * own + own_kv :],
        vec[own : 2 * own],
        joined(0),
        joined(hidden),
        down_all,
        vec[2 * own : 3 * own],
    )


def attend_back_from(query, keys, values, mixed, dmixed, probs_f):
    probs = probs_f.astype(jnp.bfloat16)
    dvals = jnp.einsum("ghij,igha->jga", probs, dmixed, preferred_element_type=jnp.float32)
    dprobs = jnp.einsum("igha,jga->ghij", dmixed, values, preferred_element_type=jnp.float32)
    delta = jnp.einsum("igha,igha->ghi", dmixed, mixed, preferred_element_type=jnp.float32)
    dscores = (probs_f * (dprobs - delta[..., None]) * (1.0 / math.sqrt(HD))).astype(jnp.bfloat16)
    dquery = jnp.einsum("ghij,jga->igha", dscores, keys, preferred_element_type=jnp.float32)
    dkeys = jnp.einsum("ghij,igha->jga", dscores, query, preferred_element_type=jnp.float32)
    return (dquery, dkeys, dvals)


MESH = pl.DeviceIdType.MESH
TN = (((1,), (1,)), ((), ()))
NN = (((1,), (0,)), ((), ()))
CN = (((0,), (0,)), ((), ()))


def mm(left, right, dims=NN):
    return lax.dot_general(left, right, dims, preferred_element_type=jnp.float32)


class Place:
    def __init__(self, size):
        self.size = size
        rep, shard = lax.axis_index("rep"), lax.axis_index("shard")
        z = shard // size["y"]
        self.at = dict(
            x=rep // size["c"],
            c=rep % size["c"],
            z=z,
            y=shard % size["y"],
            h=z // size["l"],
            l=z % size["l"],
        )

    def peer(self, d, k):
        return (self.at[d] + k + self.size[d]) % self.size[d]

    def device(self, **by):
        at = dict(self.at)
        for d, k in by.items():
            at[d] = self.peer(d, k)
        if "h" in by or "l" in by:
            at["z"] = at["h"] * self.size["l"] + at["l"]
        return (at["x"] * self.size["c"] + at["c"], at["z"] * self.size["y"] + at["y"])

    def greet(self, everyone):
        barrier = pltpu.get_barrier_semaphore()
        for by in everyone:
            pl.semaphore_signal(barrier, inc=1, device_id=self.device(**by), device_id_type=MESH)
        pl.semaphore_wait(barrier, len(everyone))


class Traffic:
    def __init__(self, place, send, recv):
        self.place, self.send, self.recv, self.used, self.sent = place, send, recv, 0, []

    def start(self, src, dst, arriving, **by):
        i = self.used
        self.used += 1
        copy = pltpu.make_async_remote_copy(
            src_ref=src,
            dst_ref=dst,
            send_sem=self.send.at[i],
            recv_sem=self.recv.at[i],
            device_id=self.place.device(**by),
            device_id_type=MESH,
        )
        copy.start()
        self.sent.append(copy)
        return pltpu.make_async_remote_copy(
            src_ref=arriving,
            dst_ref=arriving,
            send_sem=self.send.at[i],
            recv_sem=self.recv.at[i],
            device_id=self.place.device(**by),
            device_id_type=MESH,
        ).wait_recv

    def finish(self):
        for copy in self.sent:
            copy.wait_send()


def around(size):
    others = [
        dict(h=h, l=l, y=y)
        for h in range(size["h"])
        for l in range(size["l"])
        for y in range(size["y"])
        if h + l + y
    ]
    return others + [dict(x=k) for k in range(1, size["x"])] + [dict(c=k) for k in range(1, size["c"])]


def row_parts(rows):
    step = -(-rows // 48) * 16
    return [(0, step), (step, step), (2 * step, rows - 2 * step)]


def token_gather(place, traffic, buf, rows, dims):
    names = "xcyl"
    at = place.at

    def region(held, **fixed):
        index = []
        for d in names:
            if d in fixed:
                index.append(fixed[d])
            elif d in held:
                index.append(pl.ds(0, place.size[d]))
            else:
                index.append(at[d])
        return buf.at[tuple(index) + (pl.ds(*rows),)]

    def cores(held, **fixed):
        here = region(held, **fixed)
        return [
            traffic.start(here, here, region(held, **{**fixed, "c": place.peer("c", -k)}), c=k)
            for k in range(1, place.size["c"])
        ]

    last = cores("")
    held = ""
    for d in dims:
        here = region(held)
        got = [
            (k, traffic.start(here, here, region(held, **{d: place.peer(d, -k)}), **{d: k}))
            for k in range(1, place.size[d])
        ]
        yield
        for k, wait in got:
            wait()
            last += cores(held, **{d: place.peer(d, -k)})
        held += d
    yield
    for wait in last:
        wait()


def lanes_of(count, width):
    return lax.broadcasted_iota(jnp.int32, (count, width), 1)


def turn(value):
    count, width = value.shape
    half = HD // 2
    first = lanes_of(count, width) % HD < half
    return jnp.where(first, pltpu.roll(value, width - half, 1), pltpu.roll(value, half, 1))


def position_tables(lengths_ref, freq, rows):
    i0 = lax.broadcasted_iota(jnp.int32, (rows, rows), 0)
    i1 = lax.broadcasted_iota(jnp.int32, (rows, rows), 1)
    first0, first1 = jnp.zeros_like(i0), jnp.zeros_like(i1)
    end = jnp.int32(0)
    for j in range(lengths_ref.shape[1]):
        count = lengths_ref[0, j]
        end = end + count
        first0 = first0 + jnp.where(i0 >= end, count, 0)
        first1 = first1 + jnp.where(i1 >= end, count, 0)
    allowed = (first0 == first1) & (i1 <= i0)
    angle = (i0 - first0).astype(jnp.float32) * freq
    sign = jnp.where(lanes_of(rows, rows) % HD < HD // 2, -1.0, 1.0)
    return allowed, jnp.cos(angle), jnp.sin(angle) * sign


def columns(first, count, quarter):
    out = []
    while count:
        share, inside = first // quarter, first % quarter
        step = min(count, quarter - inside)
        out.append((share, inside, step))
        first, count = first + step, count - step
    return out


def pair_of(keys, pair):
    group = HEADS // KVH
    low, high = 2 * pair // group, (2 * pair + 1) // group
    if (low, high) == (0, 1):
        return keys
    other = pltpu.roll(keys.astype(jnp.float32), HD, 1).astype(keys.dtype)
    lo = lanes_of(*keys.shape) < HD
    return jnp.where(lo, keys, other) if low == 0 else jnp.where(lo, other, keys)


def halves(value):
    lo = lanes_of(*value.shape) < HD
    zero = jnp.zeros_like(value)
    return jnp.where(lo, value, zero), jnp.where(lo, zero, value)


def front_kernel(
    size,
    lengths_ref,
    tokens_ref,
    cot_ref,
    mine_ref,
    small_ref,
    freq_ref,
    sets_ref,
    down_ref,
    att_ref,
    small_all_ref,
    both_ref,
    down_all_ref,
    cot_all_ref,
    norm_all_ref,
    vec_ref,
    normed_ref,
    query_ref,
    keys_ref,
    values_ref,
    mixed_ref,
    probs_ref,
    hidden_ref,
    send,
    recv,
):
    f32, bf16 = jnp.float32, jnp.bfloat16
    place = Place(size)
    at, peer = place.at, place.peer
    traffic = Traffic(place, send, recv)
    rows, width = tokens_ref.shape
    own, quarter = mine_ref.shape
    kvd = keys_ref.shape[1]
    small_all_ref[at["z"], at["y"]] = small_ref[...]
    att_ref[at["x"], at["c"], at["z"], at["y"]] = mine_ref[...]
    cot_all_ref[at["x"], at["c"], at["y"], at["l"]] = cot_ref[...]
    q_own = at["l"] * size["y"] + at["y"]
    both_ref[at["h"], at["l"], at["y"]] = sets_ref[q_own]
    down_all_ref[at["h"]] = down_ref[...]
    place.greet(around(size))

    def block(z, y, x=None, c=None):
        return att_ref.at[at["x"] if x is None else x, at["c"] if c is None else c, z, y]

    def to_core(z, y, x):
        return [
            traffic.start(block(z, y, x), block(z, y, x), block(z, y, x, peer("c", -k)), c=k)
            for k in range(1, size["c"])
        ]

    def to_x(z, y):
        return [
            (traffic.start(block(z, y), block(z, y), block(z, y, peer("x", -k)), x=k), z, y, peer("x", -k))
            for k in range(1, size["x"])
        ]

    def to_y(z):
        return [
            (traffic.start(block(z, at["y"]), block(z, at["y"]), block(z, peer("y", -k)), y=k), z, peer("y", -k))
            for k in range(1, size["y"])
        ]

    z, y = at["z"], at["y"]
    mine = block(z, y)
    from_z = [
        (traffic.start(mine, mine, block(peer("z", -k), y), z=k), peer("z", -k))
        for k in range(1, size["z"])
    ]
    from_y, from_x = to_y(z), to_x(z, y)
    waits = to_core(z, y, at["x"])
    small_waits = []
    for by in around(size):
        if "h" in by:
            here = small_all_ref.at[z, y]
            there = small_all_ref.at[peer("h", -by["h"]) * size["l"] + peer("l", -by["l"]), peer("y", -by["y"])]
            small_waits.append(traffic.start(here, here, there, **by))
    cot_steps = token_gather(place, traffic, cot_all_ref, (0, rows), "lxy")
    next(cot_steps)

    flat = tokens_ref[...].astype(f32)
    scale = lax.rsqrt(jnp.mean(flat * flat, axis=1, keepdims=True) + eps_norm)
    allowed, cosine, sine = position_tables(lengths_ref, freq_ref[0:1, :], rows)

    for wait, zz in from_z:
        wait()
        from_y += to_y(zz)
        from_x += to_x(zz, y)
        waits += to_core(zz, y, at["x"])

    ff_waits = []
    for by in around(size):
        if "h" in by:
            q = peer("l", by["l"]) * size["y"] + peer("y", by["y"])
            ff_waits.append(
                traffic.start(
                    sets_ref.at[q],
                    both_ref.at[at["h"], at["l"], at["y"]],
                    both_ref.at[peer("h", -by["h"]), peer("l", -by["l"]), peer("y", -by["y"])],
                    **by,
                )
            )
    for k in range(1, size["h"]):
        ff_waits.append(
            traffic.start(down_ref, down_all_ref.at[at["h"]], down_all_ref.at[peer("h", -k)], h=k)
        )

    for wait, zz, yy in from_y:
        wait()
        from_x += to_x(zz, yy)
        waits += to_core(zz, yy, at["x"])
    next(cot_steps)
    for wait, zz, yy, xx in from_x:
        wait()
        waits += to_core(zz, yy, xx)
    next(cot_steps)
    for wait in small_waits + waits:
        wait()

    own_kv = kvd // (size["z"] * size["y"])
    vec = jnp.zeros((8, width), f32)
    kv = jnp.zeros((8, kvd), f32)
    for s in range(size["z"] * size["y"]):
        piece = small_all_ref[s // size["y"], s % size["y"]]
        piece_w = jnp.where(lanes_of(8, piece.shape[1]) < own, piece, 0.0)
        wider = jnp.concatenate([piece_w, jnp.zeros((8, width - piece.shape[1]), f32)], axis=1)
        vec = vec + (pltpu.roll(wider, s * own, 1) if s else wider)
        piece_kv = jnp.where(lanes_of(8, kvd) < own_kv, piece[:, :kvd], 0.0)
        kv = kv + (pltpu.roll(piece_kv, s * own_kv, 1) if s else piece_kv)
    vec_ref[...] = vec

    def weight(share, first, count):
        x, c = share // size["c"], share % size["c"]
        return att_ref[x, c, :, :, :, first : first + count].reshape(width, count)

    def project(left, first, count):
        return jnp.concatenate(
            [mm(left, weight(*piece)) for piece in columns(first, count, quarter)], axis=1
        )

    normed = (flat * scale * vec[1:2, :]).astype(bf16)
    normed_ref[...] = normed
    times = width // rows
    wide_cos = jnp.concatenate([cosine] * times, axis=1)
    wide_sin = jnp.concatenate([sine] * times, axis=1)
    query = project(normed, 0, width) + vec[0:1, :]
    query = (query * wide_cos + turn(query) * wide_sin).astype(bf16)
    query_ref[...] = query
    keys = project(normed, width, kvd) + kv[3:4, :]
    keys = (keys * cosine + turn(keys) * sine).astype(bf16)
    keys_ref[...] = keys
    values = (project(normed, width + kvd, kvd) + kv[4:5, :]).astype(bf16)
    values_ref[...] = values

    for pair in range(HEADS // 2):
        lanes = pl.ds(pair * 2 * HD, 2 * HD)
        kp, vp = pair_of(keys, pair), pair_of(values, pair)
        total = None
        for i, (qh, vh) in enumerate(zip(halves(query_ref[:, lanes]), halves(vp))):
            raw = jnp.where(allowed, mm(qh, kp, TN) * (1.0 / math.sqrt(HD)), masked_score)
            top = jnp.max(raw, axis=1, keepdims=True)
            lse = top + jnp.log(jnp.sum(jnp.exp(raw - top), axis=1, keepdims=True))
            probs = jnp.exp(raw - lse)
            probs_ref[2 * pair + i] = probs
            part = mm(probs.astype(bf16), vh)
            total = part if total is None else total + part
        mixed_ref[:, lanes] = total.astype(bf16)

    hidden = flat + project(mixed_ref[...], width + 2 * kvd, width)
    hidden_ref[...] = hidden
    scale_two = lax.rsqrt(jnp.mean(hidden * hidden, axis=1, keepdims=True) + eps_norm)
    norm_all_ref[at["x"], at["c"], at["y"], at["l"]] = (hidden * scale_two * vec[2:3, :]).astype(bf16)
    steps = [
        token_gather(place, traffic, norm_all_ref, part, dims)
        for part, dims in zip(row_parts(rows), ("lxy", "xyl", "ylx"))
    ]
    for _ in range(4):
        for step in steps:
            next(step, None)
    for step in [cot_steps, *steps]:
        for _ in step:
            pass
    for wait in ff_waits:
        wait()
    traffic.finish()


def front(size, lengths, tokens, cot, mine, small, sets, down):
    f32, bf16 = jnp.float32, jnp.bfloat16
    rows, width = tokens.shape
    own, quarter = mine.shape
    kvd = 2 * HD
    n = size
    freq = theta_base ** (-((jnp.arange(rows) % (HD // 2)).astype(f32) * (2.0 / HD)))
    freq = jnp.broadcast_to(freq[None, :], (8, rows))
    group = (n["x"], n["c"], n["y"], n["l"])
    shapes = [
        ((n["x"], n["c"], n["z"], n["y"], own, quarter), bf16),
        ((n["z"], n["y"]) + small.shape, f32),
        ((n["h"], n["l"], n["y"]) + sets.shape[1:], bf16),
        ((n["h"],) + down.shape, bf16),
        (group + (rows, width), bf16),
        (group + (rows, width), bf16),
        ((8, width), f32),
        ((rows, width), bf16),
        ((rows, width), bf16),
        ((rows, kvd), bf16),
        ((rows, kvd), bf16),
        ((rows, width), bf16),
        ((HEADS, rows, rows), f32),
        ((rows, width), f32),
    ]
    vmem = pl.BlockSpec(memory_space=pltpu.VMEM)
    return pl.pallas_call(
        functools.partial(front_kernel, size),
        out_shape=[jax.ShapeDtypeStruct(*s) for s in shapes],
        in_specs=[pl.BlockSpec(memory_space=pltpu.SMEM)] + [vmem] * 7,
        out_specs=[vmem] * len(shapes),
        scratch_shapes=[pltpu.SemaphoreType.DMA((96,)), pltpu.SemaphoreType.DMA((96,))],
        compiler_params=pltpu.CompilerParams(
            collective_id=1, has_side_effects=True, vmem_limit_bytes=56 << 20
        ),
    )(lengths, tokens, cot, mine, small, freq, sets, down)


def by_kernels(
    tokens,
    cotangent,
    lengths,
    query_weight,
    key_weight,
    value_weight,
    output_weight,
    query_bias,
    key_bias,
    value_bias,
    attn_gain,
    gate_weight,
    up_weight,
    down_weight,
    mlp_gain,
):
    grid = Grid()
    size, at = grid.size, grid.at
    shards, reps = grid.shards, grid.reps
    rep = lax.axis_index("rep")
    rows, width = tokens.shape
    own = query_weight.shape[0]
    kvd = key_weight.shape[1]
    own_kv = key_bias.shape[0]
    f32, bf16 = jnp.float32, jnp.bfloat16
    wide = width + 2 * kvd
    total_w = wide + width
    quarter = total_w // reps

    part = down_weight.shape[0] // reps
    sets = size["l"] * size["y"]
    hidden = size["h"] * part

    packed = jnp.concatenate([query_weight, key_weight, value_weight, output_weight], axis=1)
    mine = lax.dynamic_slice(packed, (0, rep * quarter), (own, quarter))
    lane = lambda v: jnp.pad(v.astype(f32), (0, 128 - v.shape[0]))
    small = jnp.stack([lane(v) for v in (query_bias, attn_gain, mlp_gain, key_bias, value_bias)])
    small = jnp.pad(small, ((0, 8 - small.shape[0]), (0, 0)))

    def column_sets(weight):
        split = weight.reshape(own, size["h"], sets, reps, part)
        split = lax.dynamic_index_in_dim(split, rep, 3, keepdims=False)
        return split.transpose(2, 0, 1, 3).reshape(sets, own, hidden)

    both_sets = jnp.concatenate([column_sets(gate_weight), column_sets(up_weight)], axis=2)
    down_part = lax.dynamic_slice(down_weight, (rep * part, 0), (part, width))
    (att, _, both_mine, down_mine, cot_all, normed_all, vec, normed_one, query_f, keys_f, values_f, mixed_flat, probs_f, hidden_one) = front(
        size, lengths, tokens, cotangent, mine, small, both_sets, down_part
    )
    both_mine = both_mine.reshape(width, 2 * hidden)
    down_mine = down_mine.reshape(hidden, width)
    cot_all = cot_all.reshape(-1, width)
    normed_all = normed_all.reshape(-1, width)
    extra = 8
    full = att.transpose(2, 3, 4, 0, 1, 5).reshape(width, total_w)
    qkv_weight, output_full = full[:, :wide], full[:, wide:]
    attn_gain_f, mlp_gain_f = vec[1], vec[2]
    segment, places, cosine, sine = jax.vmap(lambda lens: tables(lens, rows))(lengths)
    flat = tokens.astype(f32)
    scale_one = lax.rsqrt(jnp.mean(flat * flat, axis=-1, keepdims=True) + eps_norm)
    scale_two = lax.rsqrt(jnp.mean(hidden_one * hidden_one, axis=-1, keepdims=True) + eps_norm)
    query = query_f.reshape(1, rows, KVH, HEADS // KVH, HD)
    keys = keys_f.reshape(1, rows, KVH, HD)
    values = values_f.reshape(1, rows, KVH, HD)
    mixed = mixed_flat.reshape(1, rows, KVH, HEADS // KVH, HD)
    probs_f = probs_f.reshape(1, KVH, HEADS // KVH, rows, rows)

    def scatter_tokens(value):
        value = value.reshape(size["x"], size["c"], size["y"], size["l"], rows, -1).transpose(1, 0, 2, 3, 4, 5)
        for d in "cxyl":
            value = grid.scatter(value, d)
        return value

    dprod = times_transposed(cot_all, down_mine)
    both = jnp.dot(normed_all, both_mine, preferred_element_type=f32)
    gate, upper = both[:, :hidden], both[:, hidden:]
    sigma = jax.nn.sigmoid(gate)
    product = (gate * sigma * upper).astype(bf16)
    dgate = (dprod * upper * sigma * (1.0 + gate * (1.0 - sigma))).astype(bf16)
    dup = (dprod * gate * sigma).astype(bf16)
    dboth = jnp.concatenate([dgate, dup], axis=1)
    dnormed_part = times_transposed(dboth, both_mine).astype(bf16)
    out_part = jnp.dot(product, down_mine, preferred_element_type=f32).astype(bf16)
    dnormed_two = scatter_tokens(dnormed_part).astype(f32)
    out_sum = scatter_tokens(out_part).astype(f32)
    grad_both = jnp.dot(normed_all.T, dboth, preferred_element_type=f32).astype(bf16)
    grad_down = jnp.dot(product.T, cot_all, preferred_element_type=f32).astype(bf16)

    grad_both = grid.scatter(grad_both.reshape(size["h"], sets, own, 2 * hidden), "h")
    grad_down = grid.scatter(grad_down.reshape(size["h"], part, width), "h")
    owned = jnp.zeros((size["l"], size["y"], own, 2 * hidden), bf16)
    for kl in range(size["l"]):
        for ky in range(size["y"]):
            block = lax.dynamic_index_in_dim(
                grad_both, grid.peer("l", kl) * size["y"] + grid.peer("y", ky), 0, keepdims=False
            )
            got = block if kl + ky == 0 else grid.send(block, l=kl, y=ky)
            owned = lax.dynamic_update_slice(
                owned, got[None, None], (grid.peer("l", -kl), grid.peer("y", -ky), 0, 0)
            )

    def from_replicas(value):
        return grid.gather(grid.gather(value, "c"), "x").reshape((reps,) + value.shape)

    both_all = from_replicas(owned.reshape(sets, own, 2 * hidden))
    down_all = from_replicas(grad_down).reshape(reps * part, width).astype(f32)

    def joined(first):
        half = both_all[..., first : first + hidden].reshape(reps, sets, own, size["h"], part)
        return half.transpose(2, 3, 1, 0, 4).reshape(own, -1).astype(f32)

    result = (hidden_one + out_sum).astype(bf16)

    dh_two, grad_mlp_gain = norm_bwd(dnormed_two, hidden_one, scale_two, mlp_gain_f)
    dhidden = cotangent.astype(f32) + dh_two
    dres = dhidden.astype(bf16)
    grad_output = jnp.dot(mixed_flat.T, dres, preferred_element_type=f32).astype(bf16)
    dmixed = times_transposed(dres, output_full).astype(bf16)
    dmixed = dmixed.reshape(1, rows, KVH, HEADS // KVH, HD)
    dquery, dkeys, dvals = jax.vmap(attend_back_from)(
        query, keys, values, mixed, dmixed, probs_f
    )
    dquery = unrotate(dquery.reshape(1, rows, HEADS, HD), cosine, sine).reshape(rows, width)
    dkeys = unrotate(dkeys, cosine, sine).reshape(rows, kvd)
    dvals = dvals.reshape(rows, kvd)
    dqkv = jnp.concatenate([dquery, dkeys, dvals], axis=1)
    grad_bias = jnp.sum(dqkv, axis=0)
    dqkv_b = dqkv.astype(bf16)
    grad_qkv = jnp.dot(normed_one.T, dqkv_b, preferred_element_type=f32).astype(bf16)
    dnormed_one = times_transposed(dqkv_b, qkv_weight)
    dh_one, grad_attn_gain = norm_bwd(dnormed_one, flat, scale_one, attn_gain_f)
    grad_input = dhidden + dh_one

    cut = lambda v, count: v.reshape(shards, count)
    small_g = jnp.concatenate(
        [
            cut(grad_bias[:width], own),
            cut(grad_attn_gain, own),
            cut(grad_mlp_gain, own),
            cut(grad_bias[width : width + kvd], own_kv),
            cut(grad_bias[width + kvd :], own_kv),
        ],
        axis=1,
    )
    small_n = small_g.shape[1]
    small_g = jnp.pad(small_g, ((0, 0), (0, extra * quarter - small_n)))
    small_g = jnp.broadcast_to(
        small_g.reshape(shards, 1, extra, quarter).astype(bf16), (shards, reps, extra, quarter)
    )
    grads = jnp.concatenate([grad_qkv, grad_output], axis=1)
    grads = grads.reshape(shards, own, reps, quarter).transpose(0, 2, 1, 3)
    grads = jnp.concatenate([grads, small_g], axis=2)
    grads = grads.reshape(size["z"], size["y"], size["x"], size["c"], own + extra, quarter)
    grads = grid.scatter(grads.transpose(3, 2, 1, 0, 4, 5), "c")
    grads = grid.scatter(grads, "x")
    grads = grid.scatter(grads, "y")
    grads = grid.scatter(grads, "z")
    vec = grads[own:].reshape(extra * quarter)[:small_n].astype(f32)
    attn_all = from_replicas(grads[:own]).transpose(1, 0, 2).reshape(own, total_w).astype(f32)

    return (
        result,
        grad_input,
        attn_all[:, :width],
        attn_all[:, width : width + kvd],
        attn_all[:, width + kvd : wide],
        attn_all[:, wide:],
        vec[:own],
        vec[3 * own : 3 * own + own_kv],
        vec[3 * own + own_kv :],
        vec[own : 2 * own],
        joined(0),
        joined(hidden),
        down_all,
        vec[2 * own : 3 * own],
    )


def on_device(*args):
    tokens, query_weight, key_weight = args[0], args[3], args[4]
    rows, width = tokens.shape
    total_w = 2 * width + 2 * key_weight.shape[1]
    fits = (
        rows == 2 * HD
        and key_weight.shape[1] == 2 * HD
        and query_weight.shape[0] % 16 == 0
        and query_weight.shape[0] <= 128
        and (total_w // lax.axis_size("rep")) % 128 == 0
    )
    return by_kernels(*args) if fits else by_permutes(*args)


def solution(mesh):
    in_specs = (
        P(("rep", "shard"), None),
        P(("rep", "shard"), None),
        P(("rep", "shard"), None),
        P("shard", None),
        P("shard", None),
        P("shard", None),
        P("shard", None),
        P("shard"),
        P("shard"),
        P("shard"),
        P("shard"),
        P("shard", None),
        P("shard", None),
        P("shard", None),
        P("shard"),
    )
    out_specs = (
        P(("rep", "shard"), None),
        P(("rep", "shard"), None),
        P("shard", None),
        P("shard", None),
        P("shard", None),
        P("shard", None),
        P("shard"),
        P("shard"),
        P("shard"),
        P("shard"),
        P("shard", None),
        P("shard", None),
        P("shard", None),
        P("shard"),
    )
    return jax.shard_map(
        on_device, mesh=mesh, in_specs=in_specs, out_specs=out_specs, check_vma=False
    )
```

```python
import functools
import math

import jax
import jax.numpy as jnp
from jax import lax
from jax.experimental import pallas as pl
from jax.experimental.pallas import tpu as pltpu
from jax.sharding import PartitionSpec as P

HEADS = 14
KVH = 2
HD = 64


theta_base = 1000000.0
eps_norm = 1e-06
masked_score = -1000000000.0


def times_transposed(left, weight):
    return lax.dot_general(
        left, weight, (((1,), (1,)), ((), ())), preferred_element_type=jnp.float32
    )


def tables(lengths_row, rows):
    order = jnp.arange(lengths_row.shape[0])
    ends = jnp.sum(jnp.where(order[None, :] <= order[:, None], lengths_row[None, :], 0), axis=1)
    starts = ends - lengths_row
    places = jnp.arange(rows, dtype=jnp.int32)
    inside = ((places[:, None] >= starts[None, :]) & (places[:, None] < ends[None, :])).astype(
        jnp.int32
    )
    slots = jnp.arange(lengths_row.shape[0], dtype=jnp.int32)
    segment = jnp.sum(inside * slots[None, :], axis=1)
    first = jnp.sum(inside * starts[None, :], axis=1)
    offset = (places - first).astype(jnp.float32)
    half = HD // 2
    freq = theta_base ** (-(jnp.arange(half, dtype=jnp.float32) * (2.0 / HD)))
    angles = offset[:, None] * freq[None, :]
    return (segment, places, jnp.cos(angles), jnp.sin(angles))


def rotate(values, cosine, sine):
    half = values.shape[-1] // 2
    first, second = (values[..., :half], values[..., half:])
    cosine = cosine[:, :, None, :]
    sine = sine[:, :, None, :]
    return jnp.concatenate(
        [first * cosine - second * sine, second * cosine + first * sine], axis=-1
    )


def unrotate(grads, cosine, sine):
    half = grads.shape[-1] // 2
    first, second = (grads[..., :half], grads[..., half:])
    cosine = cosine[:, :, None, :]
    sine = sine[:, :, None, :]
    return jnp.concatenate(
        [first * cosine + second * sine, second * cosine - first * sine], axis=-1
    )


def norm_fwd(hidden, gain):
    scale = lax.rsqrt(jnp.mean(hidden * hidden, axis=-1, keepdims=True) + eps_norm)
    return (scale, hidden * scale * gain.astype(jnp.float32))


def norm_bwd(dnormed, hidden, scale, gain):
    gain_f = gain.astype(jnp.float32)
    dgain = jnp.sum(dnormed * hidden * scale, axis=0)
    inner = dnormed * gain_f
    dhidden = scale * inner - hidden * (scale * scale * scale) * jnp.mean(
        inner * hidden, axis=-1, keepdims=True
    )
    return (dhidden, dgain)


def scores_of(query, keys, segment, places):
    raw = jnp.einsum("igha,jga->ghij", query, keys, preferred_element_type=jnp.float32) * (
        1.0 / math.sqrt(HD)
    )
    allowed = (segment[:, None] == segment[None, :]) & (places[None, :] <= places[:, None])
    return jnp.where(allowed[None, None], raw, masked_score)


def attend(query, keys, values, segment, places):
    raw = scores_of(query, keys, segment, places)
    top = jnp.max(raw, axis=-1, keepdims=True)
    total = jnp.sum(jnp.exp(raw - top), axis=-1)
    lse = top[..., 0] + jnp.log(total)
    probs = jnp.exp(raw - lse[..., None]).astype(jnp.bfloat16)
    mixed = jnp.einsum("ghij,jga->igha", probs, values, preferred_element_type=jnp.float32).astype(
        jnp.bfloat16
    )
    return (mixed, lse)


def attend_back(query, keys, values, mixed, dmixed, lse, segment, places):
    raw = scores_of(query, keys, segment, places)
    probs_f = jnp.exp(raw - lse[..., None])
    probs = probs_f.astype(jnp.bfloat16)
    dvals = jnp.einsum("ghij,igha->jga", probs, dmixed, preferred_element_type=jnp.float32)
    dprobs = jnp.einsum("igha,jga->ghij", dmixed, values, preferred_element_type=jnp.float32)
    delta = jnp.einsum("igha,igha->ghi", dmixed, mixed, preferred_element_type=jnp.float32)
    dscores = (probs_f * (dprobs - delta[..., None]) * (1.0 / math.sqrt(HD))).astype(jnp.bfloat16)
    dquery = jnp.einsum("ghij,jga->igha", dscores, keys, preferred_element_type=jnp.float32)
    dkeys = jnp.einsum("ghij,igha->jga", dscores, query, preferred_element_type=jnp.float32)
    return (dquery, dkeys, dvals)


class Grid:
    def __init__(self):
        self.reps = lax.axis_size("rep")
        self.shards = lax.axis_size("shard")
        c = 2 if self.reps % 2 == 0 else 1
        x = self.reps // c
        y = x if self.shards % x == 0 else 1
        z = self.shards // y
        l = 2 if z % 2 == 0 else 1
        self.size = dict(x=x, c=c, h=z // l, l=l, y=y, z=z)
        rep, shard = lax.axis_index("rep"), lax.axis_index("shard")
        zz = shard // y
        self.at = dict(x=rep // c, c=rep % c, z=zz, y=shard % y, h=zz // l, l=zz % l)

    def send(self, value, **by):
        n = self.size
        pairs = []
        for rep in range(self.reps):
            for shard in range(self.shards):
                at = dict(x=rep // n["c"], c=rep % n["c"], z=shard // n["y"], y=shard % n["y"])
                if "h" in by or "l" in by:
                    h = (at["z"] // n["l"] + by.get("h", 0)) % n["h"]
                    at["z"] = h * n["l"] + (at["z"] + by.get("l", 0)) % n["l"]
                for d in "xczy":
                    at[d] = (at[d] + by.get(d, 0)) % n[d]
                pairs.append(
                    (
                        rep * self.shards + shard,
                        (at["x"] * n["c"] + at["c"]) * self.shards + at["z"] * n["y"] + at["y"],
                    )
                )
        return lax.ppermute(value, ("rep", "shard"), pairs)

    def peer(self, d, k):
        return (self.at[d] + k + self.size[d]) % self.size[d]

    def gather(self, value, d):
        out = jnp.zeros((self.size[d],) + value.shape, value.dtype)
        out = lax.dynamic_update_index_in_dim(out, value, self.at[d], 0)
        for k in range(1, self.size[d]):
            out = lax.dynamic_update_index_in_dim(
                out, self.send(value, **{d: k}), self.peer(d, -k), 0
            )
        return out

    def scatter(self, value, d):
        pick = lambda k: lax.dynamic_index_in_dim(value, self.peer(d, k), 0, keepdims=False)
        total = pick(0).astype(jnp.float32)
        for k in range(1, self.size[d]):
            total = total + self.send(pick(k), **{d: k}).astype(jnp.float32)
        return total.astype(value.dtype)


def by_permutes(
    tokens,
    cotangent,
    lengths,
    query_weight,
    key_weight,
    value_weight,
    output_weight,
    query_bias,
    key_bias,
    value_bias,
    attn_gain,
    gate_weight,
    up_weight,
    down_weight,
    mlp_gain,
):
    grid = Grid()
    size, at = grid.size, grid.at
    shards, reps = grid.shards, grid.reps
    rep = lax.axis_index("rep")
    rows, width = tokens.shape
    own = query_weight.shape[0]
    kvd = key_weight.shape[1]
    own_kv = key_bias.shape[0]
    f32, bf16 = jnp.float32, jnp.bfloat16
    wide = width + 2 * kvd
    total_w = wide + width
    quarter = total_w // reps

    small = jnp.concatenate([query_bias, attn_gain, mlp_gain, key_bias, value_bias])
    extra = 8
    small = jnp.pad(small, (0, extra * quarter - small.shape[0])).reshape(extra, quarter)
    packed = jnp.concatenate([query_weight, key_weight, value_weight, output_weight], axis=1)
    mine = lax.dynamic_slice(packed, (0, rep * quarter), (own, quarter))
    mine = jnp.concatenate([mine, small], axis=0)
    mine = grid.gather(mine, "z")
    mine = grid.gather(mine, "y")
    mine = grid.gather(mine, "x")
    mine = grid.gather(mine, "c")
    full = mine[..., :own, :].transpose(3, 2, 4, 1, 0, 5).reshape(width, total_w)
    qkv_weight = full[:, :wide]
    output_full = full[:, wide:]
    vectors = mine[0, 0, :, :, own:, :].transpose(1, 0, 2, 3).reshape(shards, extra * quarter)
    piece = lambda first, count: vectors[:, first : first + count].reshape(shards * count)
    query_bias_f, attn_gain_f, mlp_gain_f = (piece(i * own, own) for i in range(3))
    key_bias_f = piece(3 * own, own_kv)
    value_bias_f = piece(3 * own + own_kv, own_kv)
    qkv_bias = jnp.concatenate([query_bias_f, key_bias_f, value_bias_f]).astype(f32)

    part = down_weight.shape[0] // reps
    sets = size["l"] * size["y"]
    hidden = size["h"] * part

    def column_sets(weight):
        split = weight.reshape(own, size["h"], sets, reps, part)
        split = lax.dynamic_index_in_dim(split, rep, 3, keepdims=False)
        return split.transpose(2, 0, 1, 3).reshape(sets, own, hidden)

    both_sets = jnp.concatenate([column_sets(gate_weight), column_sets(up_weight)], axis=2)
    down_part = lax.dynamic_slice(down_weight, (rep * part, 0), (part, width))
    both_mine = jnp.zeros((size["h"], size["l"], size["y"], own, 2 * hidden), bf16)
    for kl in range(size["l"]):
        for ky in range(size["y"]):
            block = lax.dynamic_index_in_dim(
                both_sets, grid.peer("l", kl) * size["y"] + grid.peer("y", ky), 0, keepdims=False
            )
            for kh in range(size["h"]):
                got = block if kl + ky + kh == 0 else grid.send(block, h=kh, l=kl, y=ky)
                both_mine = lax.dynamic_update_slice(
                    both_mine,
                    got[None, None, None],
                    (grid.peer("h", -kh), grid.peer("l", -kl), grid.peer("y", -ky), 0, 0),
                )
    both_mine = both_mine.reshape(width, 2 * hidden)
    down_mine = grid.gather(down_part, "h").reshape(hidden, width)

    def gather_tokens(value):
        for d in "lyxc":
            value = grid.gather(value, d)
        return value.reshape(-1, width)

    def scatter_tokens(value):
        value = value.reshape(size["c"], size["x"], size["y"], size["l"], rows, -1)
        for d in "cxyl":
            value = grid.scatter(value, d)
        return value

    cot_all = gather_tokens(cotangent)

    segment, places, cosine, sine = jax.vmap(lambda lens: tables(lens, rows))(lengths)
    flat = tokens.astype(f32)
    scale_one, normed_one = norm_fwd(flat, attn_gain_f)
    normed_one = normed_one.astype(bf16)
    qkv = jnp.dot(normed_one, qkv_weight, preferred_element_type=f32) + qkv_bias
    query = rotate(qkv[:, :width].reshape(1, rows, HEADS, HD), cosine, sine).astype(bf16)
    query = query.reshape(1, rows, KVH, HEADS // KVH, HD)
    keys = rotate(qkv[:, width : width + kvd].reshape(1, rows, KVH, HD), cosine, sine).astype(bf16)
    values = qkv[:, width + kvd :].reshape(1, rows, KVH, HD).astype(bf16)
    mixed, lse = jax.vmap(attend)(query, keys, values, segment, places)
    mixed_flat = mixed.reshape(rows, width)
    hidden_one = flat + jnp.dot(mixed_flat, output_full, preferred_element_type=f32)
    scale_two, normed_two = norm_fwd(hidden_one, mlp_gain_f)
    normed_all = gather_tokens(normed_two.astype(bf16))

    dprod = times_transposed(cot_all, down_mine)
    both = jnp.dot(normed_all, both_mine, preferred_element_type=f32)
    gate, upper = both[:, :hidden], both[:, hidden:]
    sigma = jax.nn.sigmoid(gate)
    product = (gate * sigma * upper).astype(bf16)
    dgate = (dprod * upper * sigma * (1.0 + gate * (1.0 - sigma))).astype(bf16)
    dup = (dprod * gate * sigma).astype(bf16)
    dboth = jnp.concatenate([dgate, dup], axis=1)
    dnormed_part = times_transposed(dboth, both_mine).astype(bf16)
    out_part = jnp.dot(product, down_mine, preferred_element_type=f32).astype(bf16)
    dnormed_two = scatter_tokens(dnormed_part).astype(f32)
    out_sum = scatter_tokens(out_part).astype(f32)
    grad_both = jnp.dot(normed_all.T, dboth, preferred_element_type=f32).astype(bf16)
    grad_down = jnp.dot(product.T, cot_all, preferred_element_type=f32).astype(bf16)

    grad_both = grid.scatter(grad_both.reshape(size["h"], sets, own, 2 * hidden), "h")
    grad_down = grid.scatter(grad_down.reshape(size["h"], part, width), "h")
    owned = jnp.zeros((size["l"], size["y"], own, 2 * hidden), bf16)
    for kl in range(size["l"]):
        for ky in range(size["y"]):
            block = lax.dynamic_index_in_dim(
                grad_both, grid.peer("l", kl) * size["y"] + grid.peer("y", ky), 0, keepdims=False
            )
            got = block if kl + ky == 0 else grid.send(block, l=kl, y=ky)
            owned = lax.dynamic_update_slice(
                owned, got[None, None], (grid.peer("l", -kl), grid.peer("y", -ky), 0, 0)
            )

    def from_replicas(value):
        return grid.gather(grid.gather(value, "c"), "x").reshape((reps,) + value.shape)

    both_all = from_replicas(owned.reshape(sets, own, 2 * hidden))
    down_all = from_replicas(grad_down).reshape(reps * part, width).astype(f32)

    def joined(first):
        half = both_all[..., first : first + hidden].reshape(reps, sets, own, size["h"], part)
        return half.transpose(2, 3, 1, 0, 4).reshape(own, -1).astype(f32)

    result = (hidden_one + out_sum).astype(bf16)

    dh_two, grad_mlp_gain = norm_bwd(dnormed_two, hidden_one, scale_two, mlp_gain_f)
    dhidden = cotangent.astype(f32) + dh_two
    dres = dhidden.astype(bf16)
    grad_output = jnp.dot(mixed_flat.T, dres, preferred_element_type=f32).astype(bf16)
    dmixed = times_transposed(dres, output_full).astype(bf16)
    dmixed = dmixed.reshape(1, rows, KVH, HEADS // KVH, HD)
    dquery, dkeys, dvals = jax.vmap(attend_back)(
        query, keys, values, mixed, dmixed, lse, segment, places
    )
    dquery = unrotate(dquery.reshape(1, rows, HEADS, HD), cosine, sine).reshape(rows, width)
    dkeys = unrotate(dkeys, cosine, sine).reshape(rows, kvd)
    dvals = dvals.reshape(rows, kvd)
    dqkv = jnp.concatenate([dquery, dkeys, dvals], axis=1)
    grad_bias = jnp.sum(dqkv, axis=0)
    dqkv_b = dqkv.astype(bf16)
    grad_qkv = jnp.dot(normed_one.T, dqkv_b, preferred_element_type=f32).astype(bf16)
    dnormed_one = times_transposed(dqkv_b, qkv_weight)
    dh_one, grad_attn_gain = norm_bwd(dnormed_one, flat, scale_one, attn_gain_f)
    grad_input = dhidden + dh_one

    cut = lambda v, count: v.reshape(shards, count)
    small_g = jnp.concatenate(
        [
            cut(grad_bias[:width], own),
            cut(grad_attn_gain, own),
            cut(grad_mlp_gain, own),
            cut(grad_bias[width : width + kvd], own_kv),
            cut(grad_bias[width + kvd :], own_kv),
        ],
        axis=1,
    )
    small_n = small_g.shape[1]
    small_g = jnp.pad(small_g, ((0, 0), (0, extra * quarter - small_n)))
    small_g = jnp.broadcast_to(
        small_g.reshape(shards, 1, extra, quarter).astype(bf16), (shards, reps, extra, quarter)
    )
    grads = jnp.concatenate([grad_qkv, grad_output], axis=1)
    grads = grads.reshape(shards, own, reps, quarter).transpose(0, 2, 1, 3)
    grads = jnp.concatenate([grads, small_g], axis=2)
    grads = grads.reshape(size["z"], size["y"], size["x"], size["c"], own + extra, quarter)
    grads = grid.scatter(grads.transpose(3, 2, 1, 0, 4, 5), "c")
    grads = grid.scatter(grads, "x")
    grads = grid.scatter(grads, "y")
    grads = grid.scatter(grads, "z")
    vec = grads[own:].reshape(extra * quarter)[:small_n].astype(f32)
    attn_all = from_replicas(grads[:own]).transpose(1, 0, 2).reshape(own, total_w).astype(f32)

    return (
        result,
        grad_input,
        attn_all[:, :width],
        attn_all[:, width : width + kvd],
        attn_all[:, width + kvd : wide],
        attn_all[:, wide:],
        vec[:own],
        vec[3 * own : 3 * own + own_kv],
        vec[3 * own + own_kv :],
        vec[own : 2 * own],
        joined(0),
        joined(hidden),
        down_all,
        vec[2 * own : 3 * own],
    )


MESH = pl.DeviceIdType.MESH
TN = (((1,), (1,)), ((), ()))
NN = (((1,), (0,)), ((), ()))
CN = (((0,), (0,)), ((), ()))


def mm(left, right, dims=NN):
    return lax.dot_general(left, right, dims, preferred_element_type=jnp.float32)


class Place:
    def __init__(self, size):
        self.size = size
        rep, shard = lax.axis_index("rep"), lax.axis_index("shard")
        z = shard // size["y"]
        self.at = dict(
            x=rep // size["c"],
            c=rep % size["c"],
            z=z,
            y=shard % size["y"],
            h=z // size["l"],
            l=z % size["l"],
        )

    def peer(self, d, k):
        return (self.at[d] + k + self.size[d]) % self.size[d]

    def device(self, **by):
        at = dict(self.at)
        for d, k in by.items():
            at[d] = self.peer(d, k)
        if "h" in by or "l" in by:
            at["z"] = at["h"] * self.size["l"] + at["l"]
        return (at["x"] * self.size["c"] + at["c"], at["z"] * self.size["y"] + at["y"])

    def greet(self, everyone):
        barrier = pltpu.get_barrier_semaphore()
        for by in everyone:
            pl.semaphore_signal(barrier, inc=1, device_id=self.device(**by), device_id_type=MESH)
        pl.semaphore_wait(barrier, len(everyone))


class Traffic:
    def __init__(self, place, send, recv):
        self.place, self.send, self.recv, self.used, self.sent = place, send, recv, 0, []

    def start(self, src, dst, arriving, **by):
        i = self.used
        self.used += 1
        copy = pltpu.make_async_remote_copy(
            src_ref=src,
            dst_ref=dst,
            send_sem=self.send.at[i],
            recv_sem=self.recv.at[i],
            device_id=self.place.device(**by),
            device_id_type=MESH,
        )
        copy.start()
        self.sent.append(copy)
        return pltpu.make_async_remote_copy(
            src_ref=arriving,
            dst_ref=arriving,
            send_sem=self.send.at[i],
            recv_sem=self.recv.at[i],
            device_id=self.place.device(**by),
            device_id_type=MESH,
        ).wait_recv

    def finish(self):
        for copy in self.sent:
            copy.wait_send()


def around(size):
    others = [
        dict(h=h, l=l, y=y)
        for h in range(size["h"])
        for l in range(size["l"])
        for y in range(size["y"])
        if h + l + y
    ]
    return others + [dict(x=k) for k in range(1, size["x"])] + [dict(c=k) for k in range(1, size["c"])]


def row_parts(rows):
    step = -(-rows // 48) * 16
    return [(0, step), (step, step), (2 * step, rows - 2 * step)]


def token_gather(place, traffic, buf, rows, dims):
    names = "xcyl"
    at = place.at

    def region(held, **fixed):
        index = []
        for d in names:
            if d in fixed:
                index.append(fixed[d])
            elif d in held:
                index.append(pl.ds(0, place.size[d]))
            else:
                index.append(at[d])
        return buf.at[tuple(index) + (pl.ds(*rows),)]

    def cores(held, **fixed):
        here = region(held, **fixed)
        return [
            traffic.start(here, here, region(held, **{**fixed, "c": place.peer("c", -k)}), c=k)
            for k in range(1, place.size["c"])
        ]

    last = cores("")
    held = ""
    for d in dims:
        here = region(held)
        got = [
            (k, traffic.start(here, here, region(held, **{d: place.peer(d, -k)}), **{d: k}))
            for k in range(1, place.size[d])
        ]
        yield
        for k, wait in got:
            wait()
            last += cores(held, **{d: place.peer(d, -k)})
        held += d
    yield
    for wait in last:
        wait()


def lanes_of(count, width):
    return lax.broadcasted_iota(jnp.int32, (count, width), 1)


def turn(value):
    count, width = value.shape
    half = HD // 2
    first = lanes_of(count, width) % HD < half
    return jnp.where(first, pltpu.roll(value, width - half, 1), pltpu.roll(value, half, 1))


def position_tables(lengths_ref, freq, rows):
    i0 = lax.broadcasted_iota(jnp.int32, (rows, rows), 0)
    i1 = lax.broadcasted_iota(jnp.int32, (rows, rows), 1)
    first0, first1 = jnp.zeros_like(i0), jnp.zeros_like(i1)
    end = jnp.int32(0)
    for j in range(lengths_ref.shape[1]):
        count = lengths_ref[0, j]
        end = end + count
        first0 = first0 + jnp.where(i0 >= end, count, 0)
        first1 = first1 + jnp.where(i1 >= end, count, 0)
    allowed = (first0 == first1) & (i1 <= i0)
    angle = (i0 - first0).astype(jnp.float32) * freq
    sign = jnp.where(lanes_of(rows, rows) % HD < HD // 2, -1.0, 1.0)
    return allowed, jnp.cos(angle), jnp.sin(angle) * sign


def columns(first, count, quarter):
    out = []
    while count:
        share, inside = first // quarter, first % quarter
        step = min(count, quarter - inside)
        out.append((share, inside, step))
        first, count = first + step, count - step
    return out


def pair_of(keys, pair):
    group = HEADS // KVH
    low, high = 2 * pair // group, (2 * pair + 1) // group
    if (low, high) == (0, 1):
        return keys
    other = pltpu.roll(keys.astype(jnp.float32), HD, 1).astype(keys.dtype)
    lo = lanes_of(*keys.shape) < HD
    return jnp.where(lo, keys, other) if low == 0 else jnp.where(lo, other, keys)


def halves(value):
    lo = lanes_of(*value.shape) < HD
    zero = jnp.zeros_like(value)
    return jnp.where(lo, value, zero), jnp.where(lo, zero, value)


def front_kernel(
    size,
    lengths_ref,
    tokens_ref,
    cot_ref,
    mine_ref,
    small_ref,
    freq_ref,
    sets_ref,
    down_ref,
    att_ref,
    small_all_ref,
    both_ref,
    down_all_ref,
    cot_all_ref,
    norm_all_ref,
    vec_ref,
    normed_ref,
    query_ref,
    keys_ref,
    values_ref,
    mixed_ref,
    probs_ref,
    hidden_ref,
    send,
    recv,
):
    f32, bf16 = jnp.float32, jnp.bfloat16
    place = Place(size)
    at, peer = place.at, place.peer
    traffic = Traffic(place, send, recv)
    rows, width = tokens_ref.shape
    own, quarter = mine_ref.shape
    kvd = keys_ref.shape[1]
    small_all_ref[at["z"], at["y"]] = small_ref[...]
    att_ref[at["x"], at["c"], at["z"], at["y"]] = mine_ref[...]
    cot_all_ref[at["x"], at["c"], at["y"], at["l"]] = cot_ref[...]
    q_own = at["l"] * size["y"] + at["y"]
    both_ref[at["h"], at["l"], at["y"]] = sets_ref[q_own]
    down_all_ref[at["h"]] = down_ref[...]
    place.greet(around(size))

    def block(z, y, x=None, c=None):
        return att_ref.at[at["x"] if x is None else x, at["c"] if c is None else c, z, y]

    def to_core(z, y, x):
        return [
            traffic.start(block(z, y, x), block(z, y, x), block(z, y, x, peer("c", -k)), c=k)
            for k in range(1, size["c"])
        ]

    def to_x(z, y):
        return [
            (traffic.start(block(z, y), block(z, y), block(z, y, peer("x", -k)), x=k), z, y, peer("x", -k))
            for k in range(1, size["x"])
        ]

    def to_y(z):
        return [
            (traffic.start(block(z, at["y"]), block(z, at["y"]), block(z, peer("y", -k)), y=k), z, peer("y", -k))
            for k in range(1, size["y"])
        ]

    z, y = at["z"], at["y"]
    mine = block(z, y)
    from_z = [
        (traffic.start(mine, mine, block(peer("z", -k), y), z=k), peer("z", -k))
        for k in range(1, size["z"])
    ]
    from_y, from_x = to_y(z), to_x(z, y)
    waits = to_core(z, y, at["x"])
    small_waits = []
    for by in around(size):
        if "h" in by:
            here = small_all_ref.at[z, y]
            there = small_all_ref.at[peer("h", -by["h"]) * size["l"] + peer("l", -by["l"]), peer("y", -by["y"])]
            small_waits.append(traffic.start(here, here, there, **by))
    cot_steps = token_gather(place, traffic, cot_all_ref, (0, rows), "lxy")
    next(cot_steps)

    flat = tokens_ref[...].astype(f32)
    scale = lax.rsqrt(jnp.mean(flat * flat, axis=1, keepdims=True) + eps_norm)
    allowed, cosine, sine = position_tables(lengths_ref, freq_ref[0:1, :], rows)

    for wait, zz in from_z:
        wait()
        from_y += to_y(zz)
        from_x += to_x(zz, y)
        waits += to_core(zz, y, at["x"])

    ff_waits = []
    for by in around(size):
        if "h" in by:
            q = peer("l", by["l"]) * size["y"] + peer("y", by["y"])
            ff_waits.append(
                traffic.start(
                    sets_ref.at[q],
                    both_ref.at[at["h"], at["l"], at["y"]],
                    both_ref.at[peer("h", -by["h"]), peer("l", -by["l"]), peer("y", -by["y"])],
                    **by,
                )
            )
    for k in range(1, size["h"]):
        ff_waits.append(
            traffic.start(down_ref, down_all_ref.at[at["h"]], down_all_ref.at[peer("h", -k)], h=k)
        )

    for wait, zz, yy in from_y:
        wait()
        from_x += to_x(zz, yy)
        waits += to_core(zz, yy, at["x"])
    next(cot_steps)
    for wait, zz, yy, xx in from_x:
        wait()
        waits += to_core(zz, yy, xx)
    next(cot_steps)
    for wait in small_waits + waits:
        wait()

    own_kv = kvd // (size["z"] * size["y"])
    vec = jnp.zeros((8, width), f32)
    kv = jnp.zeros((8, kvd), f32)
    for s in range(size["z"] * size["y"]):
        piece = small_all_ref[s // size["y"], s % size["y"]]
        piece_w = jnp.where(lanes_of(8, piece.shape[1]) < own, piece, 0.0)
        wider = jnp.concatenate([piece_w, jnp.zeros((8, width - piece.shape[1]), f32)], axis=1)
        vec = vec + (pltpu.roll(wider, s * own, 1) if s else wider)
        piece_kv = jnp.where(lanes_of(8, kvd) < own_kv, piece[:, :kvd], 0.0)
        kv = kv + (pltpu.roll(piece_kv, s * own_kv, 1) if s else piece_kv)
    vec_ref[...] = vec

    def weight(share, first, count):
        x, c = share // size["c"], share % size["c"]
        return att_ref[x, c, :, :, :, first : first + count].reshape(width, count)

    def project(left, first, count):
        return jnp.concatenate(
            [mm(left, weight(*piece)) for piece in columns(first, count, quarter)], axis=1
        )

    normed = (flat * scale * vec[1:2, :]).astype(bf16)
    normed_ref[...] = normed
    times = width // rows
    wide_cos = jnp.concatenate([cosine] * times, axis=1)
    wide_sin = jnp.concatenate([sine] * times, axis=1)
    query = project(normed, 0, width) + vec[0:1, :]
    query = (query * wide_cos + turn(query) * wide_sin).astype(bf16)
    query_ref[...] = query
    keys = project(normed, width, kvd) + kv[3:4, :]
    keys = (keys * cosine + turn(keys) * sine).astype(bf16)
    keys_ref[...] = keys
    values = (project(normed, width + kvd, kvd) + kv[4:5, :]).astype(bf16)
    values_ref[...] = values

    for pair in range(HEADS // 2):
        lanes = pl.ds(pair * 2 * HD, 2 * HD)
        kp, vp = pair_of(keys, pair), pair_of(values, pair)
        total = None
        for i, (qh, vh) in enumerate(zip(halves(query_ref[:, lanes]), halves(vp))):
            raw = jnp.where(allowed, mm(qh, kp, TN) * (1.0 / math.sqrt(HD)), masked_score)
            top = jnp.max(raw, axis=1, keepdims=True)
            lse = top + jnp.log(jnp.sum(jnp.exp(raw - top), axis=1, keepdims=True))
            probs = jnp.exp(raw - lse)
            probs_ref[2 * pair + i] = probs
            part = mm(probs.astype(bf16), vh)
            total = part if total is None else total + part
        mixed_ref[:, lanes] = total.astype(bf16)

    hidden = flat + project(mixed_ref[...], width + 2 * kvd, width)
    hidden_ref[...] = hidden
    scale_two = lax.rsqrt(jnp.mean(hidden * hidden, axis=1, keepdims=True) + eps_norm)
    norm_all_ref[at["x"], at["c"], at["y"], at["l"]] = (hidden * scale_two * vec[2:3, :]).astype(bf16)
    steps = [
        token_gather(place, traffic, norm_all_ref, part, dims)
        for part, dims in zip(row_parts(rows), ("lxy", "xyl", "ylx"))
    ]
    for _ in range(4):
        for step in steps:
            next(step, None)
    for step in [cot_steps, *steps]:
        for _ in step:
            pass
    for wait in ff_waits:
        wait()
    traffic.finish()


def front(size, lengths, tokens, cot, mine, small, freq, sets, down):
    f32, bf16 = jnp.float32, jnp.bfloat16
    rows, width = tokens.shape
    own, quarter = mine.shape
    kvd = 2 * HD
    n = size
    group = (n["x"], n["c"], n["y"], n["l"])
    shapes = [
        ((n["x"], n["c"], n["z"], n["y"], own, quarter), bf16),
        ((n["z"], n["y"]) + small.shape, f32),
        ((n["h"], n["l"], n["y"]) + sets.shape[1:], bf16),
        ((n["h"],) + down.shape, bf16),
        (group + (rows, width), bf16),
        (group + (rows, width), bf16),
        ((8, width), f32),
        ((rows, width), bf16),
        ((rows, width), bf16),
        ((rows, kvd), bf16),
        ((rows, kvd), bf16),
        ((rows, width), bf16),
        ((HEADS, rows, rows), f32),
        ((rows, width), f32),
    ]
    vmem = pl.BlockSpec(memory_space=pltpu.VMEM)
    return pl.pallas_call(
        functools.partial(front_kernel, size),
        out_shape=[jax.ShapeDtypeStruct(*s) for s in shapes],
        in_specs=[pl.BlockSpec(memory_space=pltpu.SMEM)] + [vmem] * 7,
        out_specs=[vmem] * len(shapes),
        scratch_shapes=[pltpu.SemaphoreType.DMA((96,)), pltpu.SemaphoreType.DMA((96,))],
        compiler_params=pltpu.CompilerParams(
            collective_id=1, has_side_effects=True, vmem_limit_bytes=56 << 20
        ),
    )(lengths, tokens, cot, mine, small, freq, sets, down)


def reduce_over(place, traffic, inbox, acc, names, rows, dims, source=None):
    at, size, peer = place.at, place.size, place.peer

    def region(buf, done, fixed, over):
        index = []
        for d in over:
            index.append(fixed[d] if d in fixed else at[d] if d in done else pl.ds(0, size[d]))
        return buf.at[tuple(index) + (pl.ds(*rows),)]

    def blocks(done):
        found = [()]
        for d in names:
            found = [f + (v,) for f in found for v in ([at[d]] if d in done else range(size[d]))]
        return found

    cut = pl.ds(*rows)
    if source is not None:
        first, core_in = source
        with_c = names[0] + "c" + names[1:]
        wait = traffic.start(
            region(first, "", {"c": peer("c", 1)}, with_c), region(core_in, "", {}, names), region(core_in, "", {}, names), c=1
        )
        yield
        wait()
        for b in blocks(""):
            total = first[(b[0], at["c"]) + b[1:] + (cut,)].astype(jnp.float32)
            acc[b + (cut,)] = (total + core_in[b + (cut,)].astype(jnp.float32)).astype(acc.dtype)
    done = ""
    for d in dims:
        waits = [
            traffic.start(
                region(acc, done, {d: peer(d, k)}, names),
                region(inbox, done, {d: at[d]}, names),
                region(inbox, done, {d: peer(d, -k)}, names),
                **{d: k},
            )
            for k in range(1, size[d])
        ]
        yield
        for wait in waits:
            wait()
        at_d = names.index(d)
        for b in blocks(done + d):
            total = acc[b + (cut,)].astype(jnp.float32)
            for k in range(1, size[d]):
                other = b[:at_d] + (peer(d, -k),) + b[at_d + 1 :]
                total = total + inbox[other + (cut,)].astype(jnp.float32)
            acc[b + (cut,)] = total.astype(acc.dtype)
        done += d


def replica_gather(place, traffic, buf, index=()):
    at, peer, size = place.at, place.peer, place.size

    def block(x, c):
        return buf.at[(x, c) + index]

    def to_core(x):
        return [
            traffic.start(block(x, at["c"]), block(x, at["c"]), block(x, peer("c", -k)), c=k)
            for k in range(1, size["c"])
        ]

    mine = block(at["x"], at["c"])
    got = [
        (k, traffic.start(mine, mine, block(peer("x", -k), at["c"]), x=k)) for k in range(1, size["x"])
    ]
    last = to_core(at["x"])
    yield
    for k, wait in got:
        wait()
        last += to_core(peer("x", -k))
    yield
    for wait in last:
        wait()


def norm_back(dnormed, hidden, gain):
    scale = lax.rsqrt(jnp.mean(hidden * hidden, axis=1, keepdims=True) + eps_norm)
    dgain = jnp.sum(dnormed * hidden * scale, axis=0, keepdims=True)
    inner = dnormed * gain
    dhidden = scale * inner - hidden * (scale * scale * scale) * jnp.mean(
        inner * hidden, axis=1, keepdims=True
    )
    return dhidden, dgain


def back_kernel(
    size,
    lengths_ref,
    tokens_ref,
    cot_ref,
    freq_ref,
    dn_ref,
    out_ref,
    gboth_ref,
    gdown_ref,
    att_ref,
    vec_ref,
    normed_ref,
    query_ref,
    keys_ref,
    values_ref,
    mixed_ref,
    probs_ref,
    hidden_ref,
    result_ref,
    gtok_ref,
    both_all_ref,
    down_all_ref,
    attn_all_ref,
    small_ref,
    dn_core,
    dn_in,
    dn_acc,
    out_core,
    out_in,
    out_acc,
    both_in,
    down_in,
    both_sum,
    grads,
    g_core,
    g_in,
    g_acc,
    dq_ref,
    dmixed_ref,
    small_out,
    small_in,
    small_x,
    small_c,
    send,
    recv,
):
    f32, bf16 = jnp.float32, jnp.bfloat16
    place = Place(size)
    at, peer = place.at, place.peer
    traffic = Traffic(place, send, recv)
    rows, width = tokens_ref.shape
    own, quarter = att_ref.shape[-2:]
    kvd = keys_ref.shape[1]
    own_kv = kvd // (size["z"] * size["y"])
    place.greet(around(size))

    half = rows // 2
    dn_steps = [
        reduce_over(place, traffic, dn_in, dn_acc, "xyl", part, dims, (dn_ref, dn_core))
        for part, dims in zip(((0, half), (half, half)), ("xyl", "yxl"))
    ]
    out_steps = [
        reduce_over(place, traffic, out_in, out_acc, "xyl", part, dims, (out_ref, out_core))
        for part, dims in zip(((0, half), (half, half)), ("xyl", "yxl"))
    ]

    def advance(steps):
        for step in steps:
            next(step, None)

    advance(dn_steps)
    order = [(l, y) for l in reversed(range(size["l"])) for y in reversed(range(size["y"]))]
    pieces = []
    for kl, ky in order:
        q = peer("l", kl) * size["y"] + peer("y", ky)
        waits = [
            traffic.start(gboth_ref.at[peer("h", k), q], both_in.at[k - 1, q], both_in.at[k - 1, q], h=k)
            for k in range(1, size["h"])
        ]
        pieces.append((kl, ky, q, waits))
    down_waits = [
        traffic.start(gdown_ref.at[peer("h", k)], down_in.at[k - 1], down_in.at[k - 1], h=k)
        for k in range(1, size["h"])
    ]

    ff_gathers = []

    def finish_piece(kl, ky, q, waits):
        for wait in waits:
            wait()
        total = gboth_ref[at["h"], q].astype(f32)
        for k in range(1, size["h"]):
            total = total + both_in[k - 1, q].astype(f32)
        if kl + ky:
            both_sum[q] = total.astype(bf16)
            here = (at["x"], at["c"], at["l"], at["y"])
            there = (at["x"], at["c"], peer("l", -kl), peer("y", -ky))
            arrived = traffic.start(
                both_sum.at[q], both_all_ref.at[here], both_all_ref.at[there], l=kl, y=ky
            )
        else:
            both_all_ref[at["x"], at["c"], at["l"], at["y"]] = total.astype(bf16)
            arrived = None

        def spread():
            if arrived is not None:
                arrived()
            gather = replica_gather(
                place, traffic, both_all_ref, (peer("l", -kl), peer("y", -ky))
            )
            next(gather)
            ff_gathers.append(gather)

        return spread

    advance(dn_steps)
    advance(out_steps)
    advance(dn_steps)
    spreads = [finish_piece(*pieces[0])]
    advance(dn_steps)
    advance(dn_steps)

    mine = (at["x"], at["y"], at["l"])
    dnormed_two = dn_acc[mine].astype(f32)
    vec = vec_ref[...]
    hidden = hidden_ref[...]
    dh_two, g_mlp = norm_back(dnormed_two, hidden, vec[2:3, :])
    dhidden = cot_ref[...].astype(f32) + dh_two
    gtok_ref[...] = dhidden
    dres = dhidden.astype(bf16)

    advance(out_steps)
    rest = iter(pieces[1:])

    def weight(share, first, count):
        x, c = share // size["c"], share % size["c"]
        return att_ref[x, c, :, :, :, first : first + count].reshape(width, count)

    def project_back(left, first, count):
        total, used = None, 0
        for share, inside, step in columns(first, count, quarter):
            part = mm(left[:, used : used + step], weight(share, inside, step), TN)
            total = part if total is None else total + part
            used += step
        return total

    def put_grads(left, right, first):
        used = 0
        for share, inside, step in columns(first, right.shape[1], quarter):
            part = mm(left, right[:, used : used + step], CN).astype(bf16)
            x, c = share // size["c"], share % size["c"]
            grads[x, c, :, :, :, inside : inside + step] = part.reshape(size["z"], size["y"], own, step)
            used += step

    dmixed_ref[...] = project_back(dres, width + 2 * kvd, width).astype(bf16)
    put_grads(mixed_ref[...], dres, width + 2 * kvd)

    allowed, cosine, sine = position_tables(lengths_ref, freq_ref[0:1, :], rows)
    keys, values = keys_ref[...], values_ref[...]
    group = HEADS // KVH
    dk_sum, dv_sum = {}, {}
    for pair in range(HEADS // 2):
        lanes = pl.ds(pair * 2 * HD, 2 * HD)
        kp, vp = pair_of(keys, pair), pair_of(values, pair)
        dm = dmixed_ref[:, lanes]
        weighted = halves(dm.astype(f32) * mixed_ref[:, lanes].astype(f32))
        dq = dk = dv = jnp.zeros((rows, 2 * HD), f32)
        for i, (qh, kh, dmh) in enumerate(zip(halves(query_ref[:, lanes]), halves(kp), halves(dm))):
            probs = probs_ref[2 * pair + i]
            dprobs = mm(dmh, vp, TN)
            delta = jnp.sum(weighted[i], axis=1, keepdims=True)
            dscores = (probs * (dprobs - delta) * (1.0 / math.sqrt(HD))).astype(bf16)
            dq = dq + mm(dscores, kh)
            dk = dk + mm(dscores, qh, CN)
            dv = dv + mm(probs.astype(bf16), dmh, CN)
        dq_ref[:, lanes] = dq
        which = (2 * pair // group, (2 * pair + 1) // group)
        dk_sum[which] = dk_sum[which] + dk if which in dk_sum else dk
        dv_sum[which] = dv_sum[which] + dv if which in dv_sum else dv
        if pair == 2:
            advance(out_steps)
            piece = next(rest, None)
            if piece is not None:
                spreads.append(finish_piece(*piece))
    advance(out_steps)

    def join_groups(sums):
        fold = lambda v: v + pltpu.roll(v, HD, 1)
        lo = lanes_of(rows, 2 * HD) < HD
        return jnp.where(lo, fold(sums[0, 0]), fold(sums[1, 1])) + sums[0, 1]

    times = width // rows
    wide_cos = jnp.concatenate([cosine] * times, axis=1)
    wide_sin = jnp.concatenate([sine] * times, axis=1)
    dq = dq_ref[...]
    dq = dq * wide_cos - turn(dq) * wide_sin
    dk = join_groups(dk_sum)
    dk = dk * cosine - turn(dk) * sine
    dv = join_groups(dv_sum)
    normed = normed_ref[...]
    dq_b, dk_b, dv_b = dq.astype(bf16), dk.astype(bf16), dv.astype(bf16)
    put_grads(normed, dq_b, 0)
    put_grads(normed, dk_b, width)
    put_grads(normed, dv_b, width + kvd)
    g_steps = [
        reduce_over(place, traffic, g_in, g_acc, "xzy", part, dims, (grads, g_core))
        for part, dims in zip(row_parts(own), ("xyz", "yzx", "zxy"))
    ]
    advance(g_steps)

    dnormed = project_back(dq_b, 0, width) + project_back(dk_b, width, kvd)
    dnormed = dnormed + project_back(dv_b, width + kvd, kvd)
    dh_one, g_attn = norm_back(dnormed, tokens_ref[...].astype(f32), vec[1:2, :])
    gtok_ref[...] = gtok_ref[...] + dh_one

    total = lambda v: jnp.sum(v, axis=0, keepdims=True)
    tall = jnp.concatenate([total(dq), g_attn, g_mlp, jnp.zeros((5, width), f32)], axis=0)
    flat_kv = jnp.concatenate([jnp.zeros((3, kvd), f32), total(dk), total(dv), jnp.zeros((3, kvd), f32)], axis=0)
    lane = lanes_of(8, kvd)
    for s in range(size["z"] * size["y"]):
        a = pltpu.roll(tall, width - s * own, 1) if s else tall
        b = pltpu.roll(flat_kv, kvd - s * own_kv, 1) if s else flat_kv
        a = jnp.where(lane < own, a[:, :kvd], 0.0)
        small_out[s // size["y"], s % size["y"]] = a + jnp.where(lane < own_kv, b, 0.0)
    small_waits = []
    for i, by in enumerate(b for b in around(size) if "h" in b):
        there = (peer("h", by["h"]) * size["l"] + peer("l", by["l"]), peer("y", by["y"]))
        small_waits.append(traffic.start(small_out.at[there], small_in.at[i], small_in.at[i], **by))

    advance(g_steps)
    for piece in rest:
        spreads.append(finish_piece(*piece))
    for wait in down_waits:
        wait()
    down = gdown_ref[at["h"]].astype(f32)
    for k in range(1, size["h"]):
        down = down + down_in[k - 1].astype(f32)
    down_all_ref[at["x"], at["c"]] = down.astype(bf16)
    for spread in spreads:
        spread()
    down_gather = replica_gather(place, traffic, down_all_ref)
    next(down_gather)
    ff_gathers.append(down_gather)

    for wait in small_waits:
        wait()
    small = small_out[at["z"], at["y"]]
    for i in range(len(small_waits)):
        small = small + small_in[i]
    small_ref[...] = small
    advance(g_steps)
    small_waits = [
        traffic.start(small_ref, small_x.at[k - 1], small_x.at[k - 1], x=k) for k in range(1, size["x"])
    ]
    for wait in small_waits:
        wait()
    for k in range(1, size["x"]):
        small = small + small_x[k - 1]
    small_out[at["z"], at["y"]] = small
    advance(out_steps)
    result_ref[...] = (hidden + out_acc[mine].astype(f32)).astype(bf16)
    small_waits = [
        traffic.start(small_out.at[at["z"], at["y"]], small_c.at[k - 1], small_c.at[k - 1], c=k)
        for k in range(1, size["c"])
    ]
    advance(g_steps)
    advance(g_steps)
    attn_all_ref[at["x"], at["c"]] = g_acc[at["x"], at["z"], at["y"]]
    attn_gather = replica_gather(place, traffic, attn_all_ref)
    next(attn_gather)
    ff_gathers.append(attn_gather)
    for wait in small_waits:
        wait()
    for step in [*ff_gathers, *ff_gathers]:
        next(step, None)
    traffic.finish()
    for k in range(1, size["c"]):
        small = small + small_c[k - 1]
    small_ref[...] = small


def back(size, lengths, tokens, cot, freq, *more):
    f32, bf16 = jnp.float32, jnp.bfloat16
    rows, width = tokens.shape
    gboth, gdown, att = more[2], more[3], more[4]
    own, quarter = att.shape[-2:]
    n = size
    kvd = 2 * HD
    reps = (n["x"], n["c"])
    sets = (n["l"], n["y"])
    shapes = [
        ((rows, width), bf16),
        ((rows, width), f32),
        (reps + sets + gboth.shape[2:], bf16),
        (reps + gdown.shape[1:], bf16),
        (reps + (own, quarter), bf16),
        ((8, kvd), f32),
    ]
    group = (n["x"], n["y"], n["l"], rows, width)
    owners = (n["x"], n["z"], n["y"], own, quarter)
    others = n["z"] * n["y"] - 1
    scratch = (
        [pltpu.VMEM(group, bf16)] * 6
        + [
            pltpu.VMEM((max(1, n["h"] - 1),) + gboth.shape[1:], bf16),
            pltpu.VMEM((max(1, n["h"] - 1),) + gdown.shape[1:], bf16),
            pltpu.VMEM(gboth.shape[1:], bf16),
            pltpu.VMEM(att.shape, bf16),
        ]
        + [pltpu.VMEM(owners, bf16)] * 3
        + [
            pltpu.VMEM((rows, width), f32),
            pltpu.VMEM((rows, width), bf16),
            pltpu.VMEM((n["z"], n["y"], 8, kvd), f32),
            pltpu.VMEM((max(1, others), 8, kvd), f32),
            pltpu.VMEM((max(1, n["x"] - 1), 8, kvd), f32),
            pltpu.VMEM((max(1, n["c"] - 1), 8, kvd), f32),
            pltpu.SemaphoreType.DMA((96,)),
            pltpu.SemaphoreType.DMA((96,)),
        ]
    )
    vmem = pl.BlockSpec(memory_space=pltpu.VMEM)
    return pl.pallas_call(
        functools.partial(back_kernel, size),
        out_shape=[jax.ShapeDtypeStruct(*s) for s in shapes],
        in_specs=[pl.BlockSpec(memory_space=pltpu.SMEM)] + [vmem] * (3 + len(more)),
        out_specs=[vmem] * len(shapes),
        scratch_shapes=scratch,
        compiler_params=pltpu.CompilerParams(
            collective_id=2, has_side_effects=True, vmem_limit_bytes=60 << 20
        ),
    )(lengths, tokens, cot, freq, *more)


def by_kernels(
    tokens,
    cotangent,
    lengths,
    query_weight,
    key_weight,
    value_weight,
    output_weight,
    query_bias,
    key_bias,
    value_bias,
    attn_gain,
    gate_weight,
    up_weight,
    down_weight,
    mlp_gain,
):
    grid = Grid()
    size, at = grid.size, grid.at
    shards, reps = grid.shards, grid.reps
    rep = lax.axis_index("rep")
    rows, width = tokens.shape
    own = query_weight.shape[0]
    kvd = key_weight.shape[1]
    own_kv = key_bias.shape[0]
    f32, bf16 = jnp.float32, jnp.bfloat16
    wide = width + 2 * kvd
    total_w = wide + width
    quarter = total_w // reps

    part = down_weight.shape[0] // reps
    sets = size["l"] * size["y"]
    hidden = size["h"] * part

    packed = jnp.concatenate([query_weight, key_weight, value_weight, output_weight], axis=1)
    mine = lax.dynamic_slice(packed, (0, rep * quarter), (own, quarter))
    lane = lambda v: jnp.pad(v.astype(f32), (0, 128 - v.shape[0]))
    small = jnp.stack([lane(v) for v in (query_bias, attn_gain, mlp_gain, key_bias, value_bias)])
    small = jnp.pad(small, ((0, 8 - small.shape[0]), (0, 0)))

    def column_sets(weight):
        split = weight.reshape(own, size["h"], sets, reps, part)
        split = lax.dynamic_index_in_dim(split, rep, 3, keepdims=False)
        return split.transpose(2, 0, 1, 3).reshape(sets, own, hidden)

    both_sets = jnp.concatenate([column_sets(gate_weight), column_sets(up_weight)], axis=2)
    down_part = lax.dynamic_slice(down_weight, (rep * part, 0), (part, width))
    freq = theta_base ** (-((jnp.arange(rows) % (HD // 2)).astype(f32) * (2.0 / HD)))
    freq = jnp.broadcast_to(freq[None, :], (8, rows))
    att, _, both_mine, down_mine, cot_all, normed_all, *saved = front(
        size, lengths, tokens, cotangent, mine, small, freq, both_sets, down_part
    )
    group = normed_all.shape[:-1]
    both_mine = both_mine.reshape(width, 2 * hidden)
    down_mine = down_mine.reshape(hidden, width)
    cot_all = cot_all.reshape(-1, width)
    normed_all = normed_all.reshape(-1, width)

    dprod = times_transposed(cot_all, down_mine)
    both = jnp.dot(normed_all, both_mine, preferred_element_type=f32)
    gate, upper = both[:, :hidden], both[:, hidden:]
    sigma = jax.nn.sigmoid(gate)
    product = (gate * sigma * upper).astype(bf16)
    dgate = (dprod * upper * sigma * (1.0 + gate * (1.0 - sigma))).astype(bf16)
    dup = (dprod * gate * sigma).astype(bf16)
    dboth = jnp.concatenate([dgate, dup], axis=1)
    dnormed_part = times_transposed(dboth, both_mine).astype(bf16)
    out_part = jnp.dot(product, down_mine, preferred_element_type=f32).astype(bf16)
    grad_both = jnp.dot(normed_all.T, dboth, preferred_element_type=f32).astype(bf16)
    grad_down = jnp.dot(product.T, cot_all, preferred_element_type=f32).astype(bf16)

    result, grad_input, both_all, down_all, attn_all, vec = back(
        size,
        lengths,
        tokens,
        cotangent,
        freq,
        dnormed_part.reshape(group + (width,)),
        out_part.reshape(group + (width,)),
        grad_both.reshape(size["h"], sets, own, 2 * hidden),
        grad_down.reshape(size["h"], part, width),
        att,
        *saved,
    )
    both_all = both_all.reshape(reps, sets, own, 2 * hidden)
    down_all = down_all.reshape(reps * part, width).astype(f32)
    attn_all = attn_all.reshape(reps, own, quarter).transpose(1, 0, 2).reshape(own, total_w).astype(f32)

    def joined(first):
        half = both_all[..., first : first + hidden].reshape(reps, sets, own, size["h"], part)
        return half.transpose(2, 3, 1, 0, 4).reshape(own, -1).astype(f32)

    return (
        result,
        grad_input,
        attn_all[:, :width],
        attn_all[:, width : width + kvd],
        attn_all[:, width + kvd : wide],
        attn_all[:, wide:],
        vec[0, :own],
        vec[3, :own_kv],
        vec[4, :own_kv],
        vec[1, :own],
        joined(0),
        joined(hidden),
        down_all,
        vec[2, :own],
    )


def on_device(*args):
    tokens, query_weight, key_weight = args[0], args[3], args[4]
    rows, width = tokens.shape
    total_w = 2 * width + 2 * key_weight.shape[1]
    fits = (
        rows == 2 * HD
        and lax.axis_size("rep") % 2 == 0
        and HEADS // KVH % 2
        and key_weight.shape[1] == 2 * HD
        and query_weight.shape[0] % 16 == 0
        and query_weight.shape[0] <= 128
        and (total_w // lax.axis_size("rep")) % 128 == 0
    )
    return by_kernels(*args) if fits else by_permutes(*args)


def solution(mesh):
    in_specs = (
        P(("rep", "shard"), None),
        P(("rep", "shard"), None),
        P(("rep", "shard"), None),
        P("shard", None),
        P("shard", None),
        P("shard", None),
        P("shard", None),
        P("shard"),
        P("shard"),
        P("shard"),
        P("shard"),
        P("shard", None),
        P("shard", None),
        P("shard", None),
        P("shard"),
    )
    out_specs = (
        P(("rep", "shard"), None),
        P(("rep", "shard"), None),
        P("shard", None),
        P("shard", None),
        P("shard", None),
        P("shard", None),
        P("shard"),
        P("shard"),
        P("shard"),
        P("shard"),
        P("shard", None),
        P("shard", None),
        P("shard", None),
        P("shard"),
    )
    return jax.shard_map(
        on_device, mesh=mesh, in_specs=in_specs, out_specs=out_specs, check_vma=False
    )
```

```python
import functools
import math

import jax
import jax.numpy as jnp
import numpy as np
from jax import lax
from jax.experimental import pallas as pl
from jax.experimental.pallas import tpu as pltpu
from jax.sharding import PartitionSpec as P

HEADS = 14
KVH = 2
HD = 64


theta_base = 1000000.0
eps_norm = 1e-06
masked_score = -1000000000.0


def times_transposed(left, weight):
    return lax.dot_general(
        left, weight, (((1,), (1,)), ((), ())), preferred_element_type=jnp.float32
    )


def tables(lengths_row, rows):
    order = jnp.arange(lengths_row.shape[0])
    ends = jnp.sum(jnp.where(order[None, :] <= order[:, None], lengths_row[None, :], 0), axis=1)
    starts = ends - lengths_row
    places = jnp.arange(rows, dtype=jnp.int32)
    inside = ((places[:, None] >= starts[None, :]) & (places[:, None] < ends[None, :])).astype(
        jnp.int32
    )
    slots = jnp.arange(lengths_row.shape[0], dtype=jnp.int32)
    segment = jnp.sum(inside * slots[None, :], axis=1)
    first = jnp.sum(inside * starts[None, :], axis=1)
    offset = (places - first).astype(jnp.float32)
    half = HD // 2
    freq = theta_base ** (-(jnp.arange(half, dtype=jnp.float32) * (2.0 / HD)))
    angles = offset[:, None] * freq[None, :]
    return (segment, places, jnp.cos(angles), jnp.sin(angles))


def rotate(values, cosine, sine):
    half = values.shape[-1] // 2
    first, second = (values[..., :half], values[..., half:])
    cosine = cosine[:, :, None, :]
    sine = sine[:, :, None, :]
    return jnp.concatenate(
        [first * cosine - second * sine, second * cosine + first * sine], axis=-1
    )


def unrotate(grads, cosine, sine):
    half = grads.shape[-1] // 2
    first, second = (grads[..., :half], grads[..., half:])
    cosine = cosine[:, :, None, :]
    sine = sine[:, :, None, :]
    return jnp.concatenate(
        [first * cosine + second * sine, second * cosine - first * sine], axis=-1
    )


def norm_fwd(hidden, gain):
    scale = lax.rsqrt(jnp.mean(hidden * hidden, axis=-1, keepdims=True) + eps_norm)
    return (scale, hidden * scale * gain.astype(jnp.float32))


def norm_bwd(dnormed, hidden, scale, gain):
    gain_f = gain.astype(jnp.float32)
    dgain = jnp.sum(dnormed * hidden * scale, axis=0)
    inner = dnormed * gain_f
    dhidden = scale * inner - hidden * (scale * scale * scale) * jnp.mean(
        inner * hidden, axis=-1, keepdims=True
    )
    return (dhidden, dgain)


def scores_of(query, keys, segment, places):
    raw = jnp.einsum("igha,jga->ghij", query, keys, preferred_element_type=jnp.float32) * (
        1.0 / math.sqrt(HD)
    )
    allowed = (segment[:, None] == segment[None, :]) & (places[None, :] <= places[:, None])
    return jnp.where(allowed[None, None], raw, masked_score)


def attend(query, keys, values, segment, places):
    raw = scores_of(query, keys, segment, places)
    top = jnp.max(raw, axis=-1, keepdims=True)
    total = jnp.sum(jnp.exp(raw - top), axis=-1)
    lse = top[..., 0] + jnp.log(total)
    probs = jnp.exp(raw - lse[..., None]).astype(jnp.bfloat16)
    mixed = jnp.einsum("ghij,jga->igha", probs, values, preferred_element_type=jnp.float32).astype(
        jnp.bfloat16
    )
    return (mixed, lse)


def attend_back(query, keys, values, mixed, dmixed, lse, segment, places):
    raw = scores_of(query, keys, segment, places)
    probs_f = jnp.exp(raw - lse[..., None])
    probs = probs_f.astype(jnp.bfloat16)
    dvals = jnp.einsum("ghij,igha->jga", probs, dmixed, preferred_element_type=jnp.float32)
    dprobs = jnp.einsum("igha,jga->ghij", dmixed, values, preferred_element_type=jnp.float32)
    delta = jnp.einsum("igha,igha->ghi", dmixed, mixed, preferred_element_type=jnp.float32)
    dscores = (probs_f * (dprobs - delta[..., None]) * (1.0 / math.sqrt(HD))).astype(jnp.bfloat16)
    dquery = jnp.einsum("ghij,jga->igha", dscores, keys, preferred_element_type=jnp.float32)
    dkeys = jnp.einsum("ghij,igha->jga", dscores, query, preferred_element_type=jnp.float32)
    return (dquery, dkeys, dvals)


class Grid:
    def __init__(self):
        self.reps = lax.axis_size("rep")
        self.shards = lax.axis_size("shard")
        c = 2 if self.reps % 2 == 0 else 1
        x = self.reps // c
        y = x if self.shards % x == 0 else 1
        z = self.shards // y
        l = 2 if z % 2 == 0 else 1
        self.size = dict(x=x, c=c, h=z // l, l=l, y=y, z=z)
        rep, shard = lax.axis_index("rep"), lax.axis_index("shard")
        zz = shard // y
        self.at = dict(x=rep // c, c=rep % c, z=zz, y=shard % y, h=zz // l, l=zz % l)

    def send(self, value, **by):
        n = self.size
        pairs = []
        for rep in range(self.reps):
            for shard in range(self.shards):
                at = dict(x=rep // n["c"], c=rep % n["c"], z=shard // n["y"], y=shard % n["y"])
                if "h" in by or "l" in by:
                    h = (at["z"] // n["l"] + by.get("h", 0)) % n["h"]
                    at["z"] = h * n["l"] + (at["z"] + by.get("l", 0)) % n["l"]
                for d in "xczy":
                    at[d] = (at[d] + by.get(d, 0)) % n[d]
                pairs.append(
                    (
                        rep * self.shards + shard,
                        (at["x"] * n["c"] + at["c"]) * self.shards + at["z"] * n["y"] + at["y"],
                    )
                )
        return lax.ppermute(value, ("rep", "shard"), pairs)

    def peer(self, d, k):
        return (self.at[d] + k + self.size[d]) % self.size[d]

    def gather(self, value, d):
        out = jnp.zeros((self.size[d],) + value.shape, value.dtype)
        out = lax.dynamic_update_index_in_dim(out, value, self.at[d], 0)
        for k in range(1, self.size[d]):
            out = lax.dynamic_update_index_in_dim(
                out, self.send(value, **{d: k}), self.peer(d, -k), 0
            )
        return out

    def scatter(self, value, d):
        pick = lambda k: lax.dynamic_index_in_dim(value, self.peer(d, k), 0, keepdims=False)
        total = pick(0).astype(jnp.float32)
        for k in range(1, self.size[d]):
            total = total + self.send(pick(k), **{d: k}).astype(jnp.float32)
        return total.astype(value.dtype)


def by_permutes(
    tokens,
    cotangent,
    lengths,
    query_weight,
    key_weight,
    value_weight,
    output_weight,
    query_bias,
    key_bias,
    value_bias,
    attn_gain,
    gate_weight,
    up_weight,
    down_weight,
    mlp_gain,
):
    grid = Grid()
    size, at = grid.size, grid.at
    shards, reps = grid.shards, grid.reps
    rep = lax.axis_index("rep")
    rows, width = tokens.shape
    own = query_weight.shape[0]
    kvd = key_weight.shape[1]
    own_kv = key_bias.shape[0]
    f32, bf16 = jnp.float32, jnp.bfloat16
    wide = width + 2 * kvd
    total_w = wide + width
    quarter = total_w // reps

    small = jnp.concatenate([query_bias, attn_gain, mlp_gain, key_bias, value_bias])
    extra = 8
    small = jnp.pad(small, (0, extra * quarter - small.shape[0])).reshape(extra, quarter)
    packed = jnp.concatenate([query_weight, key_weight, value_weight, output_weight], axis=1)
    mine = lax.dynamic_slice(packed, (0, rep * quarter), (own, quarter))
    mine = jnp.concatenate([mine, small], axis=0)
    mine = grid.gather(mine, "z")
    mine = grid.gather(mine, "y")
    mine = grid.gather(mine, "x")
    mine = grid.gather(mine, "c")
    full = mine[..., :own, :].transpose(3, 2, 4, 1, 0, 5).reshape(width, total_w)
    qkv_weight = full[:, :wide]
    output_full = full[:, wide:]
    vectors = mine[0, 0, :, :, own:, :].transpose(1, 0, 2, 3).reshape(shards, extra * quarter)
    piece = lambda first, count: vectors[:, first : first + count].reshape(shards * count)
    query_bias_f, attn_gain_f, mlp_gain_f = (piece(i * own, own) for i in range(3))
    key_bias_f = piece(3 * own, own_kv)
    value_bias_f = piece(3 * own + own_kv, own_kv)
    qkv_bias = jnp.concatenate([query_bias_f, key_bias_f, value_bias_f]).astype(f32)

    part = down_weight.shape[0] // reps
    sets = size["l"] * size["y"]
    hidden = size["h"] * part

    def column_sets(weight):
        split = weight.reshape(own, size["h"], sets, reps, part)
        split = lax.dynamic_index_in_dim(split, rep, 3, keepdims=False)
        return split.transpose(2, 0, 1, 3).reshape(sets, own, hidden)

    both_sets = jnp.concatenate([column_sets(gate_weight), column_sets(up_weight)], axis=2)
    down_part = lax.dynamic_slice(down_weight, (rep * part, 0), (part, width))
    both_mine = jnp.zeros((size["h"], size["l"], size["y"], own, 2 * hidden), bf16)
    for kl in range(size["l"]):
        for ky in range(size["y"]):
            block = lax.dynamic_index_in_dim(
                both_sets, grid.peer("l", kl) * size["y"] + grid.peer("y", ky), 0, keepdims=False
            )
            for kh in range(size["h"]):
                got = block if kl + ky + kh == 0 else grid.send(block, h=kh, l=kl, y=ky)
                both_mine = lax.dynamic_update_slice(
                    both_mine,
                    got[None, None, None],
                    (grid.peer("h", -kh), grid.peer("l", -kl), grid.peer("y", -ky), 0, 0),
                )
    both_mine = both_mine.reshape(width, 2 * hidden)
    down_mine = grid.gather(down_part, "h").reshape(hidden, width)

    def gather_tokens(value):
        for d in "lyxc":
            value = grid.gather(value, d)
        return value.reshape(-1, width)

    def scatter_tokens(value):
        value = value.reshape(size["c"], size["x"], size["y"], size["l"], rows, -1)
        for d in "cxyl":
            value = grid.scatter(value, d)
        return value

    cot_all = gather_tokens(cotangent)

    segment, places, cosine, sine = jax.vmap(lambda lens: tables(lens, rows))(lengths)
    flat = tokens.astype(f32)
    scale_one, normed_one = norm_fwd(flat, attn_gain_f)
    normed_one = normed_one.astype(bf16)
    qkv = jnp.dot(normed_one, qkv_weight, preferred_element_type=f32) + qkv_bias
    query = rotate(qkv[:, :width].reshape(1, rows, HEADS, HD), cosine, sine).astype(bf16)
    query = query.reshape(1, rows, KVH, HEADS // KVH, HD)
    keys = rotate(qkv[:, width : width + kvd].reshape(1, rows, KVH, HD), cosine, sine).astype(bf16)
    values = qkv[:, width + kvd :].reshape(1, rows, KVH, HD).astype(bf16)
    mixed, lse = jax.vmap(attend)(query, keys, values, segment, places)
    mixed_flat = mixed.reshape(rows, width)
    hidden_one = flat + jnp.dot(mixed_flat, output_full, preferred_element_type=f32)
    scale_two, normed_two = norm_fwd(hidden_one, mlp_gain_f)
    normed_all = gather_tokens(normed_two.astype(bf16))

    dprod = times_transposed(cot_all, down_mine)
    both = jnp.dot(normed_all, both_mine, preferred_element_type=f32)
    gate, upper = both[:, :hidden], both[:, hidden:]
    sigma = jax.nn.sigmoid(gate)
    product = (gate * sigma * upper).astype(bf16)
    dgate = (dprod * upper * sigma * (1.0 + gate * (1.0 - sigma))).astype(bf16)
    dup = (dprod * gate * sigma).astype(bf16)
    dboth = jnp.concatenate([dgate, dup], axis=1)
    dnormed_part = times_transposed(dboth, both_mine).astype(bf16)
    out_part = jnp.dot(product, down_mine, preferred_element_type=f32).astype(bf16)
    dnormed_two = scatter_tokens(dnormed_part).astype(f32)
    out_sum = scatter_tokens(out_part).astype(f32)
    grad_both = jnp.dot(normed_all.T, dboth, preferred_element_type=f32).astype(bf16)
    grad_down = jnp.dot(product.T, cot_all, preferred_element_type=f32).astype(bf16)

    grad_both = grid.scatter(grad_both.reshape(size["h"], sets, own, 2 * hidden), "h")
    grad_down = grid.scatter(grad_down.reshape(size["h"], part, width), "h")
    owned = jnp.zeros((size["l"], size["y"], own, 2 * hidden), bf16)
    for kl in range(size["l"]):
        for ky in range(size["y"]):
            block = lax.dynamic_index_in_dim(
                grad_both, grid.peer("l", kl) * size["y"] + grid.peer("y", ky), 0, keepdims=False
            )
            got = block if kl + ky == 0 else grid.send(block, l=kl, y=ky)
            owned = lax.dynamic_update_slice(
                owned, got[None, None], (grid.peer("l", -kl), grid.peer("y", -ky), 0, 0)
            )

    def from_replicas(value):
        return grid.gather(grid.gather(value, "c"), "x").reshape((reps,) + value.shape)

    both_all = from_replicas(owned.reshape(sets, own, 2 * hidden))
    down_all = from_replicas(grad_down).reshape(reps * part, width).astype(f32)

    def joined(first):
        half = both_all[..., first : first + hidden].reshape(reps, sets, own, size["h"], part)
        return half.transpose(2, 3, 1, 0, 4).reshape(own, -1).astype(f32)

    result = (hidden_one + out_sum).astype(bf16)

    dh_two, grad_mlp_gain = norm_bwd(dnormed_two, hidden_one, scale_two, mlp_gain_f)
    dhidden = cotangent.astype(f32) + dh_two
    dres = dhidden.astype(bf16)
    grad_output = jnp.dot(mixed_flat.T, dres, preferred_element_type=f32).astype(bf16)
    dmixed = times_transposed(dres, output_full).astype(bf16)
    dmixed = dmixed.reshape(1, rows, KVH, HEADS // KVH, HD)
    dquery, dkeys, dvals = jax.vmap(attend_back)(
        query, keys, values, mixed, dmixed, lse, segment, places
    )
    dquery = unrotate(dquery.reshape(1, rows, HEADS, HD), cosine, sine).reshape(rows, width)
    dkeys = unrotate(dkeys, cosine, sine).reshape(rows, kvd)
    dvals = dvals.reshape(rows, kvd)
    dqkv = jnp.concatenate([dquery, dkeys, dvals], axis=1)
    grad_bias = jnp.sum(dqkv, axis=0)
    dqkv_b = dqkv.astype(bf16)
    grad_qkv = jnp.dot(normed_one.T, dqkv_b, preferred_element_type=f32).astype(bf16)
    dnormed_one = times_transposed(dqkv_b, qkv_weight)
    dh_one, grad_attn_gain = norm_bwd(dnormed_one, flat, scale_one, attn_gain_f)
    grad_input = dhidden + dh_one

    cut = lambda v, count: v.reshape(shards, count)
    small_g = jnp.concatenate(
        [
            cut(grad_bias[:width], own),
            cut(grad_attn_gain, own),
            cut(grad_mlp_gain, own),
            cut(grad_bias[width : width + kvd], own_kv),
            cut(grad_bias[width + kvd :], own_kv),
        ],
        axis=1,
    )
    small_n = small_g.shape[1]
    small_g = jnp.pad(small_g, ((0, 0), (0, extra * quarter - small_n)))
    small_g = jnp.broadcast_to(
        small_g.reshape(shards, 1, extra, quarter).astype(bf16), (shards, reps, extra, quarter)
    )
    grads = jnp.concatenate([grad_qkv, grad_output], axis=1)
    grads = grads.reshape(shards, own, reps, quarter).transpose(0, 2, 1, 3)
    grads = jnp.concatenate([grads, small_g], axis=2)
    grads = grads.reshape(size["z"], size["y"], size["x"], size["c"], own + extra, quarter)
    grads = grid.scatter(grads.transpose(3, 2, 1, 0, 4, 5), "c")
    grads = grid.scatter(grads, "x")
    grads = grid.scatter(grads, "y")
    grads = grid.scatter(grads, "z")
    vec = grads[own:].reshape(extra * quarter)[:small_n].astype(f32)
    attn_all = from_replicas(grads[:own]).transpose(1, 0, 2).reshape(own, total_w).astype(f32)

    return (
        result,
        grad_input,
        attn_all[:, :width],
        attn_all[:, width : width + kvd],
        attn_all[:, width + kvd : wide],
        attn_all[:, wide:],
        vec[:own],
        vec[3 * own : 3 * own + own_kv],
        vec[3 * own + own_kv :],
        vec[own : 2 * own],
        joined(0),
        joined(hidden),
        down_all,
        vec[2 * own : 3 * own],
    )


MESH = pl.DeviceIdType.MESH
TN = (((1,), (1,)), ((), ()))
NN = (((1,), (0,)), ((), ()))
CN = (((0,), (0,)), ((), ()))


def mm(left, right, dims=NN):
    return lax.dot_general(left, right, dims, preferred_element_type=jnp.float32)


class Place:
    def __init__(self, size):
        self.size = size
        rep, shard = lax.axis_index("rep"), lax.axis_index("shard")
        z = shard // size["y"]
        self.at = dict(
            x=rep // size["c"],
            c=rep % size["c"],
            z=z,
            y=shard % size["y"],
            h=z // size["l"],
            l=z % size["l"],
        )

    def peer(self, d, k):
        n, at = self.size[d], self.at[d]
        if n & (n - 1):
            return (at + k + n) % n
        k, bit = abs(k), 1
        while bit < n:
            if k & bit:
                at = at + bit * (1 - 2 * ((at // bit) % 2))
            bit *= 2
        return at

    def device(self, **by):
        at = dict(self.at)
        for d, k in by.items():
            at[d] = self.peer(d, k)
        if "h" in by or "l" in by:
            at["z"] = at["h"] * self.size["l"] + at["l"]
        return (at["x"] * self.size["c"] + at["c"], at["z"] * self.size["y"] + at["y"])

    def greet(self, everyone):
        barrier = pltpu.get_barrier_semaphore()
        for by in everyone:
            pl.semaphore_signal(barrier, inc=1, device_id=self.device(**by), device_id_type=MESH)
        pl.semaphore_wait(barrier, len(everyone))


class Traffic:
    def __init__(self, place, send, recv):
        self.place, self.send, self.recv, self.used, self.sent = place, send, recv, 0, []

    def start(self, src, dst, arriving, **by):
        i = self.used
        self.used += 1
        copy = pltpu.make_async_remote_copy(
            src_ref=src,
            dst_ref=dst,
            send_sem=self.send.at[i],
            recv_sem=self.recv.at[i],
            device_id=self.place.device(**by),
            device_id_type=MESH,
        )
        copy.start()
        self.sent.append(copy)
        return pltpu.make_async_remote_copy(
            src_ref=arriving,
            dst_ref=arriving,
            send_sem=self.send.at[i],
            recv_sem=self.recv.at[i],
            device_id=self.place.device(**by),
            device_id_type=MESH,
        ).wait_recv

    def finish(self):
        for copy in self.sent:
            copy.wait_send()


def around(size):
    others = [
        dict(h=h, l=l, y=y)
        for h in range(size["h"])
        for l in range(size["l"])
        for y in range(size["y"])
        if h + l + y
    ]
    return others + [dict(x=k) for k in range(1, size["x"])] + [dict(c=k) for k in range(1, size["c"])]


def row_parts(rows):
    step = -(-rows // 48) * 16
    return [(0, step), (step, step), (2 * step, rows - 2 * step)]


def token_gather(place, traffic, buf, rows, dims):
    names = "xcyl"
    at = place.at

    def region(held, **fixed):
        index = []
        for d in names:
            if d in fixed:
                index.append(fixed[d])
            elif d in held:
                index.append(pl.ds(0, place.size[d]))
            else:
                index.append(at[d])
        return buf.at[tuple(index) + (pl.ds(*rows),)]

    def cores(held, **fixed):
        here = region(held, **fixed)
        return [
            traffic.start(here, here, region(held, **{**fixed, "c": place.peer("c", -k)}), c=k)
            for k in range(1, place.size["c"])
        ]

    last = cores("")
    held = ""
    for d in dims:
        here = region(held)
        got = [
            (k, traffic.start(here, here, region(held, **{d: place.peer(d, -k)}), **{d: k}))
            for k in range(1, place.size[d])
        ]
        yield
        for k, wait in got:
            wait()
            last += cores(held, **{d: place.peer(d, -k)})
        held += d
    yield
    for wait in last:
        wait()


def lanes_of(count, width):
    return lax.broadcasted_iota(jnp.int32, (count, width), 1)


def turn(value):
    count, width = value.shape
    half = HD // 2
    first = lanes_of(count, width) % HD < half
    return jnp.where(first, pltpu.roll(value, width - half, 1), pltpu.roll(value, half, 1))


def position_tables(lengths_ref, freq, rows):
    i0 = lax.broadcasted_iota(jnp.int32, (rows, rows), 0)
    i1 = lax.broadcasted_iota(jnp.int32, (rows, rows), 1)
    first0, first1 = jnp.zeros_like(i0), jnp.zeros_like(i1)
    end = jnp.int32(0)
    for j in range(lengths_ref.shape[1]):
        count = lengths_ref[0, j]
        end = end + count
        first0 = first0 + jnp.where(i0 >= end, count, 0)
        first1 = first1 + jnp.where(i1 >= end, count, 0)
    allowed = (first0 == first1) & (i1 <= i0)
    angle = (i0 - first0).astype(jnp.float32) * freq
    sign = jnp.where(lanes_of(rows, rows) % HD < HD // 2, -1.0, 1.0)
    return allowed, jnp.cos(angle), jnp.sin(angle) * sign


def columns(first, count, quarter):
    out = []
    while count:
        share, inside = first // quarter, first % quarter
        step = min(count, quarter - inside)
        out.append((share, inside, step))
        first, count = first + step, count - step
    return out


def pair_of(keys, pair):
    group = HEADS // KVH
    low, high = 2 * pair // group, (2 * pair + 1) // group
    if (low, high) == (0, 1):
        return keys
    other = pltpu.roll(keys.astype(jnp.float32), HD, 1).astype(keys.dtype)
    lo = lanes_of(*keys.shape) < HD
    return jnp.where(lo, keys, other) if low == 0 else jnp.where(lo, other, keys)


def halves(value):
    lo = lanes_of(*value.shape) < HD
    zero = jnp.zeros_like(value)
    return jnp.where(lo, value, zero), jnp.where(lo, zero, value)


def front_kernel(
    size,
    lengths_ref,
    tokens_ref,
    cot_ref,
    freq_ref,
    query_w_ref,
    key_w_ref,
    value_w_ref,
    output_w_ref,
    query_b_ref,
    attn_gain_ref,
    mlp_gain_ref,
    key_b_ref,
    value_b_ref,
    gate_w_ref,
    up_w_ref,
    down_ref,
    att_ref,
    small_all_ref,
    both_ref,
    down_all_ref,
    cot_all_ref,
    norm_all_ref,
    vec_ref,
    normed_ref,
    query_ref,
    keys_ref,
    values_ref,
    mixed_ref,
    probs_ref,
    hidden_ref,
    sets_ref,
    send,
    recv,
):
    f32, bf16 = jnp.float32, jnp.bfloat16
    place = Place(size)
    at, peer = place.at, place.peer
    traffic = Traffic(place, send, recv)
    rows, width = tokens_ref.shape
    own, quarter = att_ref.shape[-2:]
    kvd = keys_ref.shape[1]
    reps = size["x"] * size["c"]
    rep = at["x"] * size["c"] + at["c"]
    part = down_ref.shape[0]
    groups, sets = size["h"], size["l"] * size["y"]
    hid = groups * part
    small_all_ref[at["z"], at["y"]] = jnp.zeros(small_all_ref.shape[2:], f32)
    vectors = (query_b_ref, attn_gain_ref, mlp_gain_ref, key_b_ref, value_b_ref)
    for i, ref in enumerate(vectors):
        small_all_ref[at["z"], at["y"], i : i + 1, : ref.shape[1]] = ref[...].astype(f32)
    for r in range(reps):

        @pl.when(rep == r)
        def _():
            to, start = 0, 0
            for ref in (query_w_ref, key_w_ref, value_w_ref, output_w_ref):
                first = max(r * quarter, start)
                last = min((r + 1) * quarter, start + ref.shape[1])
                if first < last:
                    count = last - first
                    att_ref[at["x"], at["c"], at["z"], at["y"], :, to : to + count] = ref[
                        :, first - start : last - start
                    ]
                    to += count
                start += ref.shape[1]

    cot_all_ref[at["x"], at["c"], at["y"], at["l"]] = cot_ref[...]
    q_own = at["l"] * size["y"] + at["y"]
    down_all_ref[at["h"]] = down_ref[...]
    place.greet(around(size))

    def block(z, y, x=None, c=None):
        return att_ref.at[at["x"] if x is None else x, at["c"] if c is None else c, z, y]

    def to_core(z, y, x):
        return [
            traffic.start(block(z, y, x), block(z, y, x), block(z, y, x, peer("c", -k)), c=k)
            for k in range(1, size["c"])
        ]

    def to_x(z, y):
        return [
            (traffic.start(block(z, y), block(z, y), block(z, y, peer("x", -k)), x=k), z, y, peer("x", -k))
            for k in range(1, size["x"])
        ]

    def to_y(z):
        return [
            (traffic.start(block(z, at["y"]), block(z, at["y"]), block(z, peer("y", -k)), y=k), z, peer("y", -k))
            for k in range(1, size["y"])
        ]

    z, y = at["z"], at["y"]
    mine = block(z, y)
    from_z = [
        (traffic.start(mine, mine, block(peer("z", -k), y), z=k), peer("z", -k))
        for k in range(1, size["z"])
    ]
    from_y, from_x = to_y(z), to_x(z, y)
    waits = to_core(z, y, at["x"])
    small_waits = []
    for by in around(size):
        if "h" in by:
            here = small_all_ref.at[z, y]
            there = small_all_ref.at[peer("h", -by["h"]) * size["l"] + peer("l", -by["l"]), peer("y", -by["y"])]
            small_waits.append(traffic.start(here, here, there, **by))
    cot_steps = [
        token_gather(place, traffic, cot_all_ref, part, dims)
        for part, dims in zip(((0, rows // 2), (rows // 2, rows // 2)), ("lxy", "lyx"))
    ]
    for step in cot_steps:
        next(step)

    flat = tokens_ref[...].astype(f32)
    scale = lax.rsqrt(jnp.mean(flat * flat, axis=1, keepdims=True) + eps_norm)
    allowed, cosine, sine = position_tables(lengths_ref, freq_ref[0:1, :], rows)
    for r in range(reps):

        @pl.when(rep == r)
        def _():
            for q in range(sets):
                for half, ref in enumerate((gate_w_ref, up_w_ref)):
                    for h in range(groups):
                        first = ((h * sets + q) * reps + r) * part
                        to = half * hid + h * part
                        sets_ref[q, :, to : to + part] = ref[:, first : first + part]

    both_ref[at["h"], at["l"], at["y"]] = sets_ref[q_own]

    for wait, zz in from_z:
        wait()
        from_y += to_y(zz)
        from_x += to_x(zz, y)
        waits += to_core(zz, y, at["x"])

    ff_waits = []
    for by in around(size):
        if "h" in by:
            q = peer("l", by["l"]) * size["y"] + peer("y", by["y"])
            ff_waits.append(
                traffic.start(
                    sets_ref.at[q],
                    both_ref.at[at["h"], at["l"], at["y"]],
                    both_ref.at[peer("h", -by["h"]), peer("l", -by["l"]), peer("y", -by["y"])],
                    **by,
                )
            )
    for k in range(1, size["h"]):
        ff_waits.append(
            traffic.start(down_ref, down_all_ref.at[at["h"]], down_all_ref.at[peer("h", -k)], h=k)
        )

    for wait, zz, yy in from_y:
        wait()
        from_x += to_x(zz, yy)
        waits += to_core(zz, yy, at["x"])
    for step in cot_steps:
        next(step)
    for wait, zz, yy, xx in from_x:
        wait()
        waits += to_core(zz, yy, xx)
    for step in cot_steps:
        next(step)
    for wait in small_waits + waits:
        wait()

    own_kv = kvd // (size["z"] * size["y"])
    vec = jnp.zeros((8, width), f32)
    kv = jnp.zeros((8, kvd), f32)
    for s in range(size["z"] * size["y"]):
        piece = small_all_ref[s // size["y"], s % size["y"]]
        piece_w = jnp.where(lanes_of(8, piece.shape[1]) < own, piece, 0.0)
        wider = jnp.concatenate([piece_w, jnp.zeros((8, width - piece.shape[1]), f32)], axis=1)
        vec = vec + (pltpu.roll(wider, s * own, 1) if s else wider)
        piece_kv = jnp.where(lanes_of(8, kvd) < own_kv, piece[:, :kvd], 0.0)
        kv = kv + (pltpu.roll(piece_kv, s * own_kv, 1) if s else piece_kv)
    vec_ref[...] = vec

    def weight(share, first, count):
        x, c = share // size["c"], share % size["c"]
        return att_ref[x, c, :, :, :, first : first + count].reshape(width, count)

    def project(left, first, count):
        return jnp.concatenate(
            [mm(left, weight(*piece)) for piece in columns(first, count, quarter)], axis=1
        )

    normed = (flat * scale * vec[1:2, :]).astype(bf16)
    normed_ref[...] = normed
    times = width // rows
    wide_cos = jnp.concatenate([cosine] * times, axis=1)
    wide_sin = jnp.concatenate([sine] * times, axis=1)
    query = project(normed, 0, width) + vec[0:1, :]
    query = (query * wide_cos + turn(query) * wide_sin).astype(bf16)
    query_ref[...] = query
    keys = project(normed, width, kvd) + kv[3:4, :]
    keys = (keys * cosine + turn(keys) * sine).astype(bf16)
    keys_ref[...] = keys
    values = (project(normed, width + kvd, kvd) + kv[4:5, :]).astype(bf16)
    values_ref[...] = values

    for pair in range(HEADS // 2):
        lanes = pl.ds(pair * 2 * HD, 2 * HD)
        kp, vp = pair_of(keys, pair), pair_of(values, pair)
        total = None
        for i, (qh, vh) in enumerate(zip(halves(query_ref[:, lanes]), halves(vp))):
            raw = jnp.where(allowed, mm(qh, kp, TN) * (1.0 / math.sqrt(HD)), masked_score)
            top = jnp.max(raw, axis=1, keepdims=True)
            lse = top + jnp.log(jnp.sum(jnp.exp(raw - top), axis=1, keepdims=True))
            probs = jnp.exp(raw - lse)
            probs_ref[2 * pair + i] = probs
            part = mm(probs.astype(bf16), vh)
            total = part if total is None else total + part
        mixed_ref[:, lanes] = total.astype(bf16)

    hidden = flat + project(mixed_ref[...], width + 2 * kvd, width)
    hidden_ref[...] = hidden
    scale_two = lax.rsqrt(jnp.mean(hidden * hidden, axis=1, keepdims=True) + eps_norm)
    norm_all_ref[at["x"], at["c"], at["y"], at["l"]] = (hidden * scale_two * vec[2:3, :]).astype(bf16)
    steps = [
        token_gather(place, traffic, norm_all_ref, part, dims)
        for part, dims in zip(row_parts(rows), ("lxy", "xyl", "ylx"))
    ]
    for _ in range(4):
        for step in steps:
            next(step, None)
    for step in [*cot_steps, *steps]:
        for _ in step:
            pass
    for wait in ff_waits:
        wait()
    traffic.finish()


def front(size, lengths, tokens, cot, freq, *params):
    f32, bf16 = jnp.float32, jnp.bfloat16
    rows, width = tokens.shape
    own = params[0].shape[0]
    down = params[-1]
    kvd = 2 * HD
    n = size
    quarter = 2 * (width + kvd) // (n["x"] * n["c"])
    sets = (n["l"] * n["y"], own, 2 * n["h"] * down.shape[0])
    group = (n["x"], n["c"], n["y"], n["l"])
    shapes = [
        ((n["x"], n["c"], n["z"], n["y"], own, quarter), bf16),
        ((n["z"], n["y"], 8, 128), f32),
        ((n["h"], n["l"], n["y"]) + sets[1:], bf16),
        ((n["h"],) + down.shape, bf16),
        (group + (rows, width), bf16),
        (group + (rows, width), bf16),
        ((8, width), f32),
        ((rows, width), bf16),
        ((rows, width), bf16),
        ((rows, kvd), bf16),
        ((rows, kvd), bf16),
        ((rows, width), bf16),
        ((HEADS, rows, rows), f32),
        ((rows, width), f32),
    ]
    vmem = pl.BlockSpec(memory_space=pltpu.VMEM)
    return pl.pallas_call(
        functools.partial(front_kernel, size),
        out_shape=[jax.ShapeDtypeStruct(*s) for s in shapes],
        in_specs=[pl.BlockSpec(memory_space=pltpu.SMEM)] + [vmem] * (3 + len(params)),
        out_specs=[vmem] * len(shapes),
        scratch_shapes=[
            pltpu.VMEM(sets, bf16),
            pltpu.SemaphoreType.DMA((96,)),
            pltpu.SemaphoreType.DMA((96,)),
        ],
        compiler_params=pltpu.CompilerParams(
            collective_id=1, has_side_effects=True, vmem_limit_bytes=56 << 20
        ),
    )(lengths, tokens, cot, freq, *params)


def reduce_over(place, traffic, inbox, acc, names, rows, dims, source=None):
    at, size, peer = place.at, place.size, place.peer

    def region(buf, done, fixed, over):
        index = []
        for d in over:
            index.append(fixed[d] if d in fixed else at[d] if d in done else pl.ds(0, size[d]))
        return buf.at[tuple(index) + (pl.ds(*rows),)]

    def blocks(done):
        found = [()]
        for d in names:
            found = [f + (v,) for f in found for v in ([at[d]] if d in done else range(size[d]))]
        return found

    cut = pl.ds(*rows)
    if source is not None:
        first, core_in = source
        with_c = names[0] + "c" + names[1:]
        wait = traffic.start(
            region(first, "", {"c": peer("c", 1)}, with_c), region(core_in, "", {}, names), region(core_in, "", {}, names), c=1
        )
        yield
        wait()
        for b in blocks(""):
            acc[b + (cut,)] = first[(b[0], at["c"]) + b[1:] + (cut,)] + core_in[b + (cut,)]
    done = ""
    for d in dims:
        waits = [
            traffic.start(
                region(acc, done, {d: peer(d, k)}, names),
                region(inbox, done, {d: at[d]}, names),
                region(inbox, done, {d: peer(d, -k)}, names),
                **{d: k},
            )
            for k in range(1, size[d])
        ]
        yield
        for wait in waits:
            wait()
        at_d = names.index(d)
        for b in blocks(done + d):
            if size[d] == 2:
                other = b[:at_d] + (peer(d, 1),) + b[at_d + 1 :]
                acc[b + (cut,)] = acc[b + (cut,)] + inbox[other + (cut,)]
                continue
            total = acc[b + (cut,)].astype(jnp.float32)
            for k in range(1, size[d]):
                other = b[:at_d] + (peer(d, -k),) + b[at_d + 1 :]
                total = total + inbox[other + (cut,)].astype(jnp.float32)
            acc[b + (cut,)] = total.astype(acc.dtype)
        done += d


def replica_gather(place, traffic, buf, index=()):
    at, peer, size = place.at, place.peer, place.size

    def block(x, c):
        return buf.at[(x, c) + index]

    def to_core(x):
        return [
            traffic.start(block(x, at["c"]), block(x, at["c"]), block(x, peer("c", -k)), c=k)
            for k in range(1, size["c"])
        ]

    mine = block(at["x"], at["c"])
    got = [
        (k, traffic.start(mine, mine, block(peer("x", -k), at["c"]), x=k)) for k in range(1, size["x"])
    ]
    last = to_core(at["x"])
    yield
    for k, wait in got:
        wait()
        last += to_core(peer("x", -k))
    yield
    for wait in last:
        wait()


def norm_back(dnormed, hidden, gain):
    scale = lax.rsqrt(jnp.mean(hidden * hidden, axis=1, keepdims=True) + eps_norm)
    dgain = jnp.sum(dnormed * hidden * scale, axis=0, keepdims=True)
    inner = dnormed * gain
    dhidden = scale * inner - hidden * (scale * scale * scale) * jnp.mean(
        inner * hidden, axis=1, keepdims=True
    )
    return dhidden, dgain


def back_kernel(
    size,
    lengths_ref,
    tokens_ref,
    cot_ref,
    freq_ref,
    dn_ref,
    out_ref,
    gboth_ref,
    gdown_ref,
    att_ref,
    vec_ref,
    normed_ref,
    query_ref,
    keys_ref,
    values_ref,
    mixed_ref,
    probs_ref,
    hidden_ref,
    result_ref,
    gtok_ref,
    both_all_ref,
    down_all_ref,
    small_ref,
    gq_ref,
    gk_ref,
    gv_ref,
    go_ref,
    attn_all_ref,
    dn_core,
    dn_in,
    dn_acc,
    out_core,
    out_in,
    out_acc,
    both_in,
    down_in,
    both_sum,
    grads,
    g_core,
    g_in,
    g_acc,
    dq_ref,
    dmixed_ref,
    small_out,
    small_in,
    small_x,
    small_c,
    send,
    recv,
):
    f32, bf16 = jnp.float32, jnp.bfloat16
    place = Place(size)
    at, peer = place.at, place.peer
    traffic = Traffic(place, send, recv)
    rows, width = tokens_ref.shape
    own, quarter = att_ref.shape[-2:]
    kvd = keys_ref.shape[1]
    own_kv = kvd // (size["z"] * size["y"])
    place.greet(around(size))

    half = rows // 2
    dn_steps = [
        reduce_over(place, traffic, dn_in, dn_acc, "xyl", part, dims, (dn_ref, dn_core))
        for part, dims in zip(((0, half), (half, half)), ("xyl", "yxl"))
    ]
    out_steps = [
        reduce_over(place, traffic, out_in, out_acc, "xyl", part, dims, (out_ref, out_core))
        for part, dims in zip(((0, half), (half, half)), ("xyl", "yxl"))
    ]

    def advance(steps):
        for step in steps:
            next(step, None)

    advance(dn_steps)
    order = [(l, y) for l in reversed(range(size["l"])) for y in reversed(range(size["y"]))]
    pieces = []
    for kl, ky in order:
        q = peer("l", kl) * size["y"] + peer("y", ky)
        waits = [
            traffic.start(gboth_ref.at[peer("h", k), q], both_in.at[k - 1, q], both_in.at[k - 1, q], h=k)
            for k in range(1, size["h"])
        ]
        pieces.append((kl, ky, q, waits))
    down_waits = [
        traffic.start(gdown_ref.at[peer("h", k)], down_in.at[k - 1], down_in.at[k - 1], h=k)
        for k in range(1, size["h"])
    ]

    ff_gathers = []

    def finish_piece(kl, ky, q, waits):
        for wait in waits:
            wait()
        total = gboth_ref[at["h"], q].astype(f32)
        for k in range(1, size["h"]):
            total = total + both_in[k - 1, q].astype(f32)
        if kl + ky:
            both_sum[q] = total.astype(bf16)
            here = (at["x"], at["c"], at["l"], at["y"])
            there = (at["x"], at["c"], peer("l", -kl), peer("y", -ky))
            arrived = traffic.start(
                both_sum.at[q], both_all_ref.at[here], both_all_ref.at[there], l=kl, y=ky
            )
        else:
            both_all_ref[at["x"], at["c"], at["l"], at["y"]] = total.astype(bf16)
            arrived = None

        def spread():
            if arrived is not None:
                arrived()
            gather = replica_gather(
                place, traffic, both_all_ref, (peer("l", -kl), peer("y", -ky))
            )
            next(gather)
            ff_gathers.append(gather)

        return spread

    advance(out_steps)
    _, cosine, sine = position_tables(lengths_ref, freq_ref[0:1, :], rows)
    spreads = []
    for _ in range(4):
        advance(dn_steps)

    mine = (at["x"], at["y"], at["l"])
    dnormed_two = dn_acc[mine].astype(f32)
    vec = vec_ref[...]
    hidden = hidden_ref[...]
    dh_two, g_mlp = norm_back(dnormed_two, hidden, vec[2:3, :])
    dhidden = cot_ref[...].astype(f32) + dh_two
    gtok_ref[...] = dhidden
    dres = dhidden.astype(bf16)

    advance(out_steps)
    rest = iter(pieces)

    def weight(share, first, count):
        x, c = share // size["c"], share % size["c"]
        return att_ref[x, c, :, :, :, first : first + count].reshape(width, count)

    def project_back(left, first, count):
        total, used = None, 0
        for share, inside, step in columns(first, count, quarter):
            part = mm(left[:, used : used + step], weight(share, inside, step), TN)
            total = part if total is None else total + part
            used += step
        return total

    def put_grads(left, right, first):
        used = 0
        for share, inside, step in columns(first, right.shape[1], quarter):
            part = mm(left, right[:, used : used + step], CN).astype(bf16)
            x, c = share // size["c"], share % size["c"]
            grads[x, c, :, :, :, inside : inside + step] = part.reshape(size["z"], size["y"], own, step)
            used += step

    dmixed_ref[...] = project_back(dres, width + 2 * kvd, width).astype(bf16)
    put_grads(mixed_ref[...], dres, width + 2 * kvd)

    keys, values = keys_ref[...], values_ref[...]
    group = HEADS // KVH
    dk_sum, dv_sum = {}, {}
    for pair in range(HEADS // 2):
        lanes = pl.ds(pair * 2 * HD, 2 * HD)
        kp, vp = pair_of(keys, pair), pair_of(values, pair)
        dm = dmixed_ref[:, lanes]
        weighted = halves(dm.astype(f32) * mixed_ref[:, lanes].astype(f32))
        dq = dk = dv = jnp.zeros((rows, 2 * HD), f32)
        for i, (qh, kh, dmh) in enumerate(zip(halves(query_ref[:, lanes]), halves(kp), halves(dm))):
            probs = probs_ref[2 * pair + i]
            dprobs = mm(dmh, vp, TN)
            delta = jnp.sum(weighted[i], axis=1, keepdims=True)
            dscores = (probs * (dprobs - delta) * (1.0 / math.sqrt(HD))).astype(bf16)
            dq = dq + mm(dscores, kh)
            dk = dk + mm(dscores, qh, CN)
            dv = dv + mm(probs.astype(bf16), dmh, CN)
        dq_ref[:, lanes] = dq
        which = (2 * pair // group, (2 * pair + 1) // group)
        dk_sum[which] = dk_sum[which] + dk if which in dk_sum else dk
        dv_sum[which] = dv_sum[which] + dv if which in dv_sum else dv
    for piece in rest:
        spreads.append(finish_piece(*piece))
    for wait in down_waits:
        wait()
    down = gdown_ref[at["h"]].astype(f32)
    for k in range(1, size["h"]):
        down = down + down_in[k - 1].astype(f32)
    down_all_ref[at["x"], at["c"]] = down.astype(bf16)
    down_gather = replica_gather(place, traffic, down_all_ref)
    next(down_gather)
    ff_gathers.append(down_gather)

    def join_groups(sums):
        fold = lambda v: v + pltpu.roll(v, HD, 1)
        lo = lanes_of(rows, 2 * HD) < HD
        return jnp.where(lo, fold(sums[0, 0]), fold(sums[1, 1])) + sums[0, 1]

    times = width // rows
    wide_cos = jnp.concatenate([cosine] * times, axis=1)
    wide_sin = jnp.concatenate([sine] * times, axis=1)
    dq = dq_ref[...]
    dq = dq * wide_cos - turn(dq) * wide_sin
    dk = join_groups(dk_sum)
    dk = dk * cosine - turn(dk) * sine
    dv = join_groups(dv_sum)
    normed = normed_ref[...]
    dq_b, dk_b, dv_b = dq.astype(bf16), dk.astype(bf16), dv.astype(bf16)
    put_grads(normed, dq_b, 0)
    put_grads(normed, dk_b, width)
    put_grads(normed, dv_b, width + kvd)
    g_steps = [
        reduce_over(place, traffic, g_in, g_acc, "xzy", part, dims, (grads, g_core))
        for part, dims in zip(row_parts(own), ("xyz", "yzx", "zxy"))
    ]
    advance(g_steps)
    advance(out_steps)

    dnormed = project_back(dq_b, 0, width) + project_back(dk_b, width, kvd)
    dnormed = dnormed + project_back(dv_b, width + kvd, kvd)
    dh_one, g_attn = norm_back(dnormed, tokens_ref[...].astype(f32), vec[1:2, :])
    gtok_ref[...] = gtok_ref[...] + dh_one

    advance(g_steps)
    for spread in spreads:
        spread()

    total = lambda v: jnp.sum(v, axis=0, keepdims=True)
    tall = jnp.concatenate([total(dq), g_attn, g_mlp, jnp.zeros((5, width), f32)], axis=0)
    flat_kv = jnp.concatenate([jnp.zeros((3, kvd), f32), total(dk), total(dv), jnp.zeros((3, kvd), f32)], axis=0)
    lane = lanes_of(8, kvd)
    for s in range(size["z"] * size["y"]):
        a = pltpu.roll(tall, width - s * own, 1) if s else tall
        b = pltpu.roll(flat_kv, kvd - s * own_kv, 1) if s else flat_kv
        a = jnp.where(lane < own, a[:, :kvd], 0.0)
        small_out[s // size["y"], s % size["y"]] = a + jnp.where(lane < own_kv, b, 0.0)
    small_waits = []
    for i, by in enumerate(b for b in around(size) if "h" in b):
        there = (peer("h", by["h"]) * size["l"] + peer("l", by["l"]), peer("y", by["y"]))
        small_waits.append(traffic.start(small_out.at[there], small_in.at[i], small_in.at[i], **by))

    for wait in small_waits:
        wait()
    small = small_out[at["z"], at["y"]]
    for i in range(len(small_waits)):
        small = small + small_in[i]
    small_ref[...] = small
    small_waits = [
        traffic.start(small_ref, small_x.at[k - 1], small_x.at[k - 1], x=k) for k in range(1, size["x"])
    ]
    advance(g_steps)
    for wait in small_waits:
        wait()
    for k in range(1, size["x"]):
        small = small + small_x[k - 1]
    small_out[at["z"], at["y"]] = small
    advance(out_steps)
    advance(out_steps)
    result_ref[...] = (hidden + out_acc[mine].astype(f32)).astype(bf16)
    small_waits = [
        traffic.start(small_out.at[at["z"], at["y"]], small_c.at[k - 1], small_c.at[k - 1], c=k)
        for k in range(1, size["c"])
    ]
    advance(g_steps)
    advance(g_steps)
    attn_all_ref[at["x"], at["c"]] = g_acc[at["x"], at["z"], at["y"]]
    attn_gather = replica_gather(place, traffic, attn_all_ref)
    next(attn_gather)
    ff_gathers.append(attn_gather)
    for wait in small_waits:
        wait()
    for step in [*ff_gathers, *ff_gathers]:
        next(step, None)
    traffic.finish()
    for k in range(1, size["c"]):
        small = small + small_c[k - 1]
    small_ref[...] = small
    start = 0
    for ref in (gq_ref, gk_ref, gv_ref, go_ref):
        to = 0
        for share, first, count in columns(start, ref.shape[1], quarter):
            x, c = share // size["c"], share % size["c"]
            ref[:, to : to + count] = attn_all_ref[x, c, :, first : first + count].astype(f32)
            to += count
        start += ref.shape[1]


def back(size, lengths, tokens, cot, freq, *more):
    f32, bf16 = jnp.float32, jnp.bfloat16
    rows, width = tokens.shape
    gboth, gdown, att = more[2], more[3], more[4]
    own, quarter = att.shape[-2:]
    n = size
    kvd = 2 * HD
    reps = (n["x"], n["c"])
    sets = (n["l"], n["y"])
    shapes = [
        ((rows, width), bf16),
        ((rows, width), f32),
        (reps + sets + gboth.shape[2:], bf16),
        (reps + gdown.shape[1:], bf16),
        ((8, kvd), f32),
        ((own, width), f32),
        ((own, kvd), f32),
        ((own, kvd), f32),
        ((own, width), f32),
    ]
    group = (n["x"], n["y"], n["l"], rows, width)
    owners = (n["x"], n["z"], n["y"], own, quarter)
    others = n["z"] * n["y"] - 1
    scratch = (
        [pltpu.VMEM(reps + (own, quarter), bf16)]
        + [pltpu.VMEM(group, bf16)] * 6
        + [
            pltpu.VMEM((max(1, n["h"] - 1),) + gboth.shape[1:], bf16),
            pltpu.VMEM((max(1, n["h"] - 1),) + gdown.shape[1:], bf16),
            pltpu.VMEM(gboth.shape[1:], bf16),
            pltpu.VMEM(att.shape, bf16),
        ]
        + [pltpu.VMEM(owners, bf16)] * 3
        + [
            pltpu.VMEM((rows, width), f32),
            pltpu.VMEM((rows, width), bf16),
            pltpu.VMEM((n["z"], n["y"], 8, kvd), f32),
            pltpu.VMEM((max(1, others), 8, kvd), f32),
            pltpu.VMEM((max(1, n["x"] - 1), 8, kvd), f32),
            pltpu.VMEM((max(1, n["c"] - 1), 8, kvd), f32),
            pltpu.SemaphoreType.DMA((96,)),
            pltpu.SemaphoreType.DMA((96,)),
        ]
    )
    vmem = pl.BlockSpec(memory_space=pltpu.VMEM)
    return pl.pallas_call(
        functools.partial(back_kernel, size),
        out_shape=[jax.ShapeDtypeStruct(*s) for s in shapes],
        in_specs=[pl.BlockSpec(memory_space=pltpu.SMEM)] + [vmem] * (3 + len(more)),
        out_specs=[vmem] * len(shapes),
        scratch_shapes=scratch,
        compiler_params=pltpu.CompilerParams(
            collective_id=2, has_side_effects=True, vmem_limit_bytes=60 << 20
        ),
    )(lengths, tokens, cot, freq, *more)


def lay_out_kernel(groups, both_ref, gate_ref, up_ref):
    reps, sets, _, wide = both_ref.shape
    part = wide // (2 * groups)
    for half, ref in enumerate((gate_ref, up_ref)):
        for h in range(groups):
            first = (half * groups + h) * part
            for q in range(sets):
                for r in range(reps):
                    to = ((h * sets + q) * reps + r) * part
                    ref[:, to : to + part] = both_ref[r, q, :, first : first + part].astype(jnp.float32)


def lay_out(both, groups):
    reps, sets, own, wide = both.shape
    full = reps * sets * wide // 2
    step = 16
    return pl.pallas_call(
        functools.partial(lay_out_kernel, groups),
        grid=(own // step,),
        out_shape=[jax.ShapeDtypeStruct((own, full), jnp.float32)] * 2,
        in_specs=[pl.BlockSpec((reps, sets, step, wide), lambda i: (0, 0, i, 0))],
        out_specs=[pl.BlockSpec((step, full), lambda i: (i, 0))] * 2,
    )(both)


def by_kernels(
    tokens,
    cotangent,
    lengths,
    query_weight,
    key_weight,
    value_weight,
    output_weight,
    query_bias,
    key_bias,
    value_bias,
    attn_gain,
    gate_weight,
    up_weight,
    down_weight,
    mlp_gain,
):
    grid = Grid()
    size, at = grid.size, grid.at
    shards, reps = grid.shards, grid.reps
    rep = lax.axis_index("rep")
    rows, width = tokens.shape
    own = query_weight.shape[0]
    kvd = key_weight.shape[1]
    own_kv = key_bias.shape[0]
    f32, bf16 = jnp.float32, jnp.bfloat16
    wide = width + 2 * kvd
    total_w = wide + width
    quarter = total_w // reps

    part = down_weight.shape[0] // reps
    sets = size["l"] * size["y"]
    hidden = size["h"] * part

    down_part = lax.dynamic_slice(down_weight, (rep * part, 0), (part, width))
    freq = theta_base ** (-((np.arange(rows) % (HD // 2)).astype(np.float32) * np.float32(2.0 / HD)))
    freq = np.broadcast_to(freq.astype(np.float32)[None, :], (8, rows))
    vectors = [v[None, :] for v in (query_bias, attn_gain, mlp_gain, key_bias, value_bias)]
    att, _, both_mine, down_mine, cot_all, normed_all, *saved = front(
        size,
        lengths,
        tokens,
        cotangent,
        freq,
        query_weight,
        key_weight,
        value_weight,
        output_weight,
        *vectors,
        gate_weight,
        up_weight,
        down_part,
    )
    group = normed_all.shape[:-1]
    both_mine = both_mine.reshape(width, 2 * hidden)
    down_mine = down_mine.reshape(hidden, width)
    cot_all = cot_all.reshape(-1, width)
    normed_all = normed_all.reshape(-1, width)

    dprod = times_transposed(cot_all, down_mine)
    both = jnp.dot(normed_all, both_mine, preferred_element_type=f32)
    gate, upper = both[:, :hidden], both[:, hidden:]
    sigma = jax.nn.sigmoid(gate)
    product = (gate * sigma * upper).astype(bf16)
    dgate = (dprod * upper * sigma * (1.0 + gate * (1.0 - sigma))).astype(bf16)
    dup = (dprod * gate * sigma).astype(bf16)
    dboth = jnp.concatenate([dgate, dup], axis=1)
    dnormed_part = times_transposed(dboth, both_mine).astype(bf16)
    out_part = jnp.dot(product, down_mine, preferred_element_type=f32).astype(bf16)
    grad_both = jnp.dot(normed_all.T, dboth, preferred_element_type=f32).astype(bf16)
    grad_down = jnp.dot(product.T, cot_all, preferred_element_type=f32).astype(bf16)

    result, grad_input, both_all, down_all, vec, *attn_grads = back(
        size,
        lengths,
        tokens,
        cotangent,
        freq,
        dnormed_part.reshape(group + (width,)),
        out_part.reshape(group + (width,)),
        grad_both.reshape(size["h"], sets, own, 2 * hidden),
        grad_down.reshape(size["h"], part, width),
        att,
        *saved,
    )
    down_all = down_all.reshape(reps * part, width).astype(f32)
    grad_gate, grad_up = lay_out(both_all.reshape(reps, sets, own, 2 * hidden), size["h"])

    return (
        result,
        grad_input,
        *attn_grads,
        vec[0, :own],
        vec[3, :own_kv],
        vec[4, :own_kv],
        vec[1, :own],
        grad_gate,
        grad_up,
        down_all,
        vec[2, :own],
    )


def on_device(*args):
    tokens, query_weight, key_weight = args[0], args[3], args[4]
    rows, width = tokens.shape
    total_w = 2 * width + 2 * key_weight.shape[1]
    fits = (
        rows == 2 * HD
        and lax.axis_size("rep") % 2 == 0
        and HEADS // KVH % 2
        and key_weight.shape[1] == 2 * HD
        and query_weight.shape[0] % 16 == 0
        and query_weight.shape[0] <= 128
        and (total_w // lax.axis_size("rep")) % 128 == 0
    )
    return by_kernels(*args) if fits else by_permutes(*args)


def solution(mesh):
    in_specs = (
        P(("rep", "shard"), None),
        P(("rep", "shard"), None),
        P(("rep", "shard"), None),
        P("shard", None),
        P("shard", None),
        P("shard", None),
        P("shard", None),
        P("shard"),
        P("shard"),
        P("shard"),
        P("shard"),
        P("shard", None),
        P("shard", None),
        P("shard", None),
        P("shard"),
    )
    out_specs = (
        P(("rep", "shard"), None),
        P(("rep", "shard"), None),
        P("shard", None),
        P("shard", None),
        P("shard", None),
        P("shard", None),
        P("shard"),
        P("shard"),
        P("shard"),
        P("shard"),
        P("shard", None),
        P("shard", None),
        P("shard", None),
        P("shard"),
    )
    return jax.shard_map(
        on_device, mesh=mesh, in_specs=in_specs, out_specs=out_specs, check_vma=False
    )
```

```python
import functools
import math

import jax
import jax.numpy as jnp
import numpy as np
from jax import lax
from jax.experimental import pallas as pl
from jax.experimental.pallas import tpu as pltpu
from jax.sharding import PartitionSpec as P

HEADS = 14
KVH = 2
HD = 64


theta_base = 1000000.0
eps_norm = 1e-06
masked_score = -1000000000.0


def times_transposed(left, weight):
    return lax.dot_general(
        left, weight, (((1,), (1,)), ((), ())), preferred_element_type=jnp.float32
    )


def tables(lengths_row, rows):
    order = jnp.arange(lengths_row.shape[0])
    ends = jnp.sum(jnp.where(order[None, :] <= order[:, None], lengths_row[None, :], 0), axis=1)
    starts = ends - lengths_row
    places = jnp.arange(rows, dtype=jnp.int32)
    inside = ((places[:, None] >= starts[None, :]) & (places[:, None] < ends[None, :])).astype(
        jnp.int32
    )
    slots = jnp.arange(lengths_row.shape[0], dtype=jnp.int32)
    segment = jnp.sum(inside * slots[None, :], axis=1)
    first = jnp.sum(inside * starts[None, :], axis=1)
    offset = (places - first).astype(jnp.float32)
    half = HD // 2
    freq = theta_base ** (-(jnp.arange(half, dtype=jnp.float32) * (2.0 / HD)))
    angles = offset[:, None] * freq[None, :]
    return (segment, places, jnp.cos(angles), jnp.sin(angles))


def rotate(values, cosine, sine):
    half = values.shape[-1] // 2
    first, second = (values[..., :half], values[..., half:])
    cosine = cosine[:, :, None, :]
    sine = sine[:, :, None, :]
    return jnp.concatenate(
        [first * cosine - second * sine, second * cosine + first * sine], axis=-1
    )


def unrotate(grads, cosine, sine):
    half = grads.shape[-1] // 2
    first, second = (grads[..., :half], grads[..., half:])
    cosine = cosine[:, :, None, :]
    sine = sine[:, :, None, :]
    return jnp.concatenate(
        [first * cosine + second * sine, second * cosine - first * sine], axis=-1
    )


def norm_fwd(hidden, gain):
    scale = lax.rsqrt(jnp.mean(hidden * hidden, axis=-1, keepdims=True) + eps_norm)
    return (scale, hidden * scale * gain.astype(jnp.float32))


def norm_bwd(dnormed, hidden, scale, gain):
    gain_f = gain.astype(jnp.float32)
    dgain = jnp.sum(dnormed * hidden * scale, axis=0)
    inner = dnormed * gain_f
    dhidden = scale * inner - hidden * (scale * scale * scale) * jnp.mean(
        inner * hidden, axis=-1, keepdims=True
    )
    return (dhidden, dgain)


def scores_of(query, keys, segment, places):
    raw = jnp.einsum("igha,jga->ghij", query, keys, preferred_element_type=jnp.float32) * (
        1.0 / math.sqrt(HD)
    )
    allowed = (segment[:, None] == segment[None, :]) & (places[None, :] <= places[:, None])
    return jnp.where(allowed[None, None], raw, masked_score)


def attend(query, keys, values, segment, places):
    raw = scores_of(query, keys, segment, places)
    top = jnp.max(raw, axis=-1, keepdims=True)
    total = jnp.sum(jnp.exp(raw - top), axis=-1)
    lse = top[..., 0] + jnp.log(total)
    probs = jnp.exp(raw - lse[..., None]).astype(jnp.bfloat16)
    mixed = jnp.einsum("ghij,jga->igha", probs, values, preferred_element_type=jnp.float32).astype(
        jnp.bfloat16
    )
    return (mixed, lse)


def attend_back(query, keys, values, mixed, dmixed, lse, segment, places):
    raw = scores_of(query, keys, segment, places)
    probs_f = jnp.exp(raw - lse[..., None])
    probs = probs_f.astype(jnp.bfloat16)
    dvals = jnp.einsum("ghij,igha->jga", probs, dmixed, preferred_element_type=jnp.float32)
    dprobs = jnp.einsum("igha,jga->ghij", dmixed, values, preferred_element_type=jnp.float32)
    delta = jnp.einsum("igha,igha->ghi", dmixed, mixed, preferred_element_type=jnp.float32)
    dscores = (probs_f * (dprobs - delta[..., None]) * (1.0 / math.sqrt(HD))).astype(jnp.bfloat16)
    dquery = jnp.einsum("ghij,jga->igha", dscores, keys, preferred_element_type=jnp.float32)
    dkeys = jnp.einsum("ghij,igha->jga", dscores, query, preferred_element_type=jnp.float32)
    return (dquery, dkeys, dvals)


class Grid:
    def __init__(self):
        self.reps = lax.axis_size("rep")
        self.shards = lax.axis_size("shard")
        c = 2 if self.reps % 2 == 0 else 1
        x = self.reps // c
        y = x if self.shards % x == 0 else 1
        z = self.shards // y
        l = 2 if z % 2 == 0 else 1
        self.size = dict(x=x, c=c, h=z // l, l=l, y=y, z=z)
        rep, shard = lax.axis_index("rep"), lax.axis_index("shard")
        zz = shard // y
        self.at = dict(x=rep // c, c=rep % c, z=zz, y=shard % y, h=zz // l, l=zz % l)

    def send(self, value, **by):
        n = self.size
        pairs = []
        for rep in range(self.reps):
            for shard in range(self.shards):
                at = dict(x=rep // n["c"], c=rep % n["c"], z=shard // n["y"], y=shard % n["y"])
                if "h" in by or "l" in by:
                    h = (at["z"] // n["l"] + by.get("h", 0)) % n["h"]
                    at["z"] = h * n["l"] + (at["z"] + by.get("l", 0)) % n["l"]
                for d in "xczy":
                    at[d] = (at[d] + by.get(d, 0)) % n[d]
                pairs.append(
                    (
                        rep * self.shards + shard,
                        (at["x"] * n["c"] + at["c"]) * self.shards + at["z"] * n["y"] + at["y"],
                    )
                )
        return lax.ppermute(value, ("rep", "shard"), pairs)

    def peer(self, d, k):
        return (self.at[d] + k + self.size[d]) % self.size[d]

    def gather(self, value, d):
        out = jnp.zeros((self.size[d],) + value.shape, value.dtype)
        out = lax.dynamic_update_index_in_dim(out, value, self.at[d], 0)
        for k in range(1, self.size[d]):
            out = lax.dynamic_update_index_in_dim(
                out, self.send(value, **{d: k}), self.peer(d, -k), 0
            )
        return out

    def scatter(self, value, d):
        pick = lambda k: lax.dynamic_index_in_dim(value, self.peer(d, k), 0, keepdims=False)
        total = pick(0).astype(jnp.float32)
        for k in range(1, self.size[d]):
            total = total + self.send(pick(k), **{d: k}).astype(jnp.float32)
        return total.astype(value.dtype)


def by_permutes(
    tokens,
    cotangent,
    lengths,
    query_weight,
    key_weight,
    value_weight,
    output_weight,
    query_bias,
    key_bias,
    value_bias,
    attn_gain,
    gate_weight,
    up_weight,
    down_weight,
    mlp_gain,
):
    grid = Grid()
    size, at = grid.size, grid.at
    shards, reps = grid.shards, grid.reps
    rep = lax.axis_index("rep")
    rows, width = tokens.shape
    own = query_weight.shape[0]
    kvd = key_weight.shape[1]
    own_kv = key_bias.shape[0]
    f32, bf16 = jnp.float32, jnp.bfloat16
    wide = width + 2 * kvd
    total_w = wide + width
    quarter = total_w // reps

    small = jnp.concatenate([query_bias, attn_gain, mlp_gain, key_bias, value_bias])
    extra = 8
    small = jnp.pad(small, (0, extra * quarter - small.shape[0])).reshape(extra, quarter)
    packed = jnp.concatenate([query_weight, key_weight, value_weight, output_weight], axis=1)
    mine = lax.dynamic_slice(packed, (0, rep * quarter), (own, quarter))
    mine = jnp.concatenate([mine, small], axis=0)
    mine = grid.gather(mine, "z")
    mine = grid.gather(mine, "y")
    mine = grid.gather(mine, "x")
    mine = grid.gather(mine, "c")
    full = mine[..., :own, :].transpose(3, 2, 4, 1, 0, 5).reshape(width, total_w)
    qkv_weight = full[:, :wide]
    output_full = full[:, wide:]
    vectors = mine[0, 0, :, :, own:, :].transpose(1, 0, 2, 3).reshape(shards, extra * quarter)
    piece = lambda first, count: vectors[:, first : first + count].reshape(shards * count)
    query_bias_f, attn_gain_f, mlp_gain_f = (piece(i * own, own) for i in range(3))
    key_bias_f = piece(3 * own, own_kv)
    value_bias_f = piece(3 * own + own_kv, own_kv)
    qkv_bias = jnp.concatenate([query_bias_f, key_bias_f, value_bias_f]).astype(f32)

    part = down_weight.shape[0] // reps
    sets = size["l"] * size["y"]
    hidden = size["h"] * part

    def column_sets(weight):
        split = weight.reshape(own, size["h"], sets, reps, part)
        split = lax.dynamic_index_in_dim(split, rep, 3, keepdims=False)
        return split.transpose(2, 0, 1, 3).reshape(sets, own, hidden)

    both_sets = jnp.concatenate([column_sets(gate_weight), column_sets(up_weight)], axis=2)
    down_part = lax.dynamic_slice(down_weight, (rep * part, 0), (part, width))
    both_mine = jnp.zeros((size["h"], size["l"], size["y"], own, 2 * hidden), bf16)
    for kl in range(size["l"]):
        for ky in range(size["y"]):
            block = lax.dynamic_index_in_dim(
                both_sets, grid.peer("l", kl) * size["y"] + grid.peer("y", ky), 0, keepdims=False
            )
            for kh in range(size["h"]):
                got = block if kl + ky + kh == 0 else grid.send(block, h=kh, l=kl, y=ky)
                both_mine = lax.dynamic_update_slice(
                    both_mine,
                    got[None, None, None],
                    (grid.peer("h", -kh), grid.peer("l", -kl), grid.peer("y", -ky), 0, 0),
                )
    both_mine = both_mine.reshape(width, 2 * hidden)
    down_mine = grid.gather(down_part, "h").reshape(hidden, width)

    def gather_tokens(value):
        for d in "lyxc":
            value = grid.gather(value, d)
        return value.reshape(-1, width)

    def scatter_tokens(value):
        value = value.reshape(size["c"], size["x"], size["y"], size["l"], rows, -1)
        for d in "cxyl":
            value = grid.scatter(value, d)
        return value

    cot_all = gather_tokens(cotangent)

    segment, places, cosine, sine = jax.vmap(lambda lens: tables(lens, rows))(lengths)
    flat = tokens.astype(f32)
    scale_one, normed_one = norm_fwd(flat, attn_gain_f)
    normed_one = normed_one.astype(bf16)
    qkv = jnp.dot(normed_one, qkv_weight, preferred_element_type=f32) + qkv_bias
    query = rotate(qkv[:, :width].reshape(1, rows, HEADS, HD), cosine, sine).astype(bf16)
    query = query.reshape(1, rows, KVH, HEADS // KVH, HD)
    keys = rotate(qkv[:, width : width + kvd].reshape(1, rows, KVH, HD), cosine, sine).astype(bf16)
    values = qkv[:, width + kvd :].reshape(1, rows, KVH, HD).astype(bf16)
    mixed, lse = jax.vmap(attend)(query, keys, values, segment, places)
    mixed_flat = mixed.reshape(rows, width)
    hidden_one = flat + jnp.dot(mixed_flat, output_full, preferred_element_type=f32)
    scale_two, normed_two = norm_fwd(hidden_one, mlp_gain_f)
    normed_all = gather_tokens(normed_two.astype(bf16))

    dprod = times_transposed(cot_all, down_mine)
    both = jnp.dot(normed_all, both_mine, preferred_element_type=f32)
    gate, upper = both[:, :hidden], both[:, hidden:]
    sigma = jax.nn.sigmoid(gate)
    product = (gate * sigma * upper).astype(bf16)
    dgate = (dprod * upper * sigma * (1.0 + gate * (1.0 - sigma))).astype(bf16)
    dup = (dprod * gate * sigma).astype(bf16)
    dboth = jnp.concatenate([dgate, dup], axis=1)
    dnormed_part = times_transposed(dboth, both_mine).astype(bf16)
    out_part = jnp.dot(product, down_mine, preferred_element_type=f32).astype(bf16)
    dnormed_two = scatter_tokens(dnormed_part).astype(f32)
    out_sum = scatter_tokens(out_part).astype(f32)
    grad_both = jnp.dot(normed_all.T, dboth, preferred_element_type=f32).astype(bf16)
    grad_down = jnp.dot(product.T, cot_all, preferred_element_type=f32).astype(bf16)

    grad_both = grid.scatter(grad_both.reshape(size["h"], sets, own, 2 * hidden), "h")
    grad_down = grid.scatter(grad_down.reshape(size["h"], part, width), "h")
    owned = jnp.zeros((size["l"], size["y"], own, 2 * hidden), bf16)
    for kl in range(size["l"]):
        for ky in range(size["y"]):
            block = lax.dynamic_index_in_dim(
                grad_both, grid.peer("l", kl) * size["y"] + grid.peer("y", ky), 0, keepdims=False
            )
            got = block if kl + ky == 0 else grid.send(block, l=kl, y=ky)
            owned = lax.dynamic_update_slice(
                owned, got[None, None], (grid.peer("l", -kl), grid.peer("y", -ky), 0, 0)
            )

    def from_replicas(value):
        return grid.gather(grid.gather(value, "c"), "x").reshape((reps,) + value.shape)

    both_all = from_replicas(owned.reshape(sets, own, 2 * hidden))
    down_all = from_replicas(grad_down).reshape(reps * part, width).astype(f32)

    def joined(first):
        half = both_all[..., first : first + hidden].reshape(reps, sets, own, size["h"], part)
        return half.transpose(2, 3, 1, 0, 4).reshape(own, -1).astype(f32)

    result = (hidden_one + out_sum).astype(bf16)

    dh_two, grad_mlp_gain = norm_bwd(dnormed_two, hidden_one, scale_two, mlp_gain_f)
    dhidden = cotangent.astype(f32) + dh_two
    dres = dhidden.astype(bf16)
    grad_output = jnp.dot(mixed_flat.T, dres, preferred_element_type=f32).astype(bf16)
    dmixed = times_transposed(dres, output_full).astype(bf16)
    dmixed = dmixed.reshape(1, rows, KVH, HEADS // KVH, HD)
    dquery, dkeys, dvals = jax.vmap(attend_back)(
        query, keys, values, mixed, dmixed, lse, segment, places
    )
    dquery = unrotate(dquery.reshape(1, rows, HEADS, HD), cosine, sine).reshape(rows, width)
    dkeys = unrotate(dkeys, cosine, sine).reshape(rows, kvd)
    dvals = dvals.reshape(rows, kvd)
    dqkv = jnp.concatenate([dquery, dkeys, dvals], axis=1)
    grad_bias = jnp.sum(dqkv, axis=0)
    dqkv_b = dqkv.astype(bf16)
    grad_qkv = jnp.dot(normed_one.T, dqkv_b, preferred_element_type=f32).astype(bf16)
    dnormed_one = times_transposed(dqkv_b, qkv_weight)
    dh_one, grad_attn_gain = norm_bwd(dnormed_one, flat, scale_one, attn_gain_f)
    grad_input = dhidden + dh_one

    cut = lambda v, count: v.reshape(shards, count)
    small_g = jnp.concatenate(
        [
            cut(grad_bias[:width], own),
            cut(grad_attn_gain, own),
            cut(grad_mlp_gain, own),
            cut(grad_bias[width : width + kvd], own_kv),
            cut(grad_bias[width + kvd :], own_kv),
        ],
        axis=1,
    )
    small_n = small_g.shape[1]
    small_g = jnp.pad(small_g, ((0, 0), (0, extra * quarter - small_n)))
    small_g = jnp.broadcast_to(
        small_g.reshape(shards, 1, extra, quarter).astype(bf16), (shards, reps, extra, quarter)
    )
    grads = jnp.concatenate([grad_qkv, grad_output], axis=1)
    grads = grads.reshape(shards, own, reps, quarter).transpose(0, 2, 1, 3)
    grads = jnp.concatenate([grads, small_g], axis=2)
    grads = grads.reshape(size["z"], size["y"], size["x"], size["c"], own + extra, quarter)
    grads = grid.scatter(grads.transpose(3, 2, 1, 0, 4, 5), "c")
    grads = grid.scatter(grads, "x")
    grads = grid.scatter(grads, "y")
    grads = grid.scatter(grads, "z")
    vec = grads[own:].reshape(extra * quarter)[:small_n].astype(f32)
    attn_all = from_replicas(grads[:own]).transpose(1, 0, 2).reshape(own, total_w).astype(f32)

    return (
        result,
        grad_input,
        attn_all[:, :width],
        attn_all[:, width : width + kvd],
        attn_all[:, width + kvd : wide],
        attn_all[:, wide:],
        vec[:own],
        vec[3 * own : 3 * own + own_kv],
        vec[3 * own + own_kv :],
        vec[own : 2 * own],
        joined(0),
        joined(hidden),
        down_all,
        vec[2 * own : 3 * own],
    )


MESH = pl.DeviceIdType.MESH
TN = (((1,), (1,)), ((), ()))
NN = (((1,), (0,)), ((), ()))
CN = (((0,), (0,)), ((), ()))


def mm(left, right, dims=NN):
    return lax.dot_general(left, right, dims, preferred_element_type=jnp.float32)


class Place:
    def __init__(self, size):
        self.size = size
        rep, shard = lax.axis_index("rep"), lax.axis_index("shard")
        z = shard // size["y"]
        self.at = dict(
            x=rep // size["c"],
            c=rep % size["c"],
            z=z,
            y=shard % size["y"],
            h=z // size["l"],
            l=z % size["l"],
        )

    def peer(self, d, k):
        n, at = self.size[d], self.at[d]
        if n & (n - 1):
            return (at + k + n) % n
        k, bit = abs(k), 1
        while bit < n:
            if k & bit:
                at = at + bit * (1 - 2 * ((at // bit) % 2))
            bit *= 2
        return at

    def device(self, **by):
        at = dict(self.at)
        for d, k in by.items():
            at[d] = self.peer(d, k)
        if "h" in by or "l" in by:
            at["z"] = at["h"] * self.size["l"] + at["l"]
        return (at["x"] * self.size["c"] + at["c"], at["z"] * self.size["y"] + at["y"])

    def greet(self, everyone):
        barrier = pltpu.get_barrier_semaphore()
        for by in everyone:
            pl.semaphore_signal(barrier, inc=1, device_id=self.device(**by), device_id_type=MESH)
        pl.semaphore_wait(barrier, len(everyone))


class Traffic:
    def __init__(self, place, send, recv):
        self.place, self.send, self.recv, self.used, self.sent = place, send, recv, 0, []

    def start(self, src, dst, arriving, **by):
        i = self.used
        self.used += 1
        copy = pltpu.make_async_remote_copy(
            src_ref=src,
            dst_ref=dst,
            send_sem=self.send.at[i],
            recv_sem=self.recv.at[i],
            device_id=self.place.device(**by),
            device_id_type=MESH,
        )
        copy.start()
        self.sent.append(copy)
        return pltpu.make_async_remote_copy(
            src_ref=arriving,
            dst_ref=arriving,
            send_sem=self.send.at[i],
            recv_sem=self.recv.at[i],
            device_id=self.place.device(**by),
            device_id_type=MESH,
        ).wait_recv

    def finish(self):
        for copy in self.sent:
            copy.wait_send()


def around(size):
    others = [
        dict(h=h, l=l, y=y)
        for h in range(size["h"])
        for l in range(size["l"])
        for y in range(size["y"])
        if h + l + y
    ]
    return others + [dict(x=k) for k in range(1, size["x"])] + [dict(c=k) for k in range(1, size["c"])]


def row_parts(rows):
    step = -(-rows // 48) * 16
    return [(0, step), (step, step), (2 * step, rows - 2 * step)]


def token_gather(place, traffic, buf, rows, dims):
    names = "xcyl"
    at = place.at

    def region(held, **fixed):
        index = []
        for d in names:
            if d in fixed:
                index.append(fixed[d])
            elif d in held:
                index.append(pl.ds(0, place.size[d]))
            else:
                index.append(at[d])
        return buf.at[tuple(index) + (pl.ds(*rows),)]

    def cores(held, **fixed):
        here = region(held, **fixed)
        return [
            traffic.start(here, here, region(held, **{**fixed, "c": place.peer("c", -k)}), c=k)
            for k in range(1, place.size["c"])
        ]

    last = cores("")
    held = ""
    for d in dims:
        here = region(held)
        got = [
            (k, traffic.start(here, here, region(held, **{d: place.peer(d, -k)}), **{d: k}))
            for k in range(1, place.size[d])
        ]
        yield
        for k, wait in got:
            wait()
            last += cores(held, **{d: place.peer(d, -k)})
        held += d
    yield
    for wait in last:
        wait()


def lanes_of(count, width):
    return lax.broadcasted_iota(jnp.int32, (count, width), 1)


def turn(value):
    count, width = value.shape
    half = HD // 2
    first = lanes_of(count, width) % HD < half
    return jnp.where(first, pltpu.roll(value, width - half, 1), pltpu.roll(value, half, 1))


def position_tables(lengths_ref, freq, rows):
    i0 = lax.broadcasted_iota(jnp.int32, (rows, rows), 0)
    i1 = lax.broadcasted_iota(jnp.int32, (rows, rows), 1)
    first0, first1 = jnp.zeros_like(i0), jnp.zeros_like(i1)
    end = jnp.int32(0)
    for j in range(lengths_ref.shape[1]):
        count = lengths_ref[0, j]
        end = end + count
        first0 = first0 + jnp.where(i0 >= end, count, 0)
        first1 = first1 + jnp.where(i1 >= end, count, 0)
    allowed = (first0 == first1) & (i1 <= i0)
    angle = (i0 - first0).astype(jnp.float32) * freq
    sign = jnp.where(lanes_of(rows, rows) % HD < HD // 2, -1.0, 1.0)
    return allowed, jnp.cos(angle), jnp.sin(angle) * sign


def columns(first, count, quarter):
    out = []
    while count:
        share, inside = first // quarter, first % quarter
        step = min(count, quarter - inside)
        out.append((share, inside, step))
        first, count = first + step, count - step
    return out


def pair_of(keys, pair):
    group = HEADS // KVH
    low, high = 2 * pair // group, (2 * pair + 1) // group
    if (low, high) == (0, 1):
        return keys
    other = pltpu.roll(keys.astype(jnp.float32), HD, 1).astype(keys.dtype)
    lo = lanes_of(*keys.shape) < HD
    return jnp.where(lo, keys, other) if low == 0 else jnp.where(lo, other, keys)


def halves(value):
    lo = lanes_of(*value.shape) < HD
    zero = jnp.zeros_like(value)
    return jnp.where(lo, value, zero), jnp.where(lo, zero, value)


def front_kernel(
    size,
    lengths_ref,
    tokens_ref,
    cot_ref,
    freq_ref,
    query_w_ref,
    key_w_ref,
    value_w_ref,
    output_w_ref,
    query_b_ref,
    attn_gain_ref,
    mlp_gain_ref,
    key_b_ref,
    value_b_ref,
    gate_w_ref,
    up_w_ref,
    down_ref,
    att_ref,
    small_all_ref,
    both_ref,
    down_all_ref,
    cot_all_ref,
    norm_all_ref,
    vec_ref,
    normed_ref,
    query_ref,
    keys_ref,
    values_ref,
    mixed_ref,
    probs_ref,
    hidden_ref,
    sets_ref,
    send,
    recv,
):
    f32, bf16 = jnp.float32, jnp.bfloat16
    place = Place(size)
    at, peer = place.at, place.peer
    traffic = Traffic(place, send, recv)
    rows, width = tokens_ref.shape
    own, quarter = att_ref.shape[-2:]
    kvd = keys_ref.shape[1]
    reps = size["x"] * size["c"]
    rep = at["x"] * size["c"] + at["c"]
    part = down_ref.shape[0]
    groups, sets = size["h"], size["l"] * size["y"]
    hid = groups * part
    small_all_ref[at["z"], at["y"]] = jnp.zeros(small_all_ref.shape[2:], f32)
    vectors = (query_b_ref, attn_gain_ref, mlp_gain_ref, key_b_ref, value_b_ref)
    for i, ref in enumerate(vectors):
        small_all_ref[at["z"], at["y"], i : i + 1, : ref.shape[1]] = ref[...].astype(f32)
    for r in range(reps):

        @pl.when(rep == r)
        def _():
            to, start = 0, 0
            for ref in (query_w_ref, key_w_ref, value_w_ref, output_w_ref):
                first = max(r * quarter, start)
                last = min((r + 1) * quarter, start + ref.shape[1])
                if first < last:
                    count = last - first
                    att_ref[at["x"], at["c"], at["z"], at["y"], :, to : to + count] = ref[
                        :, first - start : last - start
                    ]
                    to += count
                start += ref.shape[1]

    cot_all_ref[at["x"], at["c"], at["y"], at["l"]] = cot_ref[...]
    q_own = at["l"] * size["y"] + at["y"]
    down_all_ref[at["h"]] = down_ref[...]
    place.greet(around(size))

    def block(z, y, x=None, c=None):
        return att_ref.at[at["x"] if x is None else x, at["c"] if c is None else c, z, y]

    def to_core(z, y, x):
        return [
            traffic.start(block(z, y, x), block(z, y, x), block(z, y, x, peer("c", -k)), c=k)
            for k in range(1, size["c"])
        ]

    def to_x(z, y):
        return [
            (traffic.start(block(z, y), block(z, y), block(z, y, peer("x", -k)), x=k), z, y, peer("x", -k))
            for k in range(1, size["x"])
        ]

    def to_y(z):
        return [
            (traffic.start(block(z, at["y"]), block(z, at["y"]), block(z, peer("y", -k)), y=k), z, peer("y", -k))
            for k in range(1, size["y"])
        ]

    z, y = at["z"], at["y"]
    mine = block(z, y)
    from_z = [
        (traffic.start(mine, mine, block(peer("z", -k), y), z=k), peer("z", -k))
        for k in range(1, size["z"])
    ]
    from_y, from_x = to_y(z), to_x(z, y)
    waits = to_core(z, y, at["x"])
    small_waits = []
    for by in around(size):
        if "h" in by:
            here = small_all_ref.at[z, y]
            there = small_all_ref.at[peer("h", -by["h"]) * size["l"] + peer("l", -by["l"]), peer("y", -by["y"])]
            small_waits.append(traffic.start(here, here, there, **by))
    cot_steps = [
        token_gather(place, traffic, cot_all_ref, part, dims)
        for part, dims in zip(((0, rows // 2), (rows // 2, rows // 2)), ("lxy", "lyx"))
    ]
    for step in cot_steps:
        next(step)

    flat = tokens_ref[...].astype(f32)
    scale = lax.rsqrt(jnp.mean(flat * flat, axis=1, keepdims=True) + eps_norm)
    allowed, cosine, sine = position_tables(lengths_ref, freq_ref[0:1, :], rows)
    for r in range(reps):

        @pl.when(rep == r)
        def _():
            for q in range(sets):
                for half, ref in enumerate((gate_w_ref, up_w_ref)):
                    for h in range(groups):
                        first = ((h * sets + q) * reps + r) * part
                        to = half * hid + h * part
                        sets_ref[q, :, to : to + part] = ref[:, first : first + part]

    both_ref[at["h"], at["l"], at["y"]] = sets_ref[q_own]

    for wait, zz in from_z:
        wait()
        from_y += to_y(zz)
        from_x += to_x(zz, y)
        waits += to_core(zz, y, at["x"])

    ff_waits = []
    for by in around(size):
        if "h" in by:
            q = peer("l", by["l"]) * size["y"] + peer("y", by["y"])
            ff_waits.append(
                traffic.start(
                    sets_ref.at[q],
                    both_ref.at[at["h"], at["l"], at["y"]],
                    both_ref.at[peer("h", -by["h"]), peer("l", -by["l"]), peer("y", -by["y"])],
                    **by,
                )
            )
    for k in range(1, size["h"]):
        ff_waits.append(
            traffic.start(down_ref, down_all_ref.at[at["h"]], down_all_ref.at[peer("h", -k)], h=k)
        )

    for wait, zz, yy in from_y:
        wait()
        from_x += to_x(zz, yy)
        waits += to_core(zz, yy, at["x"])
    for step in cot_steps:
        next(step)
    for wait, zz, yy, xx in from_x:
        wait()
        waits += to_core(zz, yy, xx)
    for step in cot_steps:
        next(step)
    for wait in small_waits + waits:
        wait()

    own_kv = kvd // (size["z"] * size["y"])
    vec = jnp.zeros((8, width), f32)
    kv = jnp.zeros((8, kvd), f32)
    for s in range(size["z"] * size["y"]):
        piece = small_all_ref[s // size["y"], s % size["y"]]
        piece_w = jnp.where(lanes_of(8, piece.shape[1]) < own, piece, 0.0)
        wider = jnp.concatenate([piece_w, jnp.zeros((8, width - piece.shape[1]), f32)], axis=1)
        vec = vec + (pltpu.roll(wider, s * own, 1) if s else wider)
        piece_kv = jnp.where(lanes_of(8, kvd) < own_kv, piece[:, :kvd], 0.0)
        kv = kv + (pltpu.roll(piece_kv, s * own_kv, 1) if s else piece_kv)
    vec_ref[...] = vec

    def weight(share, first, count):
        x, c = share // size["c"], share % size["c"]
        return att_ref[x, c, :, :, :, first : first + count].reshape(width, count)

    def project(left, first, count):
        return jnp.concatenate(
            [mm(left, weight(*piece)) for piece in columns(first, count, quarter)], axis=1
        )

    normed = (flat * scale * vec[1:2, :]).astype(bf16)
    normed_ref[...] = normed
    times = width // rows
    wide_cos = jnp.concatenate([cosine] * times, axis=1)
    wide_sin = jnp.concatenate([sine] * times, axis=1)
    query = project(normed, 0, width) + vec[0:1, :]
    query = (query * wide_cos + turn(query) * wide_sin).astype(bf16)
    query_ref[...] = query
    keys = project(normed, width, kvd) + kv[3:4, :]
    keys = (keys * cosine + turn(keys) * sine).astype(bf16)
    keys_ref[...] = keys
    values = (project(normed, width + kvd, kvd) + kv[4:5, :]).astype(bf16)
    values_ref[...] = values

    for pair in range(HEADS // 2):
        lanes = pl.ds(pair * 2 * HD, 2 * HD)
        kp, vp = pair_of(keys, pair), pair_of(values, pair)
        total = None
        for i, (qh, vh) in enumerate(zip(halves(query_ref[:, lanes]), halves(vp))):
            raw = jnp.where(allowed, mm(qh, kp, TN) * (1.0 / math.sqrt(HD)), masked_score)
            top = jnp.max(raw, axis=1, keepdims=True)
            lse = top + jnp.log(jnp.sum(jnp.exp(raw - top), axis=1, keepdims=True))
            probs = jnp.exp(raw - lse)
            probs_ref[2 * pair + i] = probs
            part = mm(probs.astype(bf16), vh)
            total = part if total is None else total + part
        mixed_ref[:, lanes] = total.astype(bf16)

    hidden = flat + project(mixed_ref[...], width + 2 * kvd, width)
    hidden_ref[...] = hidden
    scale_two = lax.rsqrt(jnp.mean(hidden * hidden, axis=1, keepdims=True) + eps_norm)
    norm_all_ref[at["x"], at["c"], at["y"], at["l"]] = (hidden * scale_two * vec[2:3, :]).astype(bf16)
    steps = [
        token_gather(place, traffic, norm_all_ref, part, dims)
        for part, dims in zip(row_parts(rows), ("lxy", "xyl", "ylx"))
    ]
    for _ in range(4):
        for step in steps:
            next(step, None)
    for step in [*cot_steps, *steps]:
        for _ in step:
            pass
    for wait in ff_waits:
        wait()
    traffic.finish()


def front(size, lengths, tokens, cot, freq, *params):
    f32, bf16 = jnp.float32, jnp.bfloat16
    rows, width = tokens.shape
    own = params[0].shape[0]
    down = params[-1]
    kvd = 2 * HD
    n = size
    quarter = 2 * (width + kvd) // (n["x"] * n["c"])
    sets = (n["l"] * n["y"], own, 2 * n["h"] * down.shape[0])
    group = (n["x"], n["c"], n["y"], n["l"])
    shapes = [
        ((n["x"], n["c"], n["z"], n["y"], own, quarter), bf16),
        ((n["z"], n["y"], 8, 128), f32),
        ((n["h"], n["l"], n["y"]) + sets[1:], bf16),
        ((n["h"],) + down.shape, bf16),
        (group + (rows, width), bf16),
        (group + (rows, width), bf16),
        ((8, width), f32),
        ((rows, width), bf16),
        ((rows, width), bf16),
        ((rows, kvd), bf16),
        ((rows, kvd), bf16),
        ((rows, width), bf16),
        ((HEADS, rows, rows), f32),
        ((rows, width), f32),
    ]
    vmem = pl.BlockSpec(memory_space=pltpu.VMEM)
    return pl.pallas_call(
        functools.partial(front_kernel, size),
        out_shape=[jax.ShapeDtypeStruct(*s) for s in shapes],
        in_specs=[pl.BlockSpec(memory_space=pltpu.SMEM)] + [vmem] * (3 + len(params)),
        out_specs=[vmem] * len(shapes),
        scratch_shapes=[
            pltpu.VMEM(sets, bf16),
            pltpu.SemaphoreType.DMA((96,)),
            pltpu.SemaphoreType.DMA((96,)),
        ],
        compiler_params=pltpu.CompilerParams(
            collective_id=1, has_side_effects=True, vmem_limit_bytes=56 << 20
        ),
    )(lengths, tokens, cot, freq, *params)


def reduce_over(place, traffic, inbox, acc, names, rows, dims, source=None):
    at, size, peer = place.at, place.size, place.peer

    def region(buf, done, fixed, over):
        index = []
        for d in over:
            index.append(fixed[d] if d in fixed else at[d] if d in done else pl.ds(0, size[d]))
        return buf.at[tuple(index) + (pl.ds(*rows),)]

    def blocks(done):
        found = [()]
        for d in names:
            found = [f + (v,) for f in found for v in ([at[d]] if d in done else range(size[d]))]
        return found

    cut = pl.ds(*rows)
    if source is not None:
        first, core_in = source
        with_c = names[0] + "c" + names[1:]
        wait = traffic.start(
            region(first, "", {"c": peer("c", 1)}, with_c), region(core_in, "", {}, names), region(core_in, "", {}, names), c=1
        )
        yield
        wait()
        for b in blocks(""):
            acc[b + (cut,)] = first[(b[0], at["c"]) + b[1:] + (cut,)] + core_in[b + (cut,)]
    done = ""
    for d in dims:
        waits = [
            traffic.start(
                region(acc, done, {d: peer(d, k)}, names),
                region(inbox, done, {d: at[d]}, names),
                region(inbox, done, {d: peer(d, -k)}, names),
                **{d: k},
            )
            for k in range(1, size[d])
        ]
        yield
        for wait in waits:
            wait()
        at_d = names.index(d)
        for b in blocks(done + d):
            if size[d] == 2:
                other = b[:at_d] + (peer(d, 1),) + b[at_d + 1 :]
                acc[b + (cut,)] = acc[b + (cut,)] + inbox[other + (cut,)]
                continue
            total = acc[b + (cut,)].astype(jnp.float32)
            for k in range(1, size[d]):
                other = b[:at_d] + (peer(d, -k),) + b[at_d + 1 :]
                total = total + inbox[other + (cut,)].astype(jnp.float32)
            acc[b + (cut,)] = total.astype(acc.dtype)
        done += d


def replica_gather(place, traffic, buf, index=()):
    at, peer, size = place.at, place.peer, place.size

    def block(x, c):
        return buf.at[(x, c) + index]

    def to_core(x):
        return [
            traffic.start(block(x, at["c"]), block(x, at["c"]), block(x, peer("c", -k)), c=k)
            for k in range(1, size["c"])
        ]

    mine = block(at["x"], at["c"])
    got = [
        (k, traffic.start(mine, mine, block(peer("x", -k), at["c"]), x=k)) for k in range(1, size["x"])
    ]
    last = to_core(at["x"])
    yield
    for k, wait in got:
        wait()
        last += to_core(peer("x", -k))
    yield
    for wait in last:
        wait()


def norm_back(dnormed, hidden, gain):
    scale = lax.rsqrt(jnp.mean(hidden * hidden, axis=1, keepdims=True) + eps_norm)
    dgain = jnp.sum(dnormed * hidden * scale, axis=0, keepdims=True)
    inner = dnormed * gain
    dhidden = scale * inner - hidden * (scale * scale * scale) * jnp.mean(
        inner * hidden, axis=1, keepdims=True
    )
    return dhidden, dgain


def back_kernel(
    size,
    lengths_ref,
    tokens_ref,
    cot_ref,
    freq_ref,
    dn_ref,
    out_ref,
    gboth_ref,
    gdown_ref,
    att_ref,
    vec_ref,
    normed_ref,
    query_ref,
    keys_ref,
    values_ref,
    mixed_ref,
    probs_ref,
    hidden_ref,
    result_ref,
    gtok_ref,
    both_all_ref,
    down_all_ref,
    small_ref,
    attn_all_ref,
    dn_core,
    dn_in,
    dn_acc,
    out_core,
    out_in,
    out_acc,
    both_in,
    down_in,
    both_sum,
    grads,
    g_core,
    g_in,
    g_acc,
    dq_ref,
    dmixed_ref,
    small_out,
    small_in,
    small_x,
    small_c,
    send,
    recv,
):
    f32, bf16 = jnp.float32, jnp.bfloat16
    place = Place(size)
    at, peer = place.at, place.peer
    traffic = Traffic(place, send, recv)
    rows, width = tokens_ref.shape
    own, quarter = att_ref.shape[-2:]
    kvd = keys_ref.shape[1]
    own_kv = kvd // (size["z"] * size["y"])
    place.greet(around(size))

    half = rows // 2
    dn_steps = [
        reduce_over(place, traffic, dn_in, dn_acc, "xyl", part, dims, (dn_ref, dn_core))
        for part, dims in zip(((0, half), (half, half)), ("xyl", "yxl"))
    ]
    out_steps = [
        reduce_over(place, traffic, out_in, out_acc, "xyl", part, dims, (out_ref, out_core))
        for part, dims in zip(((0, half), (half, half)), ("xyl", "yxl"))
    ]

    def advance(steps):
        for step in steps:
            next(step, None)

    advance(dn_steps)
    order = [(l, y) for l in reversed(range(size["l"])) for y in reversed(range(size["y"]))]

    def start_piece(kl, ky):
        q = peer("l", kl) * size["y"] + peer("y", ky)
        waits = [
            traffic.start(gboth_ref.at[peer("h", k), q], both_in.at[k - 1, q], both_in.at[k - 1, q], h=k)
            for k in range(1, size["h"])
        ]
        return kl, ky, q, waits

    few = (len(order) + 1) // 2
    pieces = [start_piece(*piece) for piece in order[:few]]

    ff_gathers = []

    def finish_piece(kl, ky, q, waits):
        for wait in waits:
            wait()
        total = gboth_ref[at["h"], q].astype(f32)
        for k in range(1, size["h"]):
            total = total + both_in[k - 1, q].astype(f32)
        if kl + ky:
            both_sum[q] = total.astype(bf16)
            here = (at["x"], at["c"], at["l"], at["y"])
            there = (at["x"], at["c"], peer("l", -kl), peer("y", -ky))
            arrived = traffic.start(
                both_sum.at[q], both_all_ref.at[here], both_all_ref.at[there], l=kl, y=ky
            )
        else:
            both_all_ref[at["x"], at["c"], at["l"], at["y"]] = total.astype(bf16)
            arrived = None

        def spread():
            if arrived is not None:
                arrived()
            gather = replica_gather(
                place, traffic, both_all_ref, (peer("l", -kl), peer("y", -ky))
            )
            next(gather)
            ff_gathers.append(gather)

        return spread

    _, cosine, sine = position_tables(lengths_ref, freq_ref[0:1, :], rows)
    spreads = []
    advance(dn_steps)
    advance(out_steps)
    advance(dn_steps)
    pieces += [start_piece(*piece) for piece in order[few:]]
    advance(dn_steps)
    advance(dn_steps)
    down_waits = [
        traffic.start(gdown_ref.at[peer("h", k)], down_in.at[k - 1], down_in.at[k - 1], h=k)
        for k in range(1, size["h"])
    ]

    mine = (at["x"], at["y"], at["l"])
    dnormed_two = dn_acc[mine].astype(f32)
    vec = vec_ref[...]
    hidden = hidden_ref[...]
    dh_two, g_mlp = norm_back(dnormed_two, hidden, vec[2:3, :])
    dhidden = cot_ref[...].astype(f32) + dh_two
    gtok_ref[...] = dhidden
    dres = dhidden.astype(bf16)

    advance(out_steps)
    spreads += [finish_piece(*piece) for piece in pieces[:few]]

    def weight(share, first, count):
        x, c = share // size["c"], share % size["c"]
        return att_ref[x, c, :, :, :, first : first + count].reshape(width, count)

    def project_back(left, first, count):
        total, used = None, 0
        for share, inside, step in columns(first, count, quarter):
            part = mm(left[:, used : used + step], weight(share, inside, step), TN)
            total = part if total is None else total + part
            used += step
        return total

    def put_grads(left, right, first):
        used = 0
        for share, inside, step in columns(first, right.shape[1], quarter):
            part = mm(left, right[:, used : used + step], CN).astype(bf16)
            x, c = share // size["c"], share % size["c"]
            grads[x, c, :, :, :, inside : inside + step] = part.reshape(size["z"], size["y"], own, step)
            used += step

    dmixed_ref[...] = project_back(dres, width + 2 * kvd, width).astype(bf16)
    put_grads(mixed_ref[...], dres, width + 2 * kvd)

    keys, values = keys_ref[...], values_ref[...]
    group = HEADS // KVH
    dk_sum, dv_sum = {}, {}
    for pair in range(HEADS // 2):
        lanes = pl.ds(pair * 2 * HD, 2 * HD)
        kp, vp = pair_of(keys, pair), pair_of(values, pair)
        dm = dmixed_ref[:, lanes]
        weighted = halves(dm.astype(f32) * mixed_ref[:, lanes].astype(f32))
        dq = dk = dv = jnp.zeros((rows, 2 * HD), f32)
        for i, (qh, kh, dmh) in enumerate(zip(halves(query_ref[:, lanes]), halves(kp), halves(dm))):
            probs = probs_ref[2 * pair + i]
            dprobs = mm(dmh, vp, TN)
            delta = jnp.sum(weighted[i], axis=1, keepdims=True)
            dscores = (probs * (dprobs - delta) * (1.0 / math.sqrt(HD))).astype(bf16)
            dq = dq + mm(dscores, kh)
            dk = dk + mm(dscores, qh, CN)
            dv = dv + mm(probs.astype(bf16), dmh, CN)
        dq_ref[:, lanes] = dq
        which = (2 * pair // group, (2 * pair + 1) // group)
        dk_sum[which] = dk_sum[which] + dk if which in dk_sum else dk
        if pair == HEADS // 4:
            for spread in spreads:
                spread()
            spreads = []
        dv_sum[which] = dv_sum[which] + dv if which in dv_sum else dv

    spreads += [finish_piece(*piece) for piece in pieces[few:]]
    for wait in down_waits:
        wait()
    down = gdown_ref[at["h"]].astype(f32)
    for k in range(1, size["h"]):
        down = down + down_in[k - 1].astype(f32)
    down_all_ref[at["x"], at["c"]] = down.astype(bf16)
    down_gather = replica_gather(place, traffic, down_all_ref)
    next(down_gather)
    ff_gathers.append(down_gather)

    def join_groups(sums):
        fold = lambda v: v + pltpu.roll(v, HD, 1)
        lo = lanes_of(rows, 2 * HD) < HD
        return jnp.where(lo, fold(sums[0, 0]), fold(sums[1, 1])) + sums[0, 1]

    times = width // rows
    wide_cos = jnp.concatenate([cosine] * times, axis=1)
    wide_sin = jnp.concatenate([sine] * times, axis=1)
    dq = dq_ref[...]
    dq = dq * wide_cos - turn(dq) * wide_sin
    dk = join_groups(dk_sum)
    dk = dk * cosine - turn(dk) * sine
    dv = join_groups(dv_sum)
    normed = normed_ref[...]
    dq_b, dk_b, dv_b = dq.astype(bf16), dk.astype(bf16), dv.astype(bf16)
    put_grads(normed, dq_b, 0)
    put_grads(normed, dk_b, width)
    put_grads(normed, dv_b, width + kvd)
    g_steps = [
        reduce_over(place, traffic, g_in, g_acc, "xzy", part, dims, (grads, g_core))
        for part, dims in zip(row_parts(own), ("xyz", "yzx", "zxy"))
    ]
    advance(g_steps)

    dnormed = project_back(dq_b, 0, width) + project_back(dk_b, width, kvd)
    dnormed = dnormed + project_back(dv_b, width + kvd, kvd)
    dh_one, g_attn = norm_back(dnormed, tokens_ref[...].astype(f32), vec[1:2, :])
    gtok_ref[...] = gtok_ref[...] + dh_one

    advance(g_steps)
    advance(out_steps)

    total = lambda v: jnp.sum(v, axis=0, keepdims=True)
    tall = jnp.concatenate([total(dq), g_attn, g_mlp, jnp.zeros((5, width), f32)], axis=0)
    flat_kv = jnp.concatenate([jnp.zeros((3, kvd), f32), total(dk), total(dv), jnp.zeros((3, kvd), f32)], axis=0)
    lane = lanes_of(8, kvd)
    for s in range(size["z"] * size["y"]):
        a = pltpu.roll(tall, width - s * own, 1) if s else tall
        b = pltpu.roll(flat_kv, kvd - s * own_kv, 1) if s else flat_kv
        a = jnp.where(lane < own, a[:, :kvd], 0.0)
        small_out[s // size["y"], s % size["y"]] = a + jnp.where(lane < own_kv, b, 0.0)
    small_waits = []
    for i, by in enumerate(b for b in around(size) if "h" in b):
        there = (peer("h", by["h"]) * size["l"] + peer("l", by["l"]), peer("y", by["y"]))
        small_waits.append(traffic.start(small_out.at[there], small_in.at[i], small_in.at[i], **by))

    for wait in small_waits:
        wait()
    for spread in spreads:
        spread()
    small = small_out[at["z"], at["y"]]
    for i in range(len(small_waits)):
        small = small + small_in[i]
    small_ref[...] = small
    small_waits = [
        traffic.start(small_ref, small_x.at[k - 1], small_x.at[k - 1], x=k) for k in range(1, size["x"])
    ]
    advance(g_steps)
    for wait in small_waits:
        wait()
    for k in range(1, size["x"]):
        small = small + small_x[k - 1]
    small_out[at["z"], at["y"]] = small
    advance(out_steps)
    advance(out_steps)
    result_ref[...] = (hidden + out_acc[mine].astype(f32)).astype(bf16)
    small_waits = [
        traffic.start(small_out.at[at["z"], at["y"]], small_c.at[k - 1], small_c.at[k - 1], c=k)
        for k in range(1, size["c"])
    ]
    advance(g_steps)
    advance(g_steps)
    attn_all_ref[at["x"], at["c"]] = g_acc[at["x"], at["z"], at["y"]]
    attn_gather = replica_gather(place, traffic, attn_all_ref)
    next(attn_gather)
    ff_gathers.append(attn_gather)
    for wait in small_waits:
        wait()
    for step in [*ff_gathers, *ff_gathers]:
        next(step, None)
    traffic.finish()
    for k in range(1, size["c"]):
        small = small + small_c[k - 1]
    small_ref[...] = small


def back(size, lengths, tokens, cot, freq, *more):
    f32, bf16 = jnp.float32, jnp.bfloat16
    rows, width = tokens.shape
    gboth, gdown, att = more[2], more[3], more[4]
    own, quarter = att.shape[-2:]
    n = size
    kvd = 2 * HD
    reps = (n["x"], n["c"])
    sets = (n["l"], n["y"])
    shapes = [
        ((rows, width), bf16),
        ((rows, width), f32),
        (reps + sets + gboth.shape[2:], bf16),
        (reps + gdown.shape[1:], bf16),
        ((8, kvd), f32),
        (reps + (own, quarter), bf16),
    ]
    group = (n["x"], n["y"], n["l"], rows, width)
    owners = (n["x"], n["z"], n["y"], own, quarter)
    others = n["z"] * n["y"] - 1
    scratch = (
        [pltpu.VMEM(group, bf16)] * 6
        + [
            pltpu.VMEM((max(1, n["h"] - 1),) + gboth.shape[1:], bf16),
            pltpu.VMEM((max(1, n["h"] - 1),) + gdown.shape[1:], bf16),
            pltpu.VMEM(gboth.shape[1:], bf16),
            pltpu.VMEM(att.shape, bf16),
        ]
        + [pltpu.VMEM(owners, bf16)] * 3
        + [
            pltpu.VMEM((rows, width), f32),
            pltpu.VMEM((rows, width), bf16),
            pltpu.VMEM((n["z"], n["y"], 8, kvd), f32),
            pltpu.VMEM((max(1, others), 8, kvd), f32),
            pltpu.VMEM((max(1, n["x"] - 1), 8, kvd), f32),
            pltpu.VMEM((max(1, n["c"] - 1), 8, kvd), f32),
            pltpu.SemaphoreType.DMA((96,)),
            pltpu.SemaphoreType.DMA((96,)),
        ]
    )
    vmem = pl.BlockSpec(memory_space=pltpu.VMEM)
    return pl.pallas_call(
        functools.partial(back_kernel, size),
        out_shape=[jax.ShapeDtypeStruct(*s) for s in shapes],
        in_specs=[pl.BlockSpec(memory_space=pltpu.SMEM)] + [vmem] * (3 + len(more)),
        out_specs=[vmem] * len(shapes),
        scratch_shapes=scratch,
        compiler_params=pltpu.CompilerParams(
            collective_id=2, has_side_effects=True, vmem_limit_bytes=60 << 20
        ),
    )(lengths, tokens, cot, freq, *more)


def lay_out_kernel(
    groups, both_ref, attn_ref, down_in_ref, gate_ref, up_ref, gq_ref, gk_ref, gv_ref, go_ref, down_ref
):
    quarter = attn_ref.shape[-1]
    start = 0
    for ref in (gq_ref, gk_ref, gv_ref, go_ref):
        to = 0
        for share, first, count in columns(start, ref.shape[1], quarter):
            ref[:, to : to + count] = attn_ref[share, :, first : first + count].astype(jnp.float32)
            to += count
        start += ref.shape[1]

    @pl.when(pl.program_id(0) == 0)
    def _():
        rows = down_in_ref.shape[1]
        for r in range(down_in_ref.shape[0]):
            down_ref[r * rows : (r + 1) * rows, :] = down_in_ref[r].astype(jnp.float32)

    reps, sets, _, wide = both_ref.shape
    part = wide // (2 * groups)
    for half, ref in enumerate((gate_ref, up_ref)):
        for h in range(groups):
            first = (half * groups + h) * part
            for q in range(sets):
                for r in range(reps):
                    to = ((h * sets + q) * reps + r) * part
                    ref[:, to : to + part] = both_ref[r, q, :, first : first + part].astype(jnp.float32)


def lay_out(both, attn, down, groups):
    f32 = jnp.float32
    reps, sets, own, wide = both.shape
    full = reps * sets * wide // 2
    quarter, part, width = attn.shape[-1], down.shape[1], down.shape[2]
    kvd = 2 * HD
    step = 16
    cut = lambda n: pl.BlockSpec((step, n), lambda i: (i, 0))
    wide_outs = (full, full, width, kvd, kvd, width)
    return pl.pallas_call(
        functools.partial(lay_out_kernel, groups),
        grid=(own // step,),
        out_shape=[jax.ShapeDtypeStruct((own, n), f32) for n in wide_outs]
        + [jax.ShapeDtypeStruct((reps * part, width), f32)],
        in_specs=[
            pl.BlockSpec((reps, sets, step, wide), lambda i: (0, 0, i, 0)),
            pl.BlockSpec((reps, step, quarter), lambda i: (0, i, 0)),
            pl.BlockSpec((reps, part, width), lambda i: (0, 0, 0)),
        ],
        out_specs=[cut(n) for n in wide_outs]
        + [pl.BlockSpec((reps * part, width), lambda i: (0, 0))],
        compiler_params=pltpu.CompilerParams(vmem_limit_bytes=32 << 20),
    )(both, attn, down)


def by_kernels(
    tokens,
    cotangent,
    lengths,
    query_weight,
    key_weight,
    value_weight,
    output_weight,
    query_bias,
    key_bias,
    value_bias,
    attn_gain,
    gate_weight,
    up_weight,
    down_weight,
    mlp_gain,
):
    grid = Grid()
    size, at = grid.size, grid.at
    shards, reps = grid.shards, grid.reps
    rep = lax.axis_index("rep")
    rows, width = tokens.shape
    own = query_weight.shape[0]
    kvd = key_weight.shape[1]
    own_kv = key_bias.shape[0]
    f32, bf16 = jnp.float32, jnp.bfloat16
    wide = width + 2 * kvd
    total_w = wide + width
    quarter = total_w // reps

    part = down_weight.shape[0] // reps
    sets = size["l"] * size["y"]
    hidden = size["h"] * part

    down_part = lax.dynamic_slice(down_weight, (rep * part, 0), (part, width))
    freq = theta_base ** (-((np.arange(rows) % (HD // 2)).astype(np.float32) * np.float32(2.0 / HD)))
    freq = np.broadcast_to(freq.astype(np.float32)[None, :], (8, rows))
    vectors = [v[None, :] for v in (query_bias, attn_gain, mlp_gain, key_bias, value_bias)]
    att, _, both_mine, down_mine, cot_all, normed_all, *saved = front(
        size,
        lengths,
        tokens,
        cotangent,
        freq,
        query_weight,
        key_weight,
        value_weight,
        output_weight,
        *vectors,
        gate_weight,
        up_weight,
        down_part,
    )
    group = normed_all.shape[:-1]
    both_mine = both_mine.reshape(width, 2 * hidden)
    down_mine = down_mine.reshape(hidden, width)
    cot_all = cot_all.reshape(-1, width)
    normed_all = normed_all.reshape(-1, width)

    dprod = times_transposed(cot_all, down_mine)
    both = jnp.dot(normed_all, both_mine, preferred_element_type=f32)
    gate, upper = both[:, :hidden], both[:, hidden:]
    sigma = jax.nn.sigmoid(gate)
    product = (gate * sigma * upper).astype(bf16)
    dgate = (dprod * upper * sigma * (1.0 + gate * (1.0 - sigma))).astype(bf16)
    dup = (dprod * gate * sigma).astype(bf16)
    dboth = jnp.concatenate([dgate, dup], axis=1)
    dnormed_part = times_transposed(dboth, both_mine).astype(bf16)
    out_part = jnp.dot(product, down_mine, preferred_element_type=f32).astype(bf16)
    grad_both = jnp.dot(normed_all.T, dboth, preferred_element_type=f32).astype(bf16)
    grad_down = jnp.dot(product.T, cot_all, preferred_element_type=f32).astype(bf16)

    result, grad_input, both_all, down_all, vec, attn_all = back(
        size,
        lengths,
        tokens,
        cotangent,
        freq,
        dnormed_part.reshape(group + (width,)),
        out_part.reshape(group + (width,)),
        grad_both.reshape(size["h"], sets, own, 2 * hidden),
        grad_down.reshape(size["h"], part, width),
        att,
        *saved,
    )
    grad_gate, grad_up, *attn_grads, grad_down_own = lay_out(
        both_all.reshape(reps, sets, own, 2 * hidden),
        attn_all.reshape(reps, own, quarter),
        down_all.reshape(reps, part, width),
        size["h"],
    )

    return (
        result,
        grad_input,
        *attn_grads,
        vec[0, :own],
        vec[3, :own_kv],
        vec[4, :own_kv],
        vec[1, :own],
        grad_gate,
        grad_up,
        grad_down_own,
        vec[2, :own],
    )


def on_device(*args):
    tokens, query_weight, key_weight = args[0], args[3], args[4]
    rows, width = tokens.shape
    total_w = 2 * width + 2 * key_weight.shape[1]
    fits = (
        rows == 2 * HD
        and lax.axis_size("rep") % 2 == 0
        and HEADS // KVH % 2
        and key_weight.shape[1] == 2 * HD
        and query_weight.shape[0] % 16 == 0
        and query_weight.shape[0] <= 128
        and (total_w // lax.axis_size("rep")) % 128 == 0
    )
    return by_kernels(*args) if fits else by_permutes(*args)


def solution(mesh):
    in_specs = (
        P(("rep", "shard"), None),
        P(("rep", "shard"), None),
        P(("rep", "shard"), None),
        P("shard", None),
        P("shard", None),
        P("shard", None),
        P("shard", None),
        P("shard"),
        P("shard"),
        P("shard"),
        P("shard"),
        P("shard", None),
        P("shard", None),
        P("shard", None),
        P("shard"),
    )
    out_specs = (
        P(("rep", "shard"), None),
        P(("rep", "shard"), None),
        P("shard", None),
        P("shard", None),
        P("shard", None),
        P("shard", None),
        P("shard"),
        P("shard"),
        P("shard"),
        P("shard"),
        P("shard", None),
        P("shard", None),
        P("shard", None),
        P("shard"),
    )
    return jax.shard_map(
        on_device, mesh=mesh, in_specs=in_specs, out_specs=out_specs, check_vma=False
    )
```
